32 devices in a mesh: shard: 8 (over z, core), rep: 4 (over y, x).
Axes of the slice: x: 2, y: 2, z: 4, core: 2. Of those that a mesh axis runs over, the one named last changes fastest.
Arguments:
- tokens: bfloat16 [2, 8192, 1024], P(None, ('shard', 'rep')), may hold values from -6 to 6
- cotangent: bfloat16 [2, 8192, 1024], P(None, ('shard', 'rep')), may hold values from -6 to 6
- seq_lengths: int32 [2, 4, 8, 4], P(None, 'rep'), may hold values from 1 to 128, 256 in all within a row
- dealing: int32 [2, 4, 32], P(None, 'rep'), may hold values from 0 to 31, each once within a row
- attention_gain: bfloat16 [1024], P('shard'), may hold values from 0.25 to 1.75
- attention_shift: bfloat16 [1024], P('shard'), may hold values from -1 to 1
- input_weight: bfloat16 [1024, 3072], P('shard'), may hold values from -0.25 to 0.25
- query_bias: bfloat16 [1024], P('shard'), may hold values from -1 to 1
- value_bias: bfloat16 [1024], P('shard'), may hold values from -1 to 1
- output_weight: bfloat16 [1024, 1024], P('shard'), may hold values from -0.5 to 0.5
- output_bias: bfloat16 [1024], P('shard'), may hold values from -1 to 1
- feed_gain: bfloat16 [1024], P('shard'), may hold values from 0.25 to 1.75
- feed_shift: bfloat16 [1024], P('shard'), may hold values from -1 to 1
- up_weight: bfloat16 [1024, 4096], P('shard'), may hold values from -0.1875 to 0.1875
- up_bias: bfloat16 [4096], P('shard'), may hold values from -1 to 1
- down_weight: bfloat16 [4096, 1024], P('shard'), may hold values from -0.09375 to 0.09375
- down_bias: bfloat16 [1024], P('shard'), may hold values from -1 to 1
Outputs:
- block_out: bfloat16 [2, 8192, 1024], P(None, ('shard', 'rep'))
- input_grad: bfloat16 [2, 8192, 1024], P(None, ('shard', 'rep'))
- attention_gain_grad: float32 [1024], P('shard')
- attention_shift_grad: float32 [1024], P('shard')
- input_weight_grad: float32 [1024, 3072], P('shard')
- query_bias_grad: float32 [1024], P('shard')
- value_bias_grad: float32 [1024], P('shard')
- output_weight_grad: float32 [1024, 1024], P('shard')
- output_bias_grad: float32 [1024], P('shard')
- feed_gain_grad: float32 [1024], P('shard')
- feed_shift_grad: float32 [1024], P('shard')
- up_weight_grad: float32 [1024, 4096], P('shard')
- up_bias_grad: float32 [4096], P('shard')
- down_weight_grad: float32 [4096, 1024], P('shard')
- down_bias_grad: float32 [1024], P('shard')
The draws below stay inside these ranges and needn't reach their ends.
Inputs may be any that keep to these rules, and one draw needn't show every extreme that they name: `seq_lengths`: for every micro-batch and replica, the 4 lengths given for each index of shard add up to 256. `dealing`: for every micro-batch and replica, each dealt number appears once; number n goes to index n // 4 of shard.
All inputs are finite; a program needn't handle non-finite values.
Results may differ from the reference program's by a relative error of at most 0.013.
The reference program's roundings to bfloat16 on the way count: a program that leaves them out, or rounds other values in their place, can miss the bound.
Values may be sent and summed in bfloat16 or wider, within the bound.
A program may use at most 256 MiB of HBM per device.

```python
import math
from functools import partial
import jax
import jax.numpy as jnp
import numpy as np
from jax import lax

D = 1024
H = 16
HD = 64
FF = 4096
TOK_DEV = 256
SEQ_DEV = 4
MICRO = 2
TOKENS = 8192
GSEQ = 32
N_SHARD = 8
N_REP = 4


def level_of(own_key, extent, pieces, smallest, largest):
    factor_of, own = 1.0, jax.random.fold_in(own_key, 6)
    for dim, parts in pieces:
        steps = jnp.exp(jax.random.uniform(jax.random.fold_in(own, dim), (parts,), jnp.float32, smallest / len(pieces), largest / len(pieces)))
        factor_of = factor_of * jnp.repeat(steps, extent[dim] // parts).reshape([-1 if axis == dim else 1 for axis in range(len(extent))])
    return factor_of


def length_profile(count, total, bound, skew):
    weights = [(1 << 20) // math.isqrt(standing ** skew) + 1 for standing in range(2, count + 1)]
    spare, counts = total - bound - (count - 1), [1] * (count - 1)
    while spare > 0:
        candidates = [i for i in range(count - 1) if counts[i] < bound]
        whole, remaining = sum([weights[i] for i in candidates]), spare
        for i in candidates:
            addition = min(bound - counts[i], max(1, remaining * weights[i] // whole), spare)
            counts[i] = counts[i] + addition
            spare = spare - addition
    return np.array([bound] + counts)


def uneven(key, count, total, reach, skew):
    if count == 2:
        one = jax.random.randint(key, (), max(1, total - reach), min(reach, total - 1) + 1)
        return jnp.stack([one, total - one])
    lengths = jnp.asarray(length_profile(count, total, reach, skew), jnp.int32)
    couples = (count - 1) // 2
    giver, taker = lengths[1:1 + 2 * couples:2], lengths[2:2 + 2 * couples:2]
    slack = jnp.minimum(giver - 1, reach - taker)
    shifted = jax.random.randint(jax.random.fold_in(key, 1), (couples,), 0, 1 << 20) % (slack + 1)
    lengths = lengths.at[1:1 + 2 * couples:2].set(giver - shifted).at[2:2 + 2 * couples:2].set(taker + shifted)
    return lengths[jax.random.permutation(jax.random.fold_in(key, 2), count)]


def normal_values(rng, dims, width, most, shards=(), kind=jnp.bfloat16):
    values = width * jax.random.normal(rng, dims, jnp.float32)
    if shards:
        values = values * level_of(rng, dims, shards, -0.22, 0.18)
    return jnp.clip(values, -most, most).astype(kind)


def setup_inputs(seed: int = 0) -> dict:
    splits = jax.random.split(jax.random.key(seed), 18)
    return {
        "tokens": normal_values(splits[0], (MICRO, TOKENS, D), 1.0, 6.0, ((1, 32),)),
        "cotangent": normal_values(splits[1], (MICRO, TOKENS, D), 1.0, 6.0, ((1, 32),)),
        "seq_lengths": jax.vmap(lambda own: uneven(own, SEQ_DEV, TOK_DEV, TOK_DEV // 2, 2))(jax.random.split(splits[2], MICRO * N_REP * N_SHARD)).reshape((MICRO, N_REP, N_SHARD, SEQ_DEV)).astype(jnp.int32),
        "dealing": jax.vmap(lambda own: jax.random.permutation(own, GSEQ))(jax.random.split(splits[3], MICRO * N_REP)).reshape((MICRO, N_REP, GSEQ)).astype(jnp.int32),
        "attention_gain": jnp.clip(1.0 + 0.15 * jax.random.normal(splits[4], (D,), jnp.float32), 0.25, 1.75).astype(jnp.bfloat16),
        "attention_shift": normal_values(splits[5], (D,), 0.2, 1.0, ((0, 8),)),
        "input_weight": normal_values(splits[6], (D, 3 * D), (D // 2) ** -0.5, 0.25, ((0, 8),)),
        "query_bias": normal_values(splits[7], (D,), 0.2, 1.0, ((0, 8),)),
        "value_bias": normal_values(splits[8], (D,), 0.2, 1.0, ((0, 8),)),
        "output_weight": normal_values(splits[9], (D, D), (D // 8) ** -0.5, 0.5, ((0, 8),)),
        "output_bias": normal_values(splits[10], (D,), 0.2, 1.0, ((0, 8),)),
        "feed_gain": jnp.clip(1.0 + 0.15 * jax.random.normal(splits[11], (D,), jnp.float32), 0.25, 1.75).astype(jnp.bfloat16),
        "feed_shift": normal_values(splits[12], (D,), 0.2, 1.0, ((0, 8),)),
        "up_weight": normal_values(splits[13], (D, FF), D ** -0.5, 0.1875, ((0, 8),)),
        "up_bias": normal_values(splits[14], (FF,), 0.2, 1.0, ((0, 8),)),
        "down_weight": normal_values(splits[15], (FF, D), FF ** -0.5, 0.09375, ((0, 8),)),
        "down_bias": normal_values(splits[16], (D,), 0.2, 1.0, ((0, 8),)),
    }


@jax.custom_vjp
def low(v):
    return lax.optimization_barrier(v.astype(jnp.bfloat16)).astype(jnp.float32)

@jax.custom_vjp
def low_back(v):
    return v

def low_keep(v):
    return (low(v), None)

def low_pass(kept, grad):
    return (grad,)

def back_keep(v):
    return (v, None)

def back_low(kept, grad):
    return (low(grad),)
low.defvjp(low_keep, low_pass)
low_back.defvjp(back_keep, back_low)
EPSILON = 1e-05
MASKED = -1e+30
HIGHEST = lax.Precision.HIGHEST

def deal_maps(seq_lengths, dealing, rows_dev):
    groups, per_device = seq_lengths.shape
    total_seqs = groups * per_device
    numbers = jnp.arange(total_seqs, dtype=jnp.int32)
    flat_lengths = seq_lengths.reshape(total_seqs)
    matched = (dealing[:, None] == numbers[None, :]).astype(jnp.int32)
    packed_length = lax.optimization_barrier(jnp.sum(matched * flat_lengths[None, :], axis=1, dtype=jnp.int32))
    packed_start = jnp.cumsum(packed_length, dtype=jnp.int32) - packed_length
    start_of = lax.optimization_barrier(jnp.sum(matched * packed_start[:, None], axis=0, dtype=jnp.int32)).reshape(groups, per_device)
    bin_start = jnp.cumsum(seq_lengths, axis=1, dtype=jnp.int32) - seq_lengths
    places = jnp.arange(rows_dev, dtype=jnp.int32)
    inside = (places[None, :, None] >= bin_start[:, None, :]).astype(jnp.int32)
    segment = lax.optimization_barrier(jnp.sum(inside, axis=2, dtype=jnp.int32)) - 1
    picked = (segment[:, :, None] == jnp.arange(per_device, dtype=jnp.int32)[None, None, :]).astype(jnp.int32)
    position = places[None, :] - lax.optimization_barrier(jnp.sum(picked * bin_start[:, None, :], axis=2, dtype=jnp.int32))
    source = lax.optimization_barrier(jnp.sum(picked * start_of[:, None, :], axis=2, dtype=jnp.int32)) + position
    total_rows = groups * rows_dev
    all_rows = jnp.arange(total_rows, dtype=jnp.int32)
    owner_seq = lax.optimization_barrier(jnp.sum((all_rows[:, None] >= packed_start[None, :]).astype(jnp.int32), axis=1, dtype=jnp.int32)) - 1
    owner_hit = (owner_seq[:, None] == numbers[None, :]).astype(jnp.int32)
    offset = all_rows - lax.optimization_barrier(jnp.sum(owner_hit * packed_start[None, :], axis=1, dtype=jnp.int32))
    target = lax.optimization_barrier(jnp.sum(owner_hit * dealing[None, :], axis=1, dtype=jnp.int32))
    target_hit = (target[:, None] == numbers[None, :]).astype(jnp.int32)
    flat_start = bin_start.reshape(total_seqs)
    backward_row = target // per_device * rows_dev + lax.optimization_barrier(jnp.sum(target_hit * flat_start[None, :], axis=1, dtype=jnp.int32)) + offset
    return (source.reshape(total_rows), segment.reshape(total_rows), position.reshape(total_rows), backward_row)

def layer_norm(values, norm_gain, norm_shift):
    center = values - lax.optimization_barrier(jnp.mean(values, axis=-1, keepdims=True))
    spread = lax.optimization_barrier(jnp.mean(center * center, axis=-1, keepdims=True))
    return center * lax.rsqrt(spread + EPSILON) * norm_gain + norm_shift

def matmul(left, right):
    return jnp.dot(left, right, precision=HIGHEST, preferred_element_type=jnp.float32)

def block_rows(rows, segment, position, weights):
    attention_gain, attention_shift, input_weight, query_bias, value_bias, output_weight, output_bias, feed_gain, feed_shift, up_weight, up_bias, down_weight, down_bias = weights
    normed = low(layer_norm(rows, attention_gain, attention_shift))
    mixed = matmul(normed, input_weight)
    queries = low(low_back(mixed[:, :D] + query_bias)).reshape(-1, H, HD)
    keys_all = low(low_back(mixed[:, D:2 * D])).reshape(-1, H, HD)
    values_all = low(low_back(mixed[:, 2 * D:] + value_bias)).reshape(-1, H, HD)
    allowed = (segment[:, None] == segment[None, :]) & (position[None, :] <= position[:, None])
    raw_scores = jnp.einsum('qhd,khd->hqk', queries, keys_all, precision=HIGHEST)
    scores = jnp.where(allowed[None], low_back(raw_scores * float(HD) ** (-0.5)), MASKED)
    log_total = jax.nn.logsumexp(scores, axis=-1, keepdims=True)
    soft = jnp.exp(scores - log_total)
    attended = jnp.einsum('hqk,khd->qhd', low(soft), values_all, precision=HIGHEST).reshape(-1, D)
    branch = low(low_back(attended))
    middle = rows + low_back(matmul(branch, output_weight) + output_bias)
    normed_two = low(layer_norm(middle, feed_gain, feed_shift))
    hidden = low_back(matmul(normed_two, up_weight) + up_bias)
    activated = low(jax.nn.gelu(hidden, approximate=True))
    return middle + low_back(matmul(activated, down_weight) + down_bias)

def forward(token_rows, weights, seq_lengths, dealing):
    groups = N_SHARD
    grouped = token_rows.reshape(MICRO, groups, N_REP, TOK_DEV, D).transpose(0, 2, 1, 3, 4)
    grouped = grouped.reshape(MICRO, N_REP, groups * TOK_DEV, D)
    mapper = jax.vmap(jax.vmap(partial(deal_maps, rows_dev=TOK_DEV)))
    source, segment, position, backward_row = mapper(seq_lengths, dealing)
    dealt = jnp.take_along_axis(grouped, source[..., None], axis=2)
    total_bins = MICRO * N_REP * groups

    def run_bin(member):
        return jax.checkpoint(block_rows)(member[0], member[1], member[2], weights)
    computed = lax.map(run_bin, (dealt.reshape(total_bins, TOK_DEV, D), segment.reshape(total_bins, TOK_DEV), position.reshape(total_bins, TOK_DEV)))
    finished = computed.reshape(MICRO, N_REP, groups * TOK_DEV, D)
    restored = jnp.take_along_axis(finished, backward_row[..., None], axis=2)
    restored = restored.reshape(MICRO, N_REP, groups, TOK_DEV, D).transpose(0, 2, 1, 3, 4)
    return restored.reshape(MICRO, groups * N_REP * TOK_DEV, D)

def reference(tokens, cotangent, seq_lengths, dealing, attention_gain, attention_shift, input_weight, query_bias, value_bias, output_weight, output_bias, feed_gain, feed_shift, up_weight, up_bias, down_weight, down_bias):
    weights = tuple((member.astype(jnp.float32) for member in (attention_gain, attention_shift, input_weight, query_bias, value_bias, output_weight, output_bias, feed_gain, feed_shift, up_weight, up_bias, down_weight, down_bias)))

    def run_layer(token_rows, weight_set):
        return forward(token_rows, weight_set, seq_lengths, dealing)
    result, pullback = jax.vjp(run_layer, tokens.astype(jnp.float32), weights)
    input_grad, weight_grads = pullback(cotangent.astype(jnp.float32))
    return (result.astype(jnp.bfloat16), input_grad.astype(jnp.bfloat16), weight_grads[0], weight_grads[1], weight_grads[2], weight_grads[3], weight_grads[4], weight_grads[5], weight_grads[6], weight_grads[7], weight_grads[8], weight_grads[9], weight_grads[10], weight_grads[11], weight_grads[12])
```

```python
from functools import partial

import jax
import jax.numpy as jnp
from jax import lax
from jax.experimental import pallas as pl
from jax.experimental.pallas import tpu as pltpu
from jax.sharding import PartitionSpec as P

HD = 64
BLOCK = 128
EPSILON = 1e-05
MASKED = -1e30
AXES = ("shard", "rep")
F32 = jnp.float32
LOW = jnp.bfloat16


def dot(left, right):
    return jnp.dot(left, right, preferred_element_type=F32)


def rows_dot(left, right):
    return lax.dot_general(left, right, (((0,), (0,)), ((), ())), preferred_element_type=F32)


def back_dot(left, right):
    return lax.dot_general(left, right, (((1,), (1,)), ((), ())), preferred_element_type=F32)


def pick(stacked, index, axis=0):
    return lax.dynamic_index_in_dim(stacked, index, axis, keepdims=False)


def normalize(values):
    center = values - jnp.mean(values, axis=-1, keepdims=True)
    inverse = lax.rsqrt(jnp.mean(center * center, axis=-1, keepdims=True) + EPSILON)
    return center * inverse, inverse


def normalize_back(upper, gain, unit, inverse):
    scaled = upper * gain
    mean_scaled = jnp.mean(scaled, axis=-1, keepdims=True)
    mean_product = jnp.mean(scaled * unit, axis=-1, keepdims=True)
    return inverse * (scaled - mean_scaled - unit * mean_product)


def gelu_tanh(values):
    return jax.nn.gelu(values, approximate=True)


def sequence_starts(seq_lengths, dealing, first, rows):
    total = dealing.shape[0]
    numbers = jnp.arange(total, dtype=jnp.int32)
    matched = (dealing[:, None] == numbers[None, :]).astype(jnp.int32)
    packed_length = jnp.sum(matched * seq_lengths.reshape(total)[None, :], axis=1)
    before = (numbers[None, :] < numbers[:, None]).astype(jnp.int32)
    packed_start = jnp.sum(before * packed_length[None, :], axis=1)
    own = first + jnp.arange(rows, dtype=jnp.int32)
    return jnp.max(
        jnp.where(packed_start[None, :] <= own[:, None], packed_start[None, :], 0), axis=1
    )


def window(ref, row, previous, column):
    return jnp.concatenate(
        [
            ref[pl.ds(previous, BLOCK), column : column + BLOCK],
            ref[pl.ds(row, BLOCK), column : column + BLOCK],
        ],
        axis=0,
    )


def block_rows(step, blocks, body_rows):
    micro, block = step // blocks, step % blocks
    row = pl.multiple_of(step * BLOCK, BLOCK)
    previous = jnp.where(block == 0, body_rows + micro * BLOCK, row - BLOCK)
    return row, pl.multiple_of(previous, BLOCK)


def soft_weights(query_half, keys, allowed):
    scores = back_dot(query_half, keys) * float(HD) ** (-0.5)
    scores = jnp.where(allowed, scores, MASKED)
    top = jnp.max(scores, axis=1, keepdims=True)
    powers = jnp.exp(scores - top)
    return powers / jnp.sum(powers, axis=1, keepdims=True)


def allowed_keys(start_ref, row):
    places = lax.broadcasted_iota(jnp.int32, (BLOCK, 2 * BLOCK), 1)
    lines = lax.broadcasted_iota(jnp.int32, (BLOCK, 2 * BLOCK), 0)
    return (places >= start_ref[pl.ds(row, BLOCK), :]) & (places <= lines + BLOCK)


def attention_kernel(blocks, width, mixed_ref, start_ref, branch_ref):
    body_rows = branch_ref.shape[0]
    left = lax.broadcasted_iota(jnp.int32, (BLOCK, BLOCK), 1) < HD

    def step_body(step, _):
        row, previous = block_rows(step, blocks, body_rows)
        allowed = allowed_keys(start_ref, row)
        for column in range(0, width, BLOCK):
            queries = mixed_ref[pl.ds(row, BLOCK), column : column + BLOCK]
            keys = window(mixed_ref, row, previous, width + column)
            values = window(mixed_ref, row, previous, 2 * width + column)
            parts = []
            for half in (left, ~left):
                soft = soft_weights(jnp.where(half, queries, 0), keys, allowed)
                parts.append(dot(soft.astype(LOW), values))
            branch_ref[pl.ds(row, BLOCK), column : column + BLOCK] = jnp.where(
                left, parts[0], parts[1]
            ).astype(LOW)
        return 0

    lax.fori_loop(0, body_rows // BLOCK, step_body, 0)


def attention_back_kernel(blocks, width, mixed_ref, start_ref, upper_ref, grad_ref, sums_ref):
    body_rows = upper_ref.shape[0]
    left = lax.broadcasted_iota(jnp.int32, (BLOCK, BLOCK), 1) < HD
    left_tall = lax.broadcasted_iota(jnp.int32, (2 * BLOCK, BLOCK), 1) < HD
    scale = float(HD) ** (-0.5)
    sums_ref[...] = jnp.zeros_like(sums_ref)

    def step_body(step, _):
        row, previous = block_rows(step, blocks, body_rows)
        allowed = allowed_keys(start_ref, row)
        for column in range(0, width, BLOCK):
            queries = mixed_ref[pl.ds(row, BLOCK), column : column + BLOCK]
            keys = window(mixed_ref, row, previous, width + column)
            values = window(mixed_ref, row, previous, 2 * width + column)
            upper = upper_ref[pl.ds(row, BLOCK), column : column + BLOCK]
            parts = []
            for half in (left, ~left):
                soft = soft_weights(jnp.where(half, queries, 0), keys, allowed)
                soft_grad = back_dot(jnp.where(half, upper, 0), values)
                total = jnp.sum(soft * soft_grad, axis=1, keepdims=True)
                score_low = (soft * (soft_grad - total)).astype(LOW)
                parts.append(
                    (
                        dot(score_low, keys) * scale,
                        rows_dot(score_low, queries) * scale,
                        rows_dot(soft.astype(LOW), upper),
                    )
                )
            grad_ref[pl.ds(row, BLOCK), column : column + BLOCK] = jnp.where(
                left, parts[0][0], parts[1][0]
            ).astype(LOW)
            for slot in (1, 2):
                joined = jnp.where(left_tall, parts[0][slot], parts[1][slot])
                place = (slot - 1) * width + column
                sums_ref[pl.ds(previous, BLOCK), place : place + BLOCK] += joined[:BLOCK]
                sums_ref[pl.ds(row, BLOCK), place : place + BLOCK] += joined[BLOCK:]
        return 0

    lax.fori_loop(0, body_rows // BLOCK, step_body, 0)
    grad_ref[:, width:] = sums_ref[...].astype(LOW)
    grad_ref[body_rows:, :width] = jnp.zeros((grad_ref.shape[0] - body_rows, width), LOW)


def attention(mixed, starts, blocks):
    width = mixed.shape[1] // 3
    rows = starts.shape[0]
    vmem = pl.BlockSpec(memory_space=pltpu.VMEM)
    return pl.pallas_call(
        partial(attention_kernel, blocks, width),
        out_shape=jax.ShapeDtypeStruct((rows, width), LOW),
        in_specs=[vmem, vmem],
        out_specs=vmem,
        cost_estimate=pl.CostEstimate(
            flops=rows * width * BLOCK * 16, bytes_accessed=8 << 20, transcendentals=0
        ),
        compiler_params=pltpu.CompilerParams(vmem_limit_bytes=40 << 20),
    )(mixed, starts)


def attention_back(mixed, starts, upper, blocks):
    width = mixed.shape[1] // 3
    rows = starts.shape[0]
    vmem = pl.BlockSpec(memory_space=pltpu.VMEM)
    return pl.pallas_call(
        partial(attention_back_kernel, blocks, width),
        out_shape=jax.ShapeDtypeStruct(mixed.shape, LOW),
        in_specs=[vmem, vmem, vmem],
        out_specs=vmem,
        scratch_shapes=[pltpu.VMEM((mixed.shape[0], 2 * width), F32)],
        cost_estimate=pl.CostEstimate(
            flops=rows * width * BLOCK * 40, bytes_accessed=16 << 20, transcendentals=0
        ),
        compiler_params=pltpu.CompilerParams(vmem_limit_bytes=40 << 20),
    )(mixed, starts, upper)


class Links:
    def __init__(self, chips, reps):
        self.chips, self.reps = chips, reps
        shard = lax.axis_index("shard")
        self.chip, self.core, self.rep = shard // 2, shard % 2, lax.axis_index("rep")

    def flat(self, chip, core, rep):
        return (chip * 2 + core) * self.reps + rep

    def swap(self, values, chip=0, core=0, rep=0):
        pairs = [
            (self.flat(a, b, d), self.flat(a ^ chip, b ^ core, d ^ rep))
            for a in range(self.chips)
            for b in range(2)
            for d in range(self.reps)
        ]
        return lax.ppermute(values, AXES, pairs)

    def shift(self, values, by):
        pairs = [
            (self.flat(a, b, d), self.flat(a + by, b, d))
            for a in range(self.chips)
            if 0 <= a + by < self.chips
            for b in range(2)
            for d in range(self.reps)
        ]
        return lax.ppermute(values, AXES, pairs)

    def by_core(self, own, other, axis):
        first = jnp.where(self.core == 0, own, other)
        second = jnp.where(self.core == 0, other, own)
        return jnp.concatenate([first, second], axis=axis)

    def halves(self, matrix, parts):
        rows, columns = matrix.shape
        blocks = self.chips * parts
        view = matrix.reshape(rows, blocks, 2, columns // (2 * blocks))
        keep = pick(view, self.core, 2).reshape(rows, columns // 2)
        give = pick(view, 1 - self.core, 2).reshape(rows, columns // 2)
        return self.by_core(keep, self.swap(give, core=1), 0)

    def gather(self, chip_rows):
        rows, columns = chip_rows.shape
        quarter = rows // self.reps
        quarters = chip_rows.reshape(self.reps, quarter, columns)
        piece = pick(quarters, self.rep)
        pieces = jnp.stack([self.swap(piece, chip=j) for j in range(1, self.chips)])
        found = [pieces] + [None] * (self.reps - 1)
        if self.reps == 4:
            half = quarter // 2
            found[1] = self.swap(pieces, rep=1)
            found[2] = self.swap(pieces, rep=2)
            upper = self.swap(found[1][:, :half], rep=2)
            lower = self.swap(found[2][:, half:], rep=1)
            found[3] = jnp.concatenate([upper, lower], axis=1)
        else:
            for j in range(1, self.reps):
                found[j] = self.swap(pieces, rep=j)
        stacked = jnp.stack(
            [
                jnp.concatenate([pick(quarters, self.rep ^ j)[None], found[j]], axis=0)
                for j in range(self.reps)
            ]
        )
        ordered = []
        for chip in range(self.chips):
            for rep in range(self.reps):
                at = (self.rep ^ rep, self.chip ^ chip, 0, 0)
                ordered.append(
                    lax.dynamic_slice(stacked, at, (1, 1, quarter, columns)).reshape(
                        quarter, columns
                    )
                )
        return jnp.concatenate(ordered, axis=0)

    def reduce(self, grads):
        chips, reps = self.chips, self.reps
        rows, columns = grads.shape
        quarter = rows // (chips * reps)
        view = grads.astype(LOW).reshape(chips, reps, quarter, columns)
        mine = pick(view, self.rep, 1).astype(F32)
        if reps == 4:
            half = quarter // 2
            across = pick(view, self.rep ^ 3, 1)
            upper = self.swap(across[:, :half], rep=1)
            lower = self.swap(across[:, half:], rep=2)
            to_x = pick(view, self.rep ^ 1, 1)
            to_y = pick(view, self.rep ^ 2, 1)
            to_x = jnp.concatenate(
                [to_x[:, :half], (to_x[:, half:].astype(F32) + lower.astype(F32)).astype(LOW)],
                axis=1,
            )
            to_y = jnp.concatenate(
                [(to_y[:, :half].astype(F32) + upper.astype(F32)).astype(LOW), to_y[:, half:]],
                axis=1,
            )
            mine = (
                mine + self.swap(to_x, rep=1).astype(F32) + self.swap(to_y, rep=2).astype(F32)
            )
        else:
            for j in range(1, reps):
                mine = mine + self.swap(pick(view, self.rep ^ j, 1), rep=j).astype(F32)
        total = pick(mine, self.chip)
        sends = mine.astype(LOW)
        for j in range(1, chips):
            total = total + self.swap(pick(sends, self.chip ^ j), chip=j).astype(F32)
        return self.spread(total.astype(LOW))

    def spread(self, own):
        if self.reps == 4:
            half = own.shape[0] // 2
            from_x = self.swap(own, rep=1)
            from_y = self.swap(own, rep=2)
            upper = self.swap(from_x[:half], rep=2)
            lower = self.swap(from_y[half:], rep=1)
            found = [own, from_x, from_y, jnp.concatenate([upper, lower], axis=0)]
        else:
            found = [own] + [self.swap(own, rep=j) for j in range(1, self.reps)]
        stacked = jnp.stack(found)
        return jnp.concatenate([pick(stacked, self.rep ^ j) for j in range(self.reps)], axis=0)

    def unhalves(self, chip_rows, parts):
        rows, columns = chip_rows.shape
        view = chip_rows.reshape(2, rows // 2, columns)
        blocks = self.chips * parts
        keep = pick(view, self.core).reshape(rows // 2, blocks, 1, columns // blocks)
        came = self.swap(pick(view, 1 - self.core), core=1)
        came = came.reshape(rows // 2, blocks, 1, columns // blocks)
        return self.by_core(keep, came, 2).reshape(rows // 2, 2 * columns)

    def gather_vectors(self, packed):
        pair = self.by_core(packed[None], self.swap(packed, core=1)[None], 0)
        found = jnp.stack([pair] + [self.swap(pair, chip=j) for j in range(1, self.chips)])
        ordered = [pick(found, self.chip ^ j) for j in range(self.chips)]
        return jnp.concatenate(ordered, axis=0)

    def reduce_vectors(self, partial_sums):
        chips, reps = self.chips, self.reps
        view = partial_sums.reshape(chips, 2, -1)
        total = None
        for a in range(chips):
            for b in range(2):
                row = pick(pick(view, self.chip ^ a), self.core ^ b)
                row = row if a == b == 0 else self.swap(row, chip=a, core=b)
                total = row if total is None else total + row
        terms = [total] + [self.swap(total, rep=j) for j in range(1, reps)]
        while len(terms) > 1:
            terms = [terms[i] + terms[i + 1] for i in range(0, len(terms), 2)]
        return terms[0]


def shards(
    chips,
    reps,
    tokens,
    cotangent,
    seq_lengths,
    dealing,
    attention_gain,
    attention_shift,
    input_weight,
    query_bias,
    value_bias,
    output_weight,
    output_bias,
    feed_gain,
    feed_shift,
    up_weight,
    up_bias,
    down_weight,
    down_bias,
):
    links = Links(chips, reps)
    core, chip = links.core, links.chip
    micro, tok_rows, width = tokens.shape
    shard_count = 2 * chips
    own_rows = micro * tok_rows
    blocks = 2 * tok_rows // BLOCK

    def own_of(values):
        return pick(values.reshape(micro, 2, tok_rows, -1), core, 1).reshape(own_rows, -1)

    def other_of(values):
        return pick(values.reshape(micro, 2, tok_rows, -1), 1 - core, 1).reshape(own_rows, -1)

    def pair_rows(own):
        came = links.swap(own, core=1)
        shape = (micro, 1, tok_rows, own.shape[-1])
        return links.by_core(own.reshape(shape), came.reshape(shape), 1).reshape(2 * own_rows, -1)

    def pair_sum(partial_values):
        return own_of(partial_values) + links.swap(other_of(partial_values), core=1)

    vectors = (
        attention_gain,
        attention_shift,
        query_bias,
        value_bias,
        output_bias,
        feed_gain,
        feed_shift,
        down_bias,
        up_bias,
    )
    lengths = [member.shape[0] for member in vectors]
    table = links.gather_vectors(jnp.concatenate(vectors)).astype(F32)
    wholes, at = [], 0
    for length in lengths:
        wholes.append(table[:, at : at + length])
        at += length

    def whole(index):
        return wholes[index].reshape(1, -1)

    def core_part(index):
        return pick(wholes[index].reshape(chips, 2, -1), core, 1).reshape(1, -1)

    input_part = links.gather(links.halves(input_weight, 3))
    output_part = links.gather(output_weight)
    up_part = links.gather(links.halves(up_weight, 1))
    down_part = links.gather(down_weight)

    inputs = tokens.reshape(own_rows, width).astype(F32)
    unit_one, inverse_one = normalize(inputs)
    normed = (unit_one * whole(0) + whole(1)).astype(LOW)
    chip_normed = pair_rows(normed)
    tail = chip_normed.reshape(micro, 2 * tok_rows, width)[:, 2 * tok_rows - BLOCK :]
    halo = links.shift(tail.reshape(micro * BLOCK, width), 1)
    all_normed = jnp.concatenate([chip_normed, halo], axis=0)
    down_low = pair_rows(cotangent.reshape(own_rows, width))
    first = chip * 2 * tok_rows
    starts = jnp.stack(
        [
            sequence_starts(seq_lengths[m, 0], dealing[m, 0], first, 2 * tok_rows)
            for m in range(micro)
        ]
    )
    block_first = first + jnp.arange(2 * tok_rows, dtype=jnp.int32) // BLOCK * BLOCK - BLOCK
    starts = (starts - block_first[None, :]).reshape(2 * own_rows, 1)

    half = width // 2
    bias = jnp.concatenate([core_part(2), jnp.zeros((1, half), F32), core_part(3)], axis=1)
    mixed = (dot(all_normed, input_part) + bias).astype(LOW)
    branch = attention(mixed, starts, blocks)
    middle = inputs + pair_sum(dot(branch, output_part)) + whole(4)
    unit_two, inverse_two = normalize(middle)
    normed_two = pair_rows((unit_two * whole(5) + whole(6)).astype(LOW))
    hidden = dot(normed_two, up_part) + core_part(8)
    activated, gelu_back = jax.vjp(gelu_tanh, hidden)
    activated = activated.astype(LOW)
    down_grad = links.reduce(rows_dot(activated, down_low)).astype(F32)
    result = middle + pair_sum(dot(activated, down_part)) + whole(7)

    upstream = cotangent.reshape(own_rows, width).astype(F32)
    (hidden_grad,) = gelu_back(back_dot(down_low, down_part))
    hidden_low = hidden_grad.astype(LOW)
    up_grad = links.unhalves(links.reduce(rows_dot(normed_two, hidden_low)), 1).astype(F32)
    upper_two = pair_sum(back_dot(hidden_low, up_part))
    middle_grad = upstream + normalize_back(upper_two, whole(5), unit_two, inverse_two)
    output_own = middle_grad.astype(LOW)
    output_low = pair_rows(output_own)
    output_grad = links.reduce(rows_dot(branch, output_low)).astype(F32)
    attended = back_dot(output_low, output_part).astype(LOW)
    mixed_grad = attention_back(mixed, starts, attended, blocks)
    input_weight_grad = links.unhalves(links.reduce(rows_dot(all_normed, mixed_grad)), 3).astype(F32)
    back_halo = links.shift(mixed_grad[2 * own_rows :, half:], -1)
    body = mixed_grad[: 2 * own_rows].reshape(micro, 2 * tok_rows, 3 * half)
    tail_grad = body[:, 2 * tok_rows - BLOCK :, half:].astype(F32) + back_halo.reshape(
        micro, BLOCK, width
    ).astype(F32)
    body = body.at[:, 2 * tok_rows - BLOCK :, half:].set(tail_grad.astype(LOW))
    upper_one = pair_sum(back_dot(body.reshape(2 * own_rows, 3 * half), input_part))
    input_grad = middle_grad + normalize_back(upper_one, whole(0), unit_one, inverse_one)

    def by_shard(values):
        return values.reshape(shard_count, -1)

    def by_core_shard(values):
        spread = values.reshape(chips, 1, -1)
        mask = jnp.arange(2, dtype=jnp.int32)[None, :, None] == core
        return jnp.where(mask, spread, 0.0).reshape(shard_count, -1)

    def column_sum(values):
        return jnp.sum(values.astype(F32), axis=0)

    packed = jnp.concatenate(
        [
            by_shard(column_sum(upper_one * unit_one)),
            by_shard(column_sum(upper_one)),
            by_core_shard(column_sum(mixed_grad[:, :half])),
            by_core_shard(column_sum(mixed_grad[:, width:])),
            by_shard(column_sum(output_own)),
            by_shard(column_sum(upper_two * unit_two)),
            by_shard(column_sum(upper_two)),
            by_shard(column_sum(upstream)),
            by_core_shard(column_sum(hidden_low)),
        ],
        axis=1,
    )
    sums = links.reduce_vectors(packed)
    vector_grads, at = [], 0
    for length in lengths:
        vector_grads.append(sums[at : at + length])
        at += length
    return (
        result.astype(LOW).reshape(tokens.shape),
        input_grad.astype(LOW).reshape(tokens.shape),
        vector_grads[0],
        vector_grads[1],
        input_weight_grad,
        vector_grads[2],
        vector_grads[3],
        output_grad,
        vector_grads[4],
        vector_grads[5],
        vector_grads[6],
        up_grad,
        vector_grads[8],
        down_grad,
        vector_grads[7],
    )


def solution(mesh):
    rows_spec = P(None, ("shard", "rep"), None)
    vector, matrix = P("shard"), P("shard", None)
    weight_specs = (
        vector,
        vector,
        matrix,
        vector,
        vector,
        matrix,
        vector,
        vector,
        vector,
        matrix,
        vector,
        matrix,
        vector,
    )
    return jax.shard_map(
        partial(shards, mesh.shape["shard"] // 2, mesh.shape["rep"]),
        mesh=mesh,
        in_specs=(rows_spec, rows_spec, P(None, "rep", None, None), P(None, "rep", None))
        + weight_specs,
        out_specs=(rows_spec, rows_spec) + weight_specs,
        check_vma=False,
    )
```

```python
from functools import partial

import jax
import jax.numpy as jnp
from jax import lax
from jax.experimental import pallas as pl
from jax.experimental.pallas import tpu as pltpu
from jax.sharding import PartitionSpec as P

HD = 64
BLOCK = 128
EPSILON = 1e-05
MASKED = -1e30
AXES = ("shard", "rep")
F32 = jnp.float32
LOW = jnp.bfloat16


def dot(left, right):
    return jnp.dot(left, right, preferred_element_type=F32)


def rows_dot(left, right):
    return lax.dot_general(left, right, (((0,), (0,)), ((), ())), preferred_element_type=F32)


def back_dot(left, right):
    return lax.dot_general(left, right, (((1,), (1,)), ((), ())), preferred_element_type=F32)


def pick(stacked, index, axis=0):
    return lax.dynamic_index_in_dim(stacked, index, axis, keepdims=False)


def normalize(values):
    center = values - jnp.mean(values, axis=-1, keepdims=True)
    inverse = lax.rsqrt(jnp.mean(center * center, axis=-1, keepdims=True) + EPSILON)
    return center * inverse, inverse


def normalize_back(upper, gain, unit, inverse):
    scaled = upper * gain
    mean_scaled = jnp.mean(scaled, axis=-1, keepdims=True)
    mean_product = jnp.mean(scaled * unit, axis=-1, keepdims=True)
    return inverse * (scaled - mean_scaled - unit * mean_product)


def gelu_tanh(values):
    return jax.nn.gelu(values, approximate=True)


def sequence_starts(seq_lengths, dealing, first, rows):
    total = dealing.shape[0]
    numbers = jnp.arange(total, dtype=jnp.int32)
    matched = (dealing[:, None] == numbers[None, :]).astype(jnp.int32)
    packed_length = jnp.sum(matched * seq_lengths.reshape(total)[None, :], axis=1)
    before = (numbers[None, :] < numbers[:, None]).astype(jnp.int32)
    packed_start = jnp.sum(before * packed_length[None, :], axis=1)
    own = first + jnp.arange(rows, dtype=jnp.int32)
    return jnp.max(
        jnp.where(packed_start[None, :] <= own[:, None], packed_start[None, :], 0), axis=1
    )


def window(ref, row, previous, column):
    return jnp.concatenate(
        [
            ref[pl.ds(previous, BLOCK), column : column + BLOCK],
            ref[pl.ds(row, BLOCK), column : column + BLOCK],
        ],
        axis=0,
    )


def block_rows(step, blocks, body_rows):
    micro, block = step // blocks, step % blocks
    row = pl.multiple_of(step * BLOCK, BLOCK)
    previous = jnp.where(block == 0, body_rows + micro * BLOCK, row - BLOCK)
    return row, pl.multiple_of(previous, BLOCK)


def soft_weights(query_half, keys, allowed):
    scores = back_dot(query_half, keys) * float(HD) ** (-0.5)
    scores = jnp.where(allowed, scores, MASKED)
    top = jnp.max(scores, axis=1, keepdims=True)
    powers = jnp.exp(scores - top)
    return powers / jnp.sum(powers, axis=1, keepdims=True)


def allowed_keys(start_ref, row):
    places = lax.broadcasted_iota(jnp.int32, (BLOCK, 2 * BLOCK), 1)
    lines = lax.broadcasted_iota(jnp.int32, (BLOCK, 2 * BLOCK), 0)
    return (places >= start_ref[pl.ds(row, BLOCK), :]) & (places <= lines + BLOCK)


def attention_kernel(blocks, width, mixed_ref, start_ref, branch_ref):
    body_rows = branch_ref.shape[0]
    left = lax.broadcasted_iota(jnp.int32, (BLOCK, BLOCK), 1) < HD

    def step_body(step, _):
        row, previous = block_rows(step, blocks, body_rows)
        allowed = allowed_keys(start_ref, row)
        for column in range(0, width, BLOCK):
            queries = mixed_ref[pl.ds(row, BLOCK), column : column + BLOCK]
            keys = window(mixed_ref, row, previous, width + column)
            values = window(mixed_ref, row, previous, 2 * width + column)
            parts = []
            for half in (left, ~left):
                soft = soft_weights(jnp.where(half, queries, 0), keys, allowed)
                parts.append(dot(soft.astype(LOW), values))
            branch_ref[pl.ds(row, BLOCK), column : column + BLOCK] = jnp.where(
                left, parts[0], parts[1]
            ).astype(LOW)
        return 0

    lax.fori_loop(0, body_rows // BLOCK, step_body, 0)


def attention_back_kernel(blocks, width, mixed_ref, start_ref, upper_ref, grad_ref, sums_ref):
    body_rows = upper_ref.shape[0]
    left = lax.broadcasted_iota(jnp.int32, (BLOCK, BLOCK), 1) < HD
    left_tall = lax.broadcasted_iota(jnp.int32, (2 * BLOCK, BLOCK), 1) < HD
    scale = float(HD) ** (-0.5)
    sums_ref[...] = jnp.zeros_like(sums_ref)

    def step_body(step, _):
        row, previous = block_rows(step, blocks, body_rows)
        allowed = allowed_keys(start_ref, row)
        for column in range(0, width, BLOCK):
            queries = mixed_ref[pl.ds(row, BLOCK), column : column + BLOCK]
            keys = window(mixed_ref, row, previous, width + column)
            values = window(mixed_ref, row, previous, 2 * width + column)
            upper = upper_ref[pl.ds(row, BLOCK), column : column + BLOCK]
            parts = []
            for half in (left, ~left):
                soft = soft_weights(jnp.where(half, queries, 0), keys, allowed)
                soft_grad = back_dot(jnp.where(half, upper, 0), values)
                total = jnp.sum(soft * soft_grad, axis=1, keepdims=True)
                score_low = (soft * (soft_grad - total)).astype(LOW)
                parts.append(
                    (
                        dot(score_low, keys) * scale,
                        rows_dot(score_low, queries) * scale,
                        rows_dot(soft.astype(LOW), upper),
                    )
                )
            grad_ref[pl.ds(row, BLOCK), column : column + BLOCK] = jnp.where(
                left, parts[0][0], parts[1][0]
            ).astype(LOW)
            for slot in (1, 2):
                joined = jnp.where(left_tall, parts[0][slot], parts[1][slot])
                place = (slot - 1) * width + column
                sums_ref[pl.ds(previous, BLOCK), place : place + BLOCK] += joined[:BLOCK]
                sums_ref[pl.ds(row, BLOCK), place : place + BLOCK] += joined[BLOCK:]
        return 0

    lax.fori_loop(0, body_rows // BLOCK, step_body, 0)
    grad_ref[:, width:] = sums_ref[...].astype(LOW)
    grad_ref[body_rows:, :width] = jnp.zeros((grad_ref.shape[0] - body_rows, width), LOW)


def attention(mixed, starts, blocks):
    width = mixed.shape[1] // 3
    rows = starts.shape[0]
    vmem = pl.BlockSpec(memory_space=pltpu.VMEM)
    return pl.pallas_call(
        partial(attention_kernel, blocks, width),
        out_shape=jax.ShapeDtypeStruct((rows, width), LOW),
        in_specs=[vmem, vmem],
        out_specs=vmem,
        cost_estimate=pl.CostEstimate(
            flops=rows * width * BLOCK * 16, bytes_accessed=8 << 20, transcendentals=0
        ),
        compiler_params=pltpu.CompilerParams(vmem_limit_bytes=40 << 20),
    )(mixed, starts)


def attention_back(mixed, starts, upper, blocks):
    width = mixed.shape[1] // 3
    rows = starts.shape[0]
    vmem = pl.BlockSpec(memory_space=pltpu.VMEM)
    return pl.pallas_call(
        partial(attention_back_kernel, blocks, width),
        out_shape=jax.ShapeDtypeStruct(mixed.shape, LOW),
        in_specs=[vmem, vmem, vmem],
        out_specs=vmem,
        scratch_shapes=[pltpu.VMEM((mixed.shape[0], 2 * width), F32)],
        cost_estimate=pl.CostEstimate(
            flops=rows * width * BLOCK * 40, bytes_accessed=16 << 20, transcendentals=0
        ),
        compiler_params=pltpu.CompilerParams(vmem_limit_bytes=40 << 20),
    )(mixed, starts, upper)


class Links:
    def __init__(self, chips, reps):
        self.chips, self.reps = chips, reps
        shard = lax.axis_index("shard")
        self.chip, self.core, self.rep = shard // 2, shard % 2, lax.axis_index("rep")

    def flat(self, chip, core, rep):
        return (chip * 2 + core) * self.reps + rep

    def swap(self, values, chip=0, core=0, rep=0):
        pairs = [
            (self.flat(a, b, d), self.flat(a ^ chip, b ^ core, d ^ rep))
            for a in range(self.chips)
            for b in range(2)
            for d in range(self.reps)
        ]
        return lax.ppermute(values, AXES, pairs)

    def shift(self, values, by):
        pairs = [
            (self.flat(a, b, d), self.flat(a + by, b, d))
            for a in range(self.chips)
            if 0 <= a + by < self.chips
            for b in range(2)
            for d in range(self.reps)
        ]
        return lax.ppermute(values, AXES, pairs)

    def by_core(self, own, other, axis):
        first = jnp.where(self.core == 0, own, other)
        second = jnp.where(self.core == 0, other, own)
        return jnp.concatenate([first, second], axis=axis)

    def halves(self, matrix, parts):
        rows, columns = matrix.shape
        blocks = self.chips * parts
        view = matrix.reshape(rows, blocks, 2, columns // (2 * blocks))
        keep = pick(view, self.core, 2).reshape(rows, columns // 2)
        give = pick(view, 1 - self.core, 2).reshape(rows, columns // 2)
        return self.by_core(keep, self.swap(give, core=1), 0)

    def gather(self, chip_rows):
        rows, columns = chip_rows.shape
        quarter = rows // self.reps
        quarters = chip_rows.reshape(self.reps, quarter, columns)
        piece = pick(quarters, self.rep)
        pieces = jnp.stack([self.swap(piece, chip=j) for j in range(1, self.chips)])
        found = [pieces] + [None] * (self.reps - 1)
        if self.reps == 4:
            half = quarter // 2
            found[1] = self.swap(pieces, rep=1)
            found[2] = self.swap(pieces, rep=2)
            upper = self.swap(found[1][:, :half], rep=2)
            lower = self.swap(found[2][:, half:], rep=1)
            found[3] = jnp.concatenate([upper, lower], axis=1)
        else:
            for j in range(1, self.reps):
                found[j] = self.swap(pieces, rep=j)
        stacked = jnp.stack(
            [
                jnp.concatenate([pick(quarters, self.rep ^ j)[None], found[j]], axis=0)
                for j in range(self.reps)
            ]
        )
        ordered = []
        for chip in range(self.chips):
            for rep in range(self.reps):
                at = (self.rep ^ rep, self.chip ^ chip, 0, 0)
                ordered.append(
                    lax.dynamic_slice(stacked, at, (1, 1, quarter, columns)).reshape(
                        quarter, columns
                    )
                )
        return jnp.concatenate(ordered, axis=0)

    def reduce(self, grads):
        chips, reps = self.chips, self.reps
        rows, columns = grads.shape
        quarter = rows // (chips * reps)
        view = grads.astype(LOW).reshape(chips, reps, quarter, columns)
        mine = pick(view, self.rep, 1).astype(F32)
        if reps == 4:
            half = quarter // 2
            across = pick(view, self.rep ^ 3, 1)
            upper = self.swap(across[:, :half], rep=1)
            lower = self.swap(across[:, half:], rep=2)
            to_x = pick(view, self.rep ^ 1, 1)
            to_y = pick(view, self.rep ^ 2, 1)
            to_x = jnp.concatenate(
                [to_x[:, :half], (to_x[:, half:].astype(F32) + lower.astype(F32)).astype(LOW)],
                axis=1,
            )
            to_y = jnp.concatenate(
                [(to_y[:, :half].astype(F32) + upper.astype(F32)).astype(LOW), to_y[:, half:]],
                axis=1,
            )
            mine = (
                mine + self.swap(to_x, rep=1).astype(F32) + self.swap(to_y, rep=2).astype(F32)
            )
        else:
            for j in range(1, reps):
                mine = mine + self.swap(pick(view, self.rep ^ j, 1), rep=j).astype(F32)
        total = pick(mine, self.chip)
        sends = mine.astype(LOW)
        for j in range(1, chips):
            total = total + self.swap(pick(sends, self.chip ^ j), chip=j).astype(F32)
        return self.spread(total.astype(LOW))

    def spread(self, own):
        if self.reps == 4:
            half = own.shape[0] // 2
            from_x = self.swap(own, rep=1)
            from_y = self.swap(own, rep=2)
            upper = self.swap(from_x[:half], rep=2)
            lower = self.swap(from_y[half:], rep=1)
            found = [own, from_x, from_y, jnp.concatenate([upper, lower], axis=0)]
        else:
            found = [own] + [self.swap(own, rep=j) for j in range(1, self.reps)]
        stacked = jnp.stack(found)
        return jnp.concatenate([pick(stacked, self.rep ^ j) for j in range(self.reps)], axis=0)

    def unhalves(self, chip_rows, parts):
        rows, columns = chip_rows.shape
        view = chip_rows.reshape(2, rows // 2, columns)
        blocks = self.chips * parts
        keep = pick(view, self.core).reshape(rows // 2, blocks, 1, columns // blocks)
        came = self.swap(pick(view, 1 - self.core), core=1)
        came = came.reshape(rows // 2, blocks, 1, columns // blocks)
        return self.by_core(keep, came, 2).reshape(rows // 2, 2 * columns)

    def gather_vectors(self, packed):
        pair = self.by_core(packed[None], self.swap(packed, core=1)[None], 0)
        found = jnp.stack([pair] + [self.swap(pair, chip=j) for j in range(1, self.chips)])
        ordered = [pick(found, self.chip ^ j) for j in range(self.chips)]
        return jnp.concatenate(ordered, axis=0)

    def reduce_vectors(self, partial_sums):
        chips, reps = self.chips, self.reps
        view = partial_sums.reshape(chips, 2, -1)
        total = None
        for a in range(chips):
            for b in range(2):
                row = pick(pick(view, self.chip ^ a), self.core ^ b)
                row = row if a == b == 0 else self.swap(row, chip=a, core=b)
                total = row if total is None else total + row
        terms = [total] + [self.swap(total, rep=j) for j in range(1, reps)]
        while len(terms) > 1:
            terms = [terms[i] + terms[i + 1] for i in range(0, len(terms), 2)]
        return terms[0]

class Copies:
    def __init__(self, send, recv, links):
        self.send, self.recv, self.links = send, recv, links
        self.places, self.started = {}, []

    def make(self, name, source, target, device):
        place = self.places.setdefault(name, len(self.places))
        return pltpu.make_async_remote_copy(
            src_ref=source,
            dst_ref=target,
            send_sem=self.send.at[place],
            recv_sem=self.recv.at[place],
            device_id=device,
            device_id_type=pl.DeviceIdType.MESH,
        )

    def start(self, name, source, target, device, when=None):
        copy = self.make(name, source, target, device)
        run_when(when, copy.start)
        self.started.append((when, copy))

    def arrived(self, name, target, when=None):
        copy = self.make(name, target, target, self.links.other(x=1))
        run_when(when, copy.wait_recv)

    def finish(self):
        for when, copy in self.started:
            run_when(when, copy.wait_send)


def run_when(when, body):
    if when is None:
        body()
    else:
        pl.when(when)(body)


class Place:
    def __init__(self, chips):
        shard = lax.axis_index("shard")
        self.chips, self.shard = chips, shard
        self.chip, self.core, self.rep = shard // 2, lax.rem(shard, 2), lax.axis_index("rep")

    def flipped(self, bits):
        x, y = lax.rem(self.rep, 2), self.rep // 2
        x = 1 - x if bits & 1 else x
        y = 1 - y if bits & 2 else y
        return y * 2 + x

    def other(self, x=0, y=0, core=0, chip=None):
        chip = self.chip if chip is None else chip
        side = 1 - self.core if core else self.core
        return {"shard": chip * 2 + side, "rep": self.flipped(x + 2 * y)}

    def shard_at(self, step):
        return lax.rem(self.shard + step, 2 * self.chips)

    def greet(self, barrier_devices):
        barrier = pltpu.get_barrier_semaphore()
        for device in barrier_devices:
            pl.semaphore_signal(barrier, 1, device_id=device, device_id_type=pl.DeviceIdType.MESH)
        pl.semaphore_wait(barrier, len(barrier_devices))

    def neighbours(self):
        shards = [
            {"shard": self.shard_at(step), "rep": self.rep} for step in range(1, 2 * self.chips)
        ]
        return shards + [self.other(x=1), self.other(y=1)]


def gather_kernel(
    chips, splits, vec_in, in_in, out_in, up_in, down_in, *refs
):
    table, wholes, (send, recv, local) = refs[0], refs[1:5], refs[5:]
    shards_in = (in_in, out_in, up_in, down_in)
    at = Place(chips)
    copies = Copies(send, recv, at)
    at.greet(at.neighbours())
    own_copies = []

    def keep(source, target):
        copy = pltpu.make_async_copy(source, target, local.at[len(own_copies)])
        copy.start()
        own_copies.append(copy)

    keep(vec_in, table.at[at.shard])
    for step in range(1, 2 * chips):
        copies.start(
            ("vec", step), vec_in, table.at[at.shard], {"shard": at.shard_at(step), "rep": at.rep}
        )
    kept = []
    for index, (source, whole, blocks) in enumerate(zip(shards_in, wholes, splits)):
        rows = source.shape[0]
        first = len(own_copies)
        if blocks is None:
            keep(source, whole.at[pl.ds(pl.multiple_of(at.chip * rows, rows), rows)])
        else:
            width = source.shape[1] // (2 * blocks)
            place = pl.ds(pl.multiple_of(at.shard * rows, rows), rows)
            for block in range(blocks):
                columns = pl.ds(block * width, width)

                def side(core):
                    return pl.ds(pl.multiple_of((2 * block + core) * width, width), width)

                copies.start(
                    ("pair", index, block),
                    source.at[:, side(1 - at.core)],
                    whole.at[place, columns],
                    at.other(core=1),
                )
                keep(source.at[:, side(at.core)], whole.at[place, columns])
        kept.append(own_copies[first:])

    def piece(index, chip, part=None):
        whole = wholes[index]
        rows = whole.shape[0] // chips
        quarter = rows // 4
        if splits[index] is None and index == 1:
            return whole.at[pl.ds(pl.multiple_of(chip * rows, rows), rows)]
        start, size = chip * rows + at.rep * quarter, quarter
        if part is not None:
            bits, piece_half = part
            start = chip * rows + at.flipped(bits) * quarter
            if piece_half is not None:
                size = quarter // 2
                start = start + piece_half * size
        return whole.at[pl.ds(pl.multiple_of(start, size), size)]

    ways = (("up", 1), ("down", -1))

    def neighbour(step):
        return at.other(chip=jnp.clip(at.chip + step, 0, chips - 1))

    def can_send(step):
        return at.chip < chips - 1 if step > 0 else at.chip > 0

    def has(step, distance):
        return at.chip >= distance if step > 0 else at.chip + distance < chips

    def open_z(index):
        for copy in kept[index]:
            copy.wait()
        if splits[index] is not None:
            rows = shards_in[index].shape[0]
            width = shards_in[index].shape[1] // (2 * splits[index])
            place = pl.ds(pl.multiple_of((at.chip * 2 + 1 - at.core) * rows, rows), rows)
            for block in range(splits[index]):
                copies.arrived(
                    ("pair", index, block), wholes[index].at[place, pl.ds(block * width, width)]
                )
        for name, step in ways:
            mine = piece(index, at.chip)
            copies.start((name, index, 1), mine, mine, neighbour(step), can_send(step))

    def pass_on(index):
        for distance in range(1, chips):
            for name, step in ways:
                when = has(step, distance)
                chip = jnp.clip(at.chip - step * distance, 0, chips - 1)
                found = piece(index, chip)
                copies.arrived((name, index, distance), found, when)
                if distance < chips - 1:
                    copies.start(
                        (name, index, distance + 1),
                        found,
                        found,
                        neighbour(step),
                        when & can_send(step),
                    )
                if index != 1:
                    copies.start(("x", name, index, distance), found, found, at.other(x=1), when)
                    copies.start(("y", name, index, distance), found, found, at.other(y=1), when)

    def across(index):
        if index == 1:
            return
        for distance in range(1, chips):
            for name, step in ways:
                when = has(step, distance)
                chip = jnp.clip(at.chip - step * distance, 0, chips - 1)
                key = (name, index, distance)
                copies.arrived(("x",) + key, piece(index, chip, (1, None)), when)
                upper = piece(index, chip, (1, 0))
                copies.start(("xy",) + key, upper, upper, at.other(y=1), when)
                copies.arrived(("y",) + key, piece(index, chip, (2, None)), when)
                lower = piece(index, chip, (2, 1))
                copies.start(("yx",) + key, lower, lower, at.other(x=1), when)

    def close(index):
        if index == 1:
            return
        for distance in range(1, chips):
            for name, step in ways:
                when = has(step, distance)
                chip = jnp.clip(at.chip - step * distance, 0, chips - 1)
                key = (name, index, distance)
                copies.arrived(("xy",) + key, piece(index, chip, (3, 0)), when)
                copies.arrived(("yx",) + key, piece(index, chip, (3, 1)), when)

    count = len(wholes)
    open_z(0)
    for index in range(count):
        if index + 1 < count:
            open_z(index + 1)
        pass_on(index)
        across(index)
    for index in range(count):
        close(index)
    own_copies[0].wait()
    for step in range(1, 2 * chips):
        copies.arrived(("vec", step), table.at[at.shard_at(2 * chips - step)])
    copies.finish()


def gather_weights(packed, matrices, splits, chips):
    any_space = pl.BlockSpec(memory_space=pl.ANY)
    vmem = pl.BlockSpec(memory_space=pltpu.VMEM)
    shapes = [jax.ShapeDtypeStruct((2 * chips,) + packed.shape, LOW)]
    for matrix, blocks in zip(matrices, splits):
        rows, columns = matrix.shape
        shape = (chips * rows, columns) if blocks is None else (2 * chips * rows, columns // 2)
        shapes.append(jax.ShapeDtypeStruct(shape, LOW))
    return pl.pallas_call(
        partial(gather_kernel, chips, splits),
        out_shape=tuple(shapes),
        in_specs=[any_space] * 5,
        out_specs=tuple([vmem] * 5),
        scratch_shapes=[
            pltpu.SemaphoreType.DMA((160,)),
            pltpu.SemaphoreType.DMA((160,)),
            pltpu.SemaphoreType.DMA((32,)),
        ],
        compiler_params=pltpu.CompilerParams(
            collective_id=0, has_side_effects=True, vmem_limit_bytes=40 << 20
        ),
    )(packed, *matrices)


def reduce_kernel(chips, chunks, blocks_of, *refs):
    grads, sums_in = refs[:4], refs[4]
    outs, sums_out = refs[5:9], refs[9]
    scratch = refs[10:]
    count = len(chunks)
    across, from_x, from_y, mine, from_z, totals = [
        scratch[k * count : (k + 1) * count] for k in range(6)
    ]
    sums_came, rep_came, rep_sent, send, recv = scratch[6 * count :]
    at = Place(chips)
    copies = Copies(send, recv, at)
    peers = [at.other(chip=lax.rem(at.chip + step, chips)) for step in range(1, chips)]
    at.greet(at.neighbours())
    x_side, y_side = at.other(x=1), at.other(y=1)
    rep_x, rep_y, rep_xy = at.flipped(1), at.flipped(2), at.flipped(3)

    def view(n):
        index, first, width = chunks[n]
        return grads[index], pl.ds(first, width), grads[index].shape[2] // 2

    def send_across(n):
        grad, columns, half = view(n)
        upper, lower = pl.ds(0, half), pl.ds(half, half)
        copies.start(("ax", n), grad.at[:, rep_xy, upper, columns], across[n].at[0], x_side)
        copies.start(("ay", n), grad.at[:, rep_xy, lower, columns], across[n].at[1], y_side)
        copies.start(("bx", n), grad.at[:, rep_x, upper, columns], from_x[n].at[:, upper], x_side)
        copies.start(("by", n), grad.at[:, rep_y, lower, columns], from_y[n].at[:, lower], y_side)

    def add_across(n):
        grad, columns, half = view(n)
        upper, lower = pl.ds(0, half), pl.ds(half, half)
        copies.arrived(("ay", n), across[n].at[1])
        across[n][1] = (
            across[n][1].astype(F32) + grad[:, rep_x, half : 2 * half, columns].astype(F32)
        ).astype(LOW)
        copies.start(("cx", n), across[n].at[1], from_x[n].at[:, lower], x_side)
        copies.arrived(("ax", n), across[n].at[0])
        across[n][0] = (
            across[n][0].astype(F32) + grad[:, rep_y, 0:half, columns].astype(F32)
        ).astype(LOW)
        copies.start(("cy", n), across[n].at[0], from_y[n].at[:, upper], y_side)

    def add_reps(n):
        grad, columns, half = view(n)
        upper, lower = pl.ds(0, half), pl.ds(half, half)
        copies.arrived(("bx", n), from_x[n].at[:, upper])
        copies.arrived(("by", n), from_y[n].at[:, lower])
        copies.arrived(("cx", n), from_x[n].at[:, lower])
        copies.arrived(("cy", n), from_y[n].at[:, upper])
        mine[n][...] = (
            grad[:, at.rep, :, columns].astype(F32)
            + from_x[n][...].astype(F32)
            + from_y[n][...].astype(F32)
        ).astype(LOW)
        for step in range(1, chips):
            chip = lax.rem(at.chip + step, chips)
            copies.start(("z", n, step), mine[n].at[chip], from_z[n].at[step - 1], peers[step - 1])

    def add_chips(n):
        grad, columns, half = view(n)
        for step in range(1, chips):
            copies.arrived(("z", n, step), from_z[n].at[step - 1])
        total = (
            grad[at.chip, at.rep, :, columns].astype(F32)
            + from_x[n][at.chip].astype(F32)
            + from_y[n][at.chip].astype(F32)
        )
        for step in range(chips - 1):
            total = total + from_z[n][step].astype(F32)
        totals[n][at.rep] = total.astype(LOW)
        own = totals[n].at[at.rep]
        copies.start(("ex", n), own, own, x_side)
        copies.start(("ey", n), own, own, y_side)

    def spread(n):
        grad, columns, half = view(n)
        copies.arrived(("ex", n), totals[n].at[rep_x])
        part = totals[n].at[rep_x, pl.ds(0, half)]
        copies.start(("exy", n), part, part, y_side)
        copies.arrived(("ey", n), totals[n].at[rep_y])
        part = totals[n].at[rep_y, pl.ds(half, half)]
        copies.start(("eyx", n), part, part, x_side)

    def sides(n):
        index, first, width = chunks[n]
        block = blocks_of[index]
        for start in range(0, width, block):
            yield start, ((first + start) // block) * 2, block

    def deliver(n):
        index, first, width = chunks[n]
        half = grads[index].shape[2] // 2
        copies.arrived(("exy", n), totals[n].at[rep_xy, pl.ds(0, half)])
        copies.arrived(("eyx", n), totals[n].at[rep_xy, pl.ds(half, half)])
        if blocks_of[index] is None:
            outs[index][:, :, first : first + width] = totals[n][...]
            return
        for start, place, block in sides(n):
            columns = pl.ds(pl.multiple_of((place + at.core) * block, block), block)
            copies.start(
                ("pair", n, start),
                totals[n].at[pl.ds(2 * (1 - at.core), 2), :, pl.ds(start, block)],
                outs[index].at[:, :, columns],
                at.other(core=1),
            )
            outs[index][:, :, columns] = totals[n][pl.ds(2 * at.core, 2), :, start : start + block]

    def receive(n):
        index = chunks[n][0]
        if blocks_of[index] is None:
            return
        for start, place, block in sides(n):
            columns = pl.ds(pl.multiple_of((place + 1 - at.core) * block, block), block)
            copies.arrived(("pair", n, start), outs[index].at[:, :, columns])

    for step in range(1, 2 * chips):
        target = at.shard_at(step)
        copies.start(
            ("sum", step), sums_in.at[target], sums_came.at[step - 1], {"shard": target, "rep": at.rep}
        )
    stages = (send_across, add_across, add_reps, add_chips, spread, deliver, receive)
    for time in range(count + 2 * len(stages)):
        for k, stage in enumerate(stages):
            n = time - (k if k < 2 else 2 * k - 2)
            if 0 <= n < count:
                stage(n)
        if time == 1:
            total = sums_in[at.shard]
            for step in range(1, 2 * chips):
                copies.arrived(("sum", step), sums_came.at[step - 1])
                total = total + sums_came[step - 1]
            rep_sent[0] = total
            copies.start(("sumx",), rep_sent.at[0], rep_came.at[0], x_side)
        if time == 2:
            copies.arrived(("sumx",), rep_came.at[0])
            rep_sent[1] = rep_sent[0] + rep_came[0]
            copies.start(("sumy",), rep_sent.at[1], rep_came.at[1], y_side)
        if time == 3:
            copies.arrived(("sumy",), rep_came.at[1])
            sums_out[...] = rep_sent[1] + rep_came[1]
    copies.finish()


def reduce_grads(grads, sums, blocks_of, chips, chunk_width):
    chunks = []
    views = [grad.reshape(chips, 4, grad.shape[0] // (4 * chips), grad.shape[1]) for grad in grads]
    for index in (3, 2, 1, 0):
        for first in range(0, views[index].shape[3], chunk_width):
            chunks.append((index, first, min(chunk_width, views[index].shape[3] - first)))
    vmem = pl.BlockSpec(memory_space=pltpu.VMEM)
    out_shapes = []
    for member, block in zip(views, blocks_of):
        quarter, columns = member.shape[2:]
        shape = (4, quarter, columns) if block is None else (2, quarter, 2 * columns)
        out_shapes.append(jax.ShapeDtypeStruct(shape, LOW))
    out_shapes.append(jax.ShapeDtypeStruct(sums.shape[1:], F32))
    shapes = [(views[index].shape[2], width) for index, _, width in chunks]
    scratch = [pltpu.VMEM((2, chips, q // 2, w), LOW) for q, w in shapes]
    for _ in range(3):
        scratch += [pltpu.VMEM((chips, q, w), LOW) for q, w in shapes]
    scratch += [pltpu.VMEM((chips - 1, q, w), LOW) for q, w in shapes]
    scratch += [pltpu.VMEM((4, q, w), LOW) for q, w in shapes]
    scratch += [
        pltpu.VMEM((2 * chips - 1,) + sums.shape[1:], F32),
        pltpu.VMEM((2,) + sums.shape[1:], F32),
        pltpu.VMEM((2,) + sums.shape[1:], F32),
        pltpu.SemaphoreType.DMA((240,)),
        pltpu.SemaphoreType.DMA((240,)),
    ]
    reduced = pl.pallas_call(
        partial(reduce_kernel, chips, chunks, blocks_of),
        out_shape=tuple(out_shapes),
        in_specs=[vmem] * 5,
        out_specs=tuple([vmem] * 5),
        scratch_shapes=scratch,
        compiler_params=pltpu.CompilerParams(
            collective_id=1, has_side_effects=True, vmem_limit_bytes=60 << 20
        ),
    )(*views, sums)
    flat = [member.reshape(-1, member.shape[2]).astype(F32) for member in reduced[:4]]
    return flat, reduced[4]


def shards(
    chips,
    reps,
    tokens,
    cotangent,
    seq_lengths,
    dealing,
    attention_gain,
    attention_shift,
    input_weight,
    query_bias,
    value_bias,
    output_weight,
    output_bias,
    feed_gain,
    feed_shift,
    up_weight,
    up_bias,
    down_weight,
    down_bias,
):
    links = Links(chips, reps)
    core, chip = links.core, links.chip
    micro, tok_rows, width = tokens.shape
    shard_count = 2 * chips
    own_rows = micro * tok_rows
    blocks = 2 * tok_rows // BLOCK

    def own_of(values):
        return pick(values.reshape(micro, 2, tok_rows, -1), core, 1).reshape(own_rows, -1)

    def other_of(values):
        return pick(values.reshape(micro, 2, tok_rows, -1), 1 - core, 1).reshape(own_rows, -1)

    def pair_rows(own):
        came = links.swap(own, core=1)
        shape = (micro, 1, tok_rows, own.shape[-1])
        return links.by_core(own.reshape(shape), came.reshape(shape), 1).reshape(2 * own_rows, -1)

    def pair_sum(partial_values):
        return own_of(partial_values) + links.swap(other_of(partial_values), core=1)

    vectors = (
        attention_gain,
        attention_shift,
        query_bias,
        value_bias,
        output_bias,
        feed_gain,
        feed_shift,
        down_bias,
        up_bias,
    )
    lengths = [member.shape[0] for member in vectors]
    packed_length = sum(lengths)
    fast = reps == 4
    lines = -(-packed_length // (16 * BLOCK)) * 16

    def pad_lines(values):
        values = jnp.pad(values, ((0, 0), (0, lines * BLOCK - packed_length)))
        return values.reshape(-1, lines, BLOCK)

    packed_in = jnp.concatenate(vectors)
    if fast:
        table, input_part, output_part, up_part, down_part = gather_weights(
            pad_lines(packed_in[None])[0],
            (input_weight, output_weight, up_weight, down_weight),
            (3 * chips, None, chips, None),
            chips,
        )
        table = table.reshape(shard_count, -1)[:, :packed_length].astype(F32)
    else:
        table = links.gather_vectors(packed_in).astype(F32)
        input_part = links.gather(links.halves(input_weight, 3))
        output_part = links.gather(output_weight)
        up_part = links.gather(links.halves(up_weight, 1))
        down_part = links.gather(down_weight)
    wholes, at = [], 0
    for length in lengths:
        wholes.append(table[:, at : at + length])
        at += length

    def whole(index):
        return wholes[index].reshape(1, -1)

    def core_part(index):
        return pick(wholes[index].reshape(chips, 2, -1), core, 1).reshape(1, -1)

    inputs = tokens.reshape(own_rows, width).astype(F32)
    unit_one, inverse_one = normalize(inputs)
    normed = (unit_one * whole(0) + whole(1)).astype(LOW)
    chip_normed = pair_rows(normed)
    tail = chip_normed.reshape(micro, 2 * tok_rows, width)[:, 2 * tok_rows - BLOCK :]
    halo = links.shift(tail.reshape(micro * BLOCK, width), 1)
    all_normed = jnp.concatenate([chip_normed, halo], axis=0)
    down_low = pair_rows(cotangent.reshape(own_rows, width))
    first = chip * 2 * tok_rows
    starts = jnp.stack(
        [
            sequence_starts(seq_lengths[m, 0], dealing[m, 0], first, 2 * tok_rows)
            for m in range(micro)
        ]
    )
    block_first = first + jnp.arange(2 * tok_rows, dtype=jnp.int32) // BLOCK * BLOCK - BLOCK
    starts = (starts - block_first[None, :]).reshape(2 * own_rows, 1)

    half = width // 2
    bias = jnp.concatenate([core_part(2), jnp.zeros((1, half), F32), core_part(3)], axis=1)
    mixed = (dot(all_normed, input_part) + bias).astype(LOW)
    branch = attention(mixed, starts, blocks)
    middle = inputs + pair_sum(dot(branch, output_part)) + whole(4)
    unit_two, inverse_two = normalize(middle)
    normed_two = pair_rows((unit_two * whole(5) + whole(6)).astype(LOW))
    hidden = dot(normed_two, up_part) + core_part(8)
    activated, gelu_back = jax.vjp(gelu_tanh, hidden)
    activated = activated.astype(LOW)
    down_partial = rows_dot(activated, down_low).astype(LOW)
    result = middle + pair_sum(dot(activated, down_part)) + whole(7)

    upstream = cotangent.reshape(own_rows, width).astype(F32)
    (hidden_grad,) = gelu_back(back_dot(down_low, down_part))
    hidden_low = hidden_grad.astype(LOW)
    up_partial = rows_dot(normed_two, hidden_low).astype(LOW)
    upper_two = pair_sum(back_dot(hidden_low, up_part))
    middle_grad = upstream + normalize_back(upper_two, whole(5), unit_two, inverse_two)
    output_own = middle_grad.astype(LOW)
    output_low = pair_rows(output_own)
    output_partial = rows_dot(branch, output_low).astype(LOW)
    attended = back_dot(output_low, output_part).astype(LOW)
    mixed_grad = attention_back(mixed, starts, attended, blocks)
    input_partial = rows_dot(all_normed, mixed_grad).astype(LOW)
    back_halo = links.shift(mixed_grad[2 * own_rows :, half:], -1)
    body = mixed_grad[: 2 * own_rows].reshape(micro, 2 * tok_rows, 3 * half)
    tail_grad = body[:, 2 * tok_rows - BLOCK :, half:].astype(F32) + back_halo.reshape(
        micro, BLOCK, width
    ).astype(F32)
    body = body.at[:, 2 * tok_rows - BLOCK :, half:].set(tail_grad.astype(LOW))
    upper_one = pair_sum(back_dot(body.reshape(2 * own_rows, 3 * half), input_part))
    input_grad = middle_grad + normalize_back(upper_one, whole(0), unit_one, inverse_one)

    def by_shard(values):
        return values.reshape(shard_count, -1)

    def by_core_shard(values):
        spread = values.reshape(chips, 1, -1)
        mask = jnp.arange(2, dtype=jnp.int32)[None, :, None] == core
        return jnp.where(mask, spread, 0.0).reshape(shard_count, -1)

    def column_sum(values):
        return jnp.sum(values.astype(F32), axis=0)

    packed = jnp.concatenate(
        [
            by_shard(column_sum(upper_one * unit_one)),
            by_shard(column_sum(upper_one)),
            by_core_shard(column_sum(mixed_grad[:, :half])),
            by_core_shard(column_sum(mixed_grad[:, width:])),
            by_shard(column_sum(output_own)),
            by_shard(column_sum(upper_two * unit_two)),
            by_shard(column_sum(upper_two)),
            by_shard(column_sum(upstream)),
            by_core_shard(column_sum(hidden_low)),
        ],
        axis=1,
    )
    if fast:
        grads, sums = reduce_grads(
            (input_partial, output_partial, up_partial, down_partial),
            pad_lines(packed),
            (width // shard_count, None, up_part.shape[1] // chips, None),
            chips,
            512,
        )
        input_weight_grad, output_grad, up_grad, down_grad = grads
        sums = sums.reshape(-1)[:packed_length]
    else:
        sums = links.reduce_vectors(packed)
        input_weight_grad = links.unhalves(links.reduce(input_partial), 3).astype(F32)
        output_grad = links.reduce(output_partial).astype(F32)
        up_grad = links.unhalves(links.reduce(up_partial), 1).astype(F32)
        down_grad = links.reduce(down_partial).astype(F32)
    vector_grads, at = [], 0
    for length in lengths:
        vector_grads.append(sums[at : at + length])
        at += length
    return (
        result.astype(LOW).reshape(tokens.shape),
        input_grad.astype(LOW).reshape(tokens.shape),
        vector_grads[0],
        vector_grads[1],
        input_weight_grad,
        vector_grads[2],
        vector_grads[3],
        output_grad,
        vector_grads[4],
        vector_grads[5],
        vector_grads[6],
        up_grad,
        vector_grads[8],
        down_grad,
        vector_grads[7],
    )


def solution(mesh):
    rows_spec = P(None, ("shard", "rep"), None)
    vector, matrix = P("shard"), P("shard", None)
    weight_specs = (
        vector,
        vector,
        matrix,
        vector,
        vector,
        matrix,
        vector,
        vector,
        vector,
        matrix,
        vector,
        matrix,
        vector,
    )
    return jax.shard_map(
        partial(shards, mesh.shape["shard"] // 2, mesh.shape["rep"]),
        mesh=mesh,
        in_specs=(rows_spec, rows_spec, P(None, "rep", None, None), P(None, "rep", None))
        + weight_specs,
        out_specs=(rows_spec, rows_spec) + weight_specs,
        check_vma=False,
    )
```

```python
from functools import partial

import jax
import jax.numpy as jnp
from jax import lax
from jax.experimental import pallas as pl
from jax.experimental.pallas import tpu as pltpu
from jax.sharding import PartitionSpec as P

HD = 64
BLOCK = 128
EPSILON = 1e-05
MASKED = -1e30
AXES = ("shard", "rep")
F32 = jnp.float32
LOW = jnp.bfloat16


def dot(left, right):
    return jnp.dot(left, right, preferred_element_type=F32)


def rows_dot(left, right):
    return lax.dot_general(left, right, (((0,), (0,)), ((), ())), preferred_element_type=F32)


def back_dot(left, right):
    return lax.dot_general(left, right, (((1,), (1,)), ((), ())), preferred_element_type=F32)


def pick(stacked, index, axis=0):
    return lax.dynamic_index_in_dim(stacked, index, axis, keepdims=False)


def normalize(values):
    center = values - jnp.mean(values, axis=-1, keepdims=True)
    inverse = lax.rsqrt(jnp.mean(center * center, axis=-1, keepdims=True) + EPSILON)
    return center * inverse, inverse


def normalize_back(upper, gain, unit, inverse):
    scaled = upper * gain
    mean_scaled = jnp.mean(scaled, axis=-1, keepdims=True)
    mean_product = jnp.mean(scaled * unit, axis=-1, keepdims=True)
    return inverse * (scaled - mean_scaled - unit * mean_product)


def gelu_tanh(values):
    return jax.nn.gelu(values, approximate=True)


def sequence_starts(seq_lengths, dealing, first, rows):
    total = dealing.shape[0]
    numbers = jnp.arange(total, dtype=jnp.int32)
    matched = (dealing[:, None] == numbers[None, :]).astype(jnp.int32)
    packed_length = jnp.sum(matched * seq_lengths.reshape(total)[None, :], axis=1)
    before = (numbers[None, :] < numbers[:, None]).astype(jnp.int32)
    packed_start = jnp.sum(before * packed_length[None, :], axis=1)
    own = first + jnp.arange(rows, dtype=jnp.int32)
    return jnp.max(
        jnp.where(packed_start[None, :] <= own[:, None], packed_start[None, :], 0), axis=1
    )


def window(ref, row, previous, column):
    return jnp.concatenate(
        [
            ref[pl.ds(previous, BLOCK), column : column + BLOCK],
            ref[pl.ds(row, BLOCK), column : column + BLOCK],
        ],
        axis=0,
    )


def block_rows(step, blocks, body_rows):
    micro, block = step // blocks, step % blocks
    row = pl.multiple_of(step * BLOCK, BLOCK)
    previous = jnp.where(block == 0, body_rows + micro * BLOCK, row - BLOCK)
    return row, pl.multiple_of(previous, BLOCK)


def soft_weights(query_half, keys, allowed):
    scores = back_dot(query_half, keys) * float(HD) ** (-0.5)
    scores = jnp.where(allowed, scores, MASKED)
    top = jnp.max(scores, axis=1, keepdims=True)
    powers = jnp.exp(scores - top)
    return powers / jnp.sum(powers, axis=1, keepdims=True)


def allowed_keys(start_ref, row):
    places = lax.broadcasted_iota(jnp.int32, (BLOCK, 2 * BLOCK), 1)
    lines = lax.broadcasted_iota(jnp.int32, (BLOCK, 2 * BLOCK), 0)
    return (places >= start_ref[pl.ds(row, BLOCK), :]) & (places <= lines + BLOCK)


def attention_kernel(blocks, width, mixed_ref, start_ref, branch_ref):
    body_rows = branch_ref.shape[0]
    left = lax.broadcasted_iota(jnp.int32, (BLOCK, BLOCK), 1) < HD

    def step_body(step, _):
        row, previous = block_rows(step, blocks, body_rows)
        allowed = allowed_keys(start_ref, row)
        for column in range(0, width, BLOCK):
            queries = mixed_ref[pl.ds(row, BLOCK), column : column + BLOCK]
            keys = window(mixed_ref, row, previous, width + column)
            values = window(mixed_ref, row, previous, 2 * width + column)
            parts = []
            for half in (left, ~left):
                soft = soft_weights(jnp.where(half, queries, 0), keys, allowed)
                parts.append(dot(soft.astype(LOW), values))
            branch_ref[pl.ds(row, BLOCK), column : column + BLOCK] = jnp.where(
                left, parts[0], parts[1]
            ).astype(LOW)
        return 0

    lax.fori_loop(0, body_rows // BLOCK, step_body, 0)


def attention_back_kernel(blocks, width, mixed_ref, start_ref, upper_ref, grad_ref, sums_ref):
    body_rows = upper_ref.shape[0]
    left = lax.broadcasted_iota(jnp.int32, (BLOCK, BLOCK), 1) < HD
    left_tall = lax.broadcasted_iota(jnp.int32, (2 * BLOCK, BLOCK), 1) < HD
    scale = float(HD) ** (-0.5)
    sums_ref[...] = jnp.zeros_like(sums_ref)

    def step_body(step, _):
        row, previous = block_rows(step, blocks, body_rows)
        allowed = allowed_keys(start_ref, row)
        for column in range(0, width, BLOCK):
            queries = mixed_ref[pl.ds(row, BLOCK), column : column + BLOCK]
            keys = window(mixed_ref, row, previous, width + column)
            values = window(mixed_ref, row, previous, 2 * width + column)
            upper = upper_ref[pl.ds(row, BLOCK), column : column + BLOCK]
            parts = []
            for half in (left, ~left):
                soft = soft_weights(jnp.where(half, queries, 0), keys, allowed)
                soft_grad = back_dot(jnp.where(half, upper, 0), values)
                total = jnp.sum(soft * soft_grad, axis=1, keepdims=True)
                score_low = (soft * (soft_grad - total)).astype(LOW)
                parts.append(
                    (
                        dot(score_low, keys) * scale,
                        rows_dot(score_low, queries) * scale,
                        rows_dot(soft.astype(LOW), upper),
                    )
                )
            grad_ref[pl.ds(row, BLOCK), column : column + BLOCK] = jnp.where(
                left, parts[0][0], parts[1][0]
            ).astype(LOW)
            for slot in (1, 2):
                joined = jnp.where(left_tall, parts[0][slot], parts[1][slot])
                place = (slot - 1) * width + column
                sums_ref[pl.ds(previous, BLOCK), place : place + BLOCK] += joined[:BLOCK]
                sums_ref[pl.ds(row, BLOCK), place : place + BLOCK] += joined[BLOCK:]
        return 0

    lax.fori_loop(0, body_rows // BLOCK, step_body, 0)
    grad_ref[:, width:] = sums_ref[...].astype(LOW)
    grad_ref[body_rows:, :width] = jnp.zeros((grad_ref.shape[0] - body_rows, width), LOW)


def attention(mixed, starts, blocks):
    width = mixed.shape[1] // 3
    rows = starts.shape[0]
    vmem = pl.BlockSpec(memory_space=pltpu.VMEM)
    return pl.pallas_call(
        partial(attention_kernel, blocks, width),
        out_shape=jax.ShapeDtypeStruct((rows, width), LOW),
        in_specs=[vmem, vmem],
        out_specs=vmem,
        cost_estimate=pl.CostEstimate(
            flops=rows * width * BLOCK * 16, bytes_accessed=8 << 20, transcendentals=0
        ),
        compiler_params=pltpu.CompilerParams(vmem_limit_bytes=40 << 20),
    )(mixed, starts)


def attention_back(mixed, starts, upper, blocks):
    width = mixed.shape[1] // 3
    rows = starts.shape[0]
    vmem = pl.BlockSpec(memory_space=pltpu.VMEM)
    return pl.pallas_call(
        partial(attention_back_kernel, blocks, width),
        out_shape=jax.ShapeDtypeStruct(mixed.shape, LOW),
        in_specs=[vmem, vmem, vmem],
        out_specs=vmem,
        scratch_shapes=[pltpu.VMEM((mixed.shape[0], 2 * width), F32)],
        cost_estimate=pl.CostEstimate(
            flops=rows * width * BLOCK * 40, bytes_accessed=16 << 20, transcendentals=0
        ),
        compiler_params=pltpu.CompilerParams(vmem_limit_bytes=40 << 20),
    )(mixed, starts, upper)


class Links:
    def __init__(self, chips, reps):
        self.chips, self.reps = chips, reps
        shard = lax.axis_index("shard")
        self.chip, self.core, self.rep = shard // 2, shard % 2, lax.axis_index("rep")

    def flat(self, chip, core, rep):
        return (chip * 2 + core) * self.reps + rep

    def swap(self, values, chip=0, core=0, rep=0):
        pairs = [
            (self.flat(a, b, d), self.flat(a ^ chip, b ^ core, d ^ rep))
            for a in range(self.chips)
            for b in range(2)
            for d in range(self.reps)
        ]
        return lax.ppermute(values, AXES, pairs)

    def shift(self, values, by):
        pairs = [
            (self.flat(a, b, d), self.flat(a + by, b, d))
            for a in range(self.chips)
            if 0 <= a + by < self.chips
            for b in range(2)
            for d in range(self.reps)
        ]
        return lax.ppermute(values, AXES, pairs)

    def by_core(self, own, other, axis):
        first = jnp.where(self.core == 0, own, other)
        second = jnp.where(self.core == 0, other, own)
        return jnp.concatenate([first, second], axis=axis)

    def halves(self, matrix, parts):
        rows, columns = matrix.shape
        blocks = self.chips * parts
        view = matrix.reshape(rows, blocks, 2, columns // (2 * blocks))
        keep = pick(view, self.core, 2).reshape(rows, columns // 2)
        give = pick(view, 1 - self.core, 2).reshape(rows, columns // 2)
        return self.by_core(keep, self.swap(give, core=1), 0)

    def gather(self, chip_rows):
        rows, columns = chip_rows.shape
        quarter = rows // self.reps
        quarters = chip_rows.reshape(self.reps, quarter, columns)
        piece = pick(quarters, self.rep)
        pieces = jnp.stack([self.swap(piece, chip=j) for j in range(1, self.chips)])
        found = [pieces] + [None] * (self.reps - 1)
        if self.reps == 4:
            half = quarter // 2
            found[1] = self.swap(pieces, rep=1)
            found[2] = self.swap(pieces, rep=2)
            upper = self.swap(found[1][:, :half], rep=2)
            lower = self.swap(found[2][:, half:], rep=1)
            found[3] = jnp.concatenate([upper, lower], axis=1)
        else:
            for j in range(1, self.reps):
                found[j] = self.swap(pieces, rep=j)
        stacked = jnp.stack(
            [
                jnp.concatenate([pick(quarters, self.rep ^ j)[None], found[j]], axis=0)
                for j in range(self.reps)
            ]
        )
        ordered = []
        for chip in range(self.chips):
            for rep in range(self.reps):
                at = (self.rep ^ rep, self.chip ^ chip, 0, 0)
                ordered.append(
                    lax.dynamic_slice(stacked, at, (1, 1, quarter, columns)).reshape(
                        quarter, columns
                    )
                )
        return jnp.concatenate(ordered, axis=0)

    def reduce(self, grads):
        chips, reps = self.chips, self.reps
        rows, columns = grads.shape
        quarter = rows // (chips * reps)
        view = grads.astype(LOW).reshape(chips, reps, quarter, columns)
        mine = pick(view, self.rep, 1).astype(F32)
        if reps == 4:
            half = quarter // 2
            across = pick(view, self.rep ^ 3, 1)
            upper = self.swap(across[:, :half], rep=1)
            lower = self.swap(across[:, half:], rep=2)
            to_x = pick(view, self.rep ^ 1, 1)
            to_y = pick(view, self.rep ^ 2, 1)
            to_x = jnp.concatenate(
                [to_x[:, :half], (to_x[:, half:].astype(F32) + lower.astype(F32)).astype(LOW)],
                axis=1,
            )
            to_y = jnp.concatenate(
                [(to_y[:, :half].astype(F32) + upper.astype(F32)).astype(LOW), to_y[:, half:]],
                axis=1,
            )
            mine = (
                mine + self.swap(to_x, rep=1).astype(F32) + self.swap(to_y, rep=2).astype(F32)
            )
        else:
            for j in range(1, reps):
                mine = mine + self.swap(pick(view, self.rep ^ j, 1), rep=j).astype(F32)
        total = pick(mine, self.chip)
        sends = mine.astype(LOW)
        for j in range(1, chips):
            total = total + self.swap(pick(sends, self.chip ^ j), chip=j).astype(F32)
        return self.spread(total.astype(LOW))

    def spread(self, own):
        if self.reps == 4:
            half = own.shape[0] // 2
            from_x = self.swap(own, rep=1)
            from_y = self.swap(own, rep=2)
            upper = self.swap(from_x[:half], rep=2)
            lower = self.swap(from_y[half:], rep=1)
            found = [own, from_x, from_y, jnp.concatenate([upper, lower], axis=0)]
        else:
            found = [own] + [self.swap(own, rep=j) for j in range(1, self.reps)]
        stacked = jnp.stack(found)
        return jnp.concatenate([pick(stacked, self.rep ^ j) for j in range(self.reps)], axis=0)

    def unhalves(self, chip_rows, parts):
        rows, columns = chip_rows.shape
        view = chip_rows.reshape(2, rows // 2, columns)
        blocks = self.chips * parts
        keep = pick(view, self.core).reshape(rows // 2, blocks, 1, columns // blocks)
        came = self.swap(pick(view, 1 - self.core), core=1)
        came = came.reshape(rows // 2, blocks, 1, columns // blocks)
        return self.by_core(keep, came, 2).reshape(rows // 2, 2 * columns)

    def gather_vectors(self, packed):
        pair = self.by_core(packed[None], self.swap(packed, core=1)[None], 0)
        found = jnp.stack([pair] + [self.swap(pair, chip=j) for j in range(1, self.chips)])
        ordered = [pick(found, self.chip ^ j) for j in range(self.chips)]
        return jnp.concatenate(ordered, axis=0)

    def reduce_vectors(self, partial_sums):
        chips, reps = self.chips, self.reps
        view = partial_sums.reshape(chips, 2, -1)
        total = None
        for a in range(chips):
            for b in range(2):
                row = pick(pick(view, self.chip ^ a), self.core ^ b)
                row = row if a == b == 0 else self.swap(row, chip=a, core=b)
                total = row if total is None else total + row
        terms = [total] + [self.swap(total, rep=j) for j in range(1, reps)]
        while len(terms) > 1:
            terms = [terms[i] + terms[i + 1] for i in range(0, len(terms), 2)]
        return terms[0]

class Copies:
    def __init__(self, send, recv, links):
        self.send, self.recv, self.links = send, recv, links
        self.places, self.started = {}, []

    def make(self, name, source, target, device):
        place = self.places.setdefault(name, len(self.places))
        return pltpu.make_async_remote_copy(
            src_ref=source,
            dst_ref=target,
            send_sem=self.send.at[place],
            recv_sem=self.recv.at[place],
            device_id=device,
            device_id_type=pl.DeviceIdType.MESH,
        )

    def start(self, name, source, target, device, when=None):
        copy = self.make(name, source, target, device)
        run_when(when, copy.start)
        self.started.append((name, when, copy))

    def arrived(self, name, target, when=None):
        copy = self.make(name, target, target, self.links.other(x=1))
        run_when(when, copy.wait_recv)

    def sent(self, name):
        for item in [item for item in self.started if item[0] == name]:
            run_when(item[1], item[2].wait_send)
            self.started.remove(item)

    def finish(self):
        for _, when, copy in self.started:
            run_when(when, copy.wait_send)


def run_when(when, body):
    if when is None:
        body()
    else:
        pl.when(when)(body)


class Place:
    def __init__(self, chips):
        shard = lax.axis_index("shard")
        self.chips, self.shard = chips, shard
        self.chip, self.core, self.rep = shard // 2, lax.rem(shard, 2), lax.axis_index("rep")

    def flipped(self, bits):
        x, y = lax.rem(self.rep, 2), self.rep // 2
        x = 1 - x if bits & 1 else x
        y = 1 - y if bits & 2 else y
        return y * 2 + x

    def other(self, x=0, y=0, core=0, chip=None):
        chip = self.chip if chip is None else chip
        side = 1 - self.core if core else self.core
        return {"shard": chip * 2 + side, "rep": self.flipped(x + 2 * y)}

    def shard_at(self, step):
        return lax.rem(self.shard + step, 2 * self.chips)

    def greet(self, barrier_devices):
        barrier = pltpu.get_barrier_semaphore()
        for device in barrier_devices:
            pl.semaphore_signal(barrier, 1, device_id=device, device_id_type=pl.DeviceIdType.MESH)
        pl.semaphore_wait(barrier, len(barrier_devices))

    def neighbours(self):
        shards = [
            {"shard": self.shard_at(step), "rep": self.rep} for step in range(1, 2 * self.chips)
        ]
        return shards + [self.other(x=1), self.other(y=1)]


def gather_kernel(
    chips, splits, vec_in, in_in, out_in, up_in, down_in, *refs
):
    table, wholes, (send, recv, local) = refs[0], refs[1:5], refs[5:]
    shards_in = (in_in, out_in, up_in, down_in)
    at = Place(chips)
    copies = Copies(send, recv, at)
    at.greet(at.neighbours())
    own_copies = []

    def keep(source, target):
        copy = pltpu.make_async_copy(source, target, local.at[len(own_copies)])
        copy.start()
        own_copies.append(copy)

    keep(vec_in, table.at[at.shard])
    for step in range(1, 2 * chips):
        copies.start(
            ("vec", step), vec_in, table.at[at.shard], {"shard": at.shard_at(step), "rep": at.rep}
        )
    kept = []
    for index, (source, whole, blocks) in enumerate(zip(shards_in, wholes, splits)):
        rows = source.shape[0]
        first = len(own_copies)
        if blocks is None:
            keep(source, whole.at[pl.ds(pl.multiple_of(at.chip * rows, rows), rows)])
        else:
            width = source.shape[1] // (2 * blocks)
            place = pl.ds(pl.multiple_of(at.shard * rows, rows), rows)
            for block in range(blocks):
                columns = pl.ds(block * width, width)

                def side(core):
                    return pl.ds(pl.multiple_of((2 * block + core) * width, width), width)

                copies.start(
                    ("pair", index, block),
                    source.at[:, side(1 - at.core)],
                    whole.at[place, columns],
                    at.other(core=1),
                )
                keep(source.at[:, side(at.core)], whole.at[place, columns])
        kept.append(own_copies[first:])

    def piece(index, chip, part=None):
        whole = wholes[index]
        rows = whole.shape[0] // chips
        quarter = rows // 4
        if splits[index] is None and index == 1:
            return whole.at[pl.ds(pl.multiple_of(chip * rows, rows), rows)]
        start, size = chip * rows + at.rep * quarter, quarter
        if part is not None:
            bits, piece_half = part
            start = chip * rows + at.flipped(bits) * quarter
            if piece_half is not None:
                size = quarter // 2
                start = start + piece_half * size
        return whole.at[pl.ds(pl.multiple_of(start, size), size)]

    ways = (("up", 1), ("down", -1))

    def neighbour(step):
        return at.other(chip=jnp.clip(at.chip + step, 0, chips - 1))

    def can_send(step):
        return at.chip < chips - 1 if step > 0 else at.chip > 0

    def has(step, distance):
        return at.chip >= distance if step > 0 else at.chip + distance < chips

    def open_z(index):
        for copy in kept[index]:
            copy.wait()
        if splits[index] is not None:
            rows = shards_in[index].shape[0]
            width = shards_in[index].shape[1] // (2 * splits[index])
            place = pl.ds(pl.multiple_of((at.chip * 2 + 1 - at.core) * rows, rows), rows)
            for block in range(splits[index]):
                copies.arrived(
                    ("pair", index, block), wholes[index].at[place, pl.ds(block * width, width)]
                )
        for name, step in ways:
            mine = piece(index, at.chip)
            copies.start((name, index, 1), mine, mine, neighbour(step), can_send(step))

    def pass_on(index):
        for distance in range(1, chips):
            for name, step in ways:
                when = has(step, distance)
                chip = jnp.clip(at.chip - step * distance, 0, chips - 1)
                found = piece(index, chip)
                copies.arrived((name, index, distance), found, when)
                if distance < chips - 1:
                    copies.start(
                        (name, index, distance + 1),
                        found,
                        found,
                        neighbour(step),
                        when & can_send(step),
                    )
                if index != 1:
                    copies.start(("x", name, index, distance), found, found, at.other(x=1), when)
                    copies.start(("y", name, index, distance), found, found, at.other(y=1), when)

    def across(index):
        if index == 1:
            return
        for distance in range(1, chips):
            for name, step in ways:
                when = has(step, distance)
                chip = jnp.clip(at.chip - step * distance, 0, chips - 1)
                key = (name, index, distance)
                copies.arrived(("x",) + key, piece(index, chip, (1, None)), when)
                upper = piece(index, chip, (1, 0))
                copies.start(("xy",) + key, upper, upper, at.other(y=1), when)
                copies.arrived(("y",) + key, piece(index, chip, (2, None)), when)
                lower = piece(index, chip, (2, 1))
                copies.start(("yx",) + key, lower, lower, at.other(x=1), when)

    def close(index):
        if index == 1:
            return
        for distance in range(1, chips):
            for name, step in ways:
                when = has(step, distance)
                chip = jnp.clip(at.chip - step * distance, 0, chips - 1)
                key = (name, index, distance)
                copies.arrived(("xy",) + key, piece(index, chip, (3, 0)), when)
                copies.arrived(("yx",) + key, piece(index, chip, (3, 1)), when)

    count = len(wholes)
    open_z(0)
    for index in range(count):
        if index + 1 < count:
            open_z(index + 1)
        pass_on(index)
        across(index)
    for index in range(count):
        close(index)
    own_copies[0].wait()
    for step in range(1, 2 * chips):
        copies.arrived(("vec", step), table.at[at.shard_at(2 * chips - step)])
    copies.finish()


def gather_weights(packed, matrices, splits, chips):
    any_space = pl.BlockSpec(memory_space=pl.ANY)
    vmem = pl.BlockSpec(memory_space=pltpu.VMEM)
    shapes = [jax.ShapeDtypeStruct((2 * chips,) + packed.shape, LOW)]
    for matrix, blocks in zip(matrices, splits):
        rows, columns = matrix.shape
        shape = (chips * rows, columns) if blocks is None else (2 * chips * rows, columns // 2)
        shapes.append(jax.ShapeDtypeStruct(shape, LOW))
    return pl.pallas_call(
        partial(gather_kernel, chips, splits),
        out_shape=tuple(shapes),
        in_specs=[any_space] * 5,
        out_specs=tuple([vmem] * 5),
        scratch_shapes=[
            pltpu.SemaphoreType.DMA((160,)),
            pltpu.SemaphoreType.DMA((160,)),
            pltpu.SemaphoreType.DMA((32,)),
        ],
        compiler_params=pltpu.CompilerParams(
            collective_id=0, has_side_effects=True, vmem_limit_bytes=40 << 20
        ),
    )(packed, *matrices)


class Reduction:
    def __init__(self, at, copies, blocks_of, outs):
        self.at, self.copies, self.blocks_of, self.outs = at, copies, blocks_of, outs
        self.x_side, self.y_side = at.other(x=1), at.other(y=1)
        self.rep_x, self.rep_y, self.rep_xy = at.flipped(1), at.flipped(2), at.flipped(3)
        self.chunks = []

    def add(self, index, line, first, grad, across, from_x, from_y, from_z, totals):
        self.chunks.append((index, line, first, grad, across, from_x, from_y, from_z, totals))

    def send_across(self, n):
        _, _, _, grad, across, from_x, from_y, _, _ = self.chunks[n]
        half = grad.shape[2] // 2
        upper, lower = pl.ds(0, half), pl.ds(half, half)
        start = self.copies.start
        start(("ax", n), grad.at[:, self.rep_xy, upper], across.at[0], self.x_side)
        start(("ay", n), grad.at[:, self.rep_xy, lower], across.at[1], self.y_side)
        start(("bx", n), grad.at[:, self.rep_x, upper], from_x.at[:, upper], self.x_side)
        start(("by", n), grad.at[:, self.rep_y, lower], from_y.at[:, lower], self.y_side)

    def add_across(self, n):
        _, _, _, grad, across, from_x, from_y, _, _ = self.chunks[n]
        half = grad.shape[2] // 2
        upper, lower = pl.ds(0, half), pl.ds(half, half)
        self.copies.arrived(("ay", n), across.at[1])
        across[1] = (
            across[1].astype(F32) + grad[:, self.rep_x, half : 2 * half].astype(F32)
        ).astype(LOW)
        self.copies.start(("cx", n), across.at[1], from_x.at[:, lower], self.x_side)
        self.copies.arrived(("ax", n), across.at[0])
        across[0] = (across[0].astype(F32) + grad[:, self.rep_y, 0:half].astype(F32)).astype(LOW)
        self.copies.start(("cy", n), across.at[0], from_y.at[:, upper], self.y_side)

    def add_reps(self, n):
        _, _, _, grad, _, from_x, from_y, from_z, _ = self.chunks[n]
        at, half = self.at, grad.shape[2] // 2
        upper, lower = pl.ds(0, half), pl.ds(half, half)
        self.copies.arrived(("bx", n), from_x.at[:, upper])
        self.copies.arrived(("by", n), from_y.at[:, lower])
        self.copies.arrived(("cx", n), from_x.at[:, lower])
        self.copies.arrived(("cy", n), from_y.at[:, upper])
        from_x[...] = (
            grad[:, at.rep].astype(F32) + from_x[...].astype(F32) + from_y[...].astype(F32)
        ).astype(LOW)
        for step in range(1, at.chips):
            chip = lax.rem(at.chip + step, at.chips)
            self.copies.start(
                ("z", n, step), from_x.at[chip], from_z.at[step - 1], at.other(chip=chip)
            )

    def add_chips(self, n):
        _, _, _, grad, _, from_x, _, from_z, totals = self.chunks[n]
        at = self.at
        total = from_x[at.chip].astype(F32)
        for step in range(1, at.chips):
            self.copies.arrived(("z", n, step), from_z.at[step - 1])
            total = total + from_z[step - 1].astype(F32)
        totals[at.rep] = total.astype(LOW)
        own = totals.at[at.rep]
        self.copies.start(("ex", n), own, own, self.x_side)
        self.copies.start(("ey", n), own, own, self.y_side)

    def spread(self, n):
        totals = self.chunks[n][-1]
        half = totals.shape[1] // 2
        self.copies.arrived(("ex", n), totals.at[self.rep_x])
        part = totals.at[self.rep_x, pl.ds(0, half)]
        self.copies.start(("exy", n), part, part, self.y_side)
        self.copies.arrived(("ey", n), totals.at[self.rep_y])
        part = totals.at[self.rep_y, pl.ds(half, half)]
        self.copies.start(("eyx", n), part, part, self.x_side)

    def sides(self, n):
        index, first, width = self.chunks[n][0], self.chunks[n][2], self.chunks[n][-1].shape[2]
        block = self.blocks_of[index]
        for start in range(0, width, block):
            yield start, ((first + start) // block) * 2, block

    def deliver(self, n):
        index, line, first, totals = *self.chunks[n][:3], self.chunks[n][-1]
        quarter, width = totals.shape[1:]
        half, at = quarter // 2, self.at
        self.copies.arrived(("exy", n), totals.at[self.rep_xy, pl.ds(0, half)])
        self.copies.arrived(("eyx", n), totals.at[self.rep_xy, pl.ds(half, half)])
        out = self.outs[index]
        if self.blocks_of[index] is None:
            out[:, line : line + quarter, first : first + width] = totals[...]
            return
        for start, place, block in self.sides(n):
            columns = pl.ds(pl.multiple_of((place + at.core) * block, block), block)
            self.copies.start(
                ("pair", n, start),
                totals.at[pl.ds(2 * (1 - at.core), 2), :, pl.ds(start, block)],
                out.at[:, :, columns],
                at.other(core=1),
            )
            out[:, :, columns] = totals[pl.ds(2 * at.core, 2), :, start : start + block]

    def receive(self, n):
        index = self.chunks[n][0]
        if self.blocks_of[index] is None:
            return
        for start, place, block in self.sides(n):
            columns = pl.ds(pl.multiple_of((place + 1 - self.at.core) * block, block), block)
            self.copies.arrived(("pair", n, start), self.outs[index].at[:, :, columns])

    def tick(self, time):
        stages = (
            self.send_across,
            self.add_across,
            self.add_reps,
            self.add_chips,
            self.spread,
            self.deliver,
            self.receive,
        )
        for stage, offset in zip(stages, OFFSETS):
            if 0 <= time - offset < len(self.chunks):
                stage(time - offset)


OFFSETS = (0, 1, 2, 3, 5, 6, 7)
PART = 512
VECTOR_ROWS = 16


def loop(count, body):
    def step(index, carry):
        body(index)
        return carry

    lax.fori_loop(0, count, step, 0)


def backward_kernel(chips, micro, blocks, blocks_of, *refs):
    (
        activated_in,
        down_low_in,
        hidden_low_in,
        normed_two_in,
        up_in,
        out_in,
        in_in,
        branch_in,
        mixed_in,
        all_normed_in,
        middle_in,
        tokens_in,
        starts,
        gains,
    ) = refs[:14]
    outs, vectors_out, input_grad_out = refs[14:18], refs[18], refs[19]
    refs = refs[20:]
    (
        wide,
        deep,
        matrix,
        out_matrix,
        low,
        normed,
        branch,
        attended,
        give,
        came,
        middle,
        tokens,
        key_sums,
        halo,
        vectors,
        vectors_came,
    ) = refs[:16]
    send, recv, local = refs[-3:]
    pools = refs[16:-3]
    at = Place(chips)
    core = at.core
    width = down_low_in.shape[1]
    rows = down_low_in.shape[0]
    body_rows, all_rows = rows, mixed_in.shape[0]
    part_width = mixed_in.shape[1] // 3
    hidden_width = hidden_low_in.shape[1]
    own_rows, micro_rows = rows // 2, rows // micro
    own_micro = micro_rows // 2
    copies = Copies(send, recv, at)

    loads = []

    def load(source, target):
        copy = pltpu.make_async_copy(source, target, local.at[len(loads)])
        copy.start()
        loads.append(copy)
        return copy

    activated = wide.at[pl.ds(0, rows)]
    hidden_low = deep.at[pl.ds(0, rows)]
    mixed = wide.at[:, pl.ds(0, 3 * part_width)]
    mixed_grad = deep.at[:, pl.ds(0, 3 * part_width)]
    in_matrix = matrix.at[:, pl.ds(0, 3 * part_width)]
    normed_two = normed.at[pl.ds(0, rows)]
    load_first = [load(activated_in, activated), load(down_low_in, low)]
    load_up = [load(hidden_low_in, hidden_low), load(normed_two_in, normed_two)]
    load_two = [load(up_in, matrix), load(middle_in, middle)]
    load_three = [load(out_in, out_matrix), load(branch_in, branch), load(tokens_in, tokens)]
    vectors[...] = jnp.zeros_like(vectors)
    at.greet(at.neighbours())

    reduction = Reduction(at, copies, blocks_of, outs)
    (
        grad_pool,
        grad_pool_out,
        across_pool,
        across_out,
        x_pool,
        x_out,
        y_pool,
        y_out,
        z_pool,
        z_out,
        t_pool,
        t_out,
    ) = pools
    quarter = PART // 8

    def pooled(n, grad_place, index, line, first):
        reduction.add(
            index,
            line,
            first,
            grad_pool.at[grad_place],
            across_pool.at[n],
            x_pool.at[n],
            y_pool.at[n],
            z_pool.at[n],
            t_pool.at[n],
        )

    down_parts, up_parts, in_parts = width // PART, hidden_width // PART, 3 * part_width // PART
    for part in range(down_parts):
        for line in range(2):
            n = 2 * part + line
            pooled(n, n, 3, line * quarter, part * PART)
    for part in range(up_parts):
        n = 2 * down_parts + part
        pooled(n, n, 2, 0, part * PART)
    reduction.add(1, 0, 0, grad_pool_out, across_out, x_out, y_out, z_out, t_out)
    first_in = len(reduction.chunks)
    for part in range(in_parts):
        pooled(first_in - 1 + part, part, 0, 0, part * PART)

    def own_place(row_side, step):
        return pl.ds(pl.multiple_of(step * micro_rows + row_side * own_micro, own_micro), own_micro)

    def dot_down(part):
        block = activated_in.shape[1] // chips

        def body(chip):
            left = activated[:, pl.ds(pl.multiple_of(chip * block, block), block)]
            result = rows_dot(left, low[:, part * PART : (part + 1) * PART]).astype(LOW)
            result = result.reshape(4, 2, quarter, PART)
            grad_pool[2 * part, chip] = result[:, 0]
            grad_pool[2 * part + 1, chip] = result[:, 1]

        loop(chips, body)

    def dot_pair(place, left, right, part):
        block = width // chips

        def body(chip):
            columns = left[:, pl.ds(pl.multiple_of(chip * block, block), block)]
            result = rows_dot(columns, right[:, part * PART : (part + 1) * PART]).astype(LOW)
            grad_pool[place, chip] = result.reshape(4, quarter, PART)

        loop(chips, body)

    def dot_up(part):
        dot_pair(2 * down_parts + part, normed_two, hidden_low, part)

    def dot_in(part):
        for key in ("ax", "ay", "bx", "by"):
            copies.sent((key, part))
        dot_pair(part, normed, mixed_grad, part)

    def dot_out():
        block = part_width // chips

        def body(chip):
            left = branch[:, pl.ds(pl.multiple_of(chip * block, block), block)]
            grad_pool_out[chip] = rows_dot(left, low[...]).astype(LOW).reshape(4, block // 4, width)

        loop(chips, body)

    def back_product(left, left_rows, right, target, target_rows, adding):
        tile = 256

        def body(step):
            columns = pl.ds(pl.multiple_of(step * tile, tile), tile)
            result = back_dot(left[left_rows, :], right[columns, :])
            if adding:
                result = result + target[target_rows, columns]
            target[target_rows, columns] = result.astype(target.dtype)

        loop(right.shape[0] // tile, body)

    def give_partial(name, left, right):
        for step in range(micro):
            place = pl.ds(step * own_micro, own_micro)
            back_product(left, own_place(1 - core, step), right, give, place, False)
        copies.start(name, give, came, at.other(core=1))

    def own_partial(name, left, right):
        copies.arrived(name, came)
        for step in range(micro):
            place = pl.ds(step * own_micro, own_micro)
            back_product(left, own_place(core, step), right, came, place, True)

    def column_sum(row, values):
        vectors[0, row : row + 1, :] += jnp.sum(values, axis=0, keepdims=True)

    lines = 32

    def second_norm_back():
        gain = gains[1:2, :]

        def body(step):
            place = pl.ds(pl.multiple_of(step * lines, lines), lines)
            chip_row = step // (own_micro // lines) * micro_rows + core * own_micro
            chip_row = chip_row + lax.rem(step, own_micro // lines) * lines
            chip_place = pl.ds(pl.multiple_of(chip_row, lines), lines)
            unit, inverse = normalize(middle[place, :])
            upper = came[place, :]
            upstream = low[chip_place, :].astype(F32)
            total = upstream + normalize_back(upper, gain, unit, inverse)
            middle[place, :] = total
            rounded = total.astype(LOW)
            low[chip_place, :] = rounded
            column_sum(2, rounded.astype(F32))
            column_sum(3, upper * unit)
            column_sum(4, upper)
            column_sum(5, upstream)

        loop(own_rows // lines, body)
        for step in range(micro):
            place = low.at[own_place(core, step)]
            copies.start(("low", step), place, place, at.other(core=1))

    def first_norm_back():
        gain = gains[0:1, :]

        def body(step):
            place = pl.ds(pl.multiple_of(step * lines, lines), lines)
            unit, inverse = normalize(tokens[place, :].astype(F32))
            upper = came[place, :]
            total = middle[place, :] + normalize_back(upper, gain, unit, inverse)
            input_grad_out[place, :] = total.astype(LOW)
            column_sum(0, upper * unit)
            column_sum(1, upper)

        loop(own_rows // lines, body)

    def hidden_sums():
        def body(step):
            place = pl.ds(pl.multiple_of(step * lines, lines), lines)
            for side in range(hidden_width // width):
                column_sum(
                    9 + side, hidden_low[place, side * width : (side + 1) * width].astype(F32)
                )

        loop(rows // lines, body)

    def mixed_sums():
        def body(step):
            place = pl.ds(pl.multiple_of(step * lines, lines), lines)
            joined = jnp.concatenate(
                [
                    mixed_grad[place, 0:part_width].astype(F32),
                    mixed_grad[place, 2 * part_width : 3 * part_width].astype(F32),
                ],
                axis=1,
            )
            column_sum(8, joined)

        loop(all_rows // lines, body)

    left = lax.broadcasted_iota(jnp.int32, (BLOCK, BLOCK), 1) < HD
    left_tall = lax.broadcasted_iota(jnp.int32, (2 * BLOCK, BLOCK), 1) < HD
    scale = float(HD) ** (-0.5)

    def attention_group(column):
        key_sums[...] = jnp.zeros_like(key_sums)

        def body(step):
            row, previous = block_rows(step, blocks, body_rows)
            allowed = allowed_keys(starts, row)
            queries = mixed[pl.ds(row, BLOCK), column : column + BLOCK]
            keys = window(mixed, row, previous, part_width + column)
            values = window(mixed, row, previous, 2 * part_width + column)
            upper = attended[pl.ds(row, BLOCK), column : column + BLOCK]
            parts = []
            for side in (left, ~left):
                soft = soft_weights(jnp.where(side, queries, 0), keys, allowed)
                soft_grad = back_dot(jnp.where(side, upper, 0), values)
                total = jnp.sum(soft * soft_grad, axis=1, keepdims=True)
                score_low = (soft * (soft_grad - total)).astype(LOW)
                parts.append(
                    (
                        dot(score_low, keys) * scale,
                        rows_dot(score_low, queries) * scale,
                        rows_dot(soft.astype(LOW), upper),
                    )
                )
            mixed_grad[pl.ds(row, BLOCK), column : column + BLOCK] = jnp.where(
                left, parts[0][0], parts[1][0]
            ).astype(LOW)
            for slot in (1, 2):
                joined = jnp.where(left_tall, parts[0][slot], parts[1][slot])
                place = (slot - 1) * BLOCK
                key_sums[pl.ds(previous, BLOCK), place : place + BLOCK] += joined[:BLOCK]
                key_sums[pl.ds(row, BLOCK), place : place + BLOCK] += joined[BLOCK:]

        loop(body_rows // BLOCK, body)
        for slot in (1, 2):
            place = (slot - 1) * BLOCK
            mixed_grad[:, slot * part_width + column : slot * part_width + column + BLOCK] = (
                key_sums[:, place : place + BLOCK].astype(LOW)
            )
        mixed_grad[body_rows:, column : column + BLOCK] = jnp.zeros(
            (all_rows - body_rows, BLOCK), LOW
        )

    lower_chip = at.other(chip=jnp.maximum(at.chip - 1, 0))

    def send_halo():
        copies.start(
            ("halo",),
            mixed_grad.at[pl.ds(body_rows, all_rows - body_rows), pl.ds(part_width, 2 * part_width)],
            halo,
            lower_chip,
            at.chip > 0,
        )

    def add_halo():
        copies.arrived(("halo",), halo, at.chip < chips - 1)

        def body():
            for step in range(micro):
                place = pl.ds((step + 1) * micro_rows - BLOCK, BLOCK)
                mixed_grad[place, part_width : 3 * part_width] = (
                    mixed_grad[place, part_width : 3 * part_width].astype(F32)
                    + halo[step * BLOCK : (step + 1) * BLOCK, :].astype(F32)
                ).astype(LOW)

        pl.when(at.chip < chips - 1)(body)

    time = iter(range(100))

    def tick():
        reduction.tick(next(time))

    def wait_for(members):
        for member in members:
            member.wait()

    wait_for(load_first)
    dot_down(0)
    tick()
    for part in range(1, down_parts):
        dot_down(part)
    tick()
    load_mixed = [load(mixed_in, mixed)]
    wait_for(load_up)
    wait_for(load_two)
    for part in range(up_parts // 2):
        dot_up(part)
    give_partial(("partial", 0), hidden_low, matrix)
    tick()
    for part in range(up_parts // 2, up_parts):
        dot_up(part)
    own_partial(("partial", 0), hidden_low, matrix)
    load_last = [load(in_in, in_matrix), load(all_normed_in, normed)]
    second_norm_back()
    hidden_sums()
    tick()
    wait_for(load_three)
    for step in range(micro):
        back_product(
            low, own_place(core, step), out_matrix, attended, own_place(core, step), False
        )
    for step in range(micro):
        copies.arrived(("low", step), low.at[own_place(1 - core, step)])
        back_product(
            low, own_place(1 - core, step), out_matrix, attended, own_place(1 - core, step), False
        )
    dot_out()
    tick()
    wait_for(load_mixed)
    for column in range(0, part_width, BLOCK):
        attention_group(column)
        tick()
    send_halo()
    wait_for(load_last)
    dot_in(0)
    tick()
    for part in range(1, in_parts):
        dot_in(part)
        if part == in_parts - 1:
            mixed_sums()
            copies.sent(("halo",))
            add_halo()
            copies.sent(("partial", 0))
            give_partial(("partial", 1), mixed_grad, in_matrix)
        tick()
    own_partial(("partial", 1), mixed_grad, in_matrix)
    tick()
    first_norm_back()
    copies.start(("sum", "core"), vectors.at[0, pl.ds(0, 8)], vectors_came.at[0, pl.ds(0, 8)], at.other(core=1))
    tick()
    copies.arrived(("sum", "core"), vectors_came.at[0, pl.ds(0, 8)])
    vectors[1, 0:8, :] = vectors[0, 0:8, :] + vectors_came[0, 0:8, :]
    vectors[1, 8:16, :] = vectors[0, 8:16, :]
    copies.start(("sum", "x"), vectors.at[1], vectors_came.at[1], at.other(x=1))
    tick()
    copies.arrived(("sum", "x"), vectors_came.at[1])
    vectors[2] = vectors[1] + vectors_came[1]
    copies.start(("sum", "y"), vectors.at[2], vectors_came.at[2], at.other(y=1))
    tick()
    copies.arrived(("sum", "y"), vectors_came.at[2])
    vectors[3] = vectors[2] + vectors_came[2]
    for step in range(1, chips):
        copies.start(
            ("sum", "z", step),
            vectors.at[3],
            vectors_came.at[2 + step],
            at.other(chip=lax.rem(at.chip + step, chips)),
        )
    tick()
    total = vectors[3]
    for step in range(1, chips):
        copies.arrived(("sum", "z", step), vectors_came.at[2 + step])
        total = total + vectors_came[2 + step]
    vectors_out[...] = total
    for _ in range(OFFSETS[-1]):
        tick()
    copies.finish()


def backward(chips, micro, blocks, blocks_of, members, starts, gains):
    activated, down_low, hidden_low, normed_two, up, out_matrix, in_matrix, branch, mixed = members[:9]
    rows, width = down_low.shape
    all_rows, hidden_width, part_width = mixed.shape[0], hidden_low.shape[1], branch.shape[1]
    own_rows = rows // 2
    quarter = PART // 8
    down_parts, up_parts, in_parts = width // PART, hidden_width // PART, 3 * part_width // PART
    pooled = 2 * down_parts + up_parts + in_parts
    any_space = pl.BlockSpec(memory_space=pl.ANY)
    vmem = pl.BlockSpec(memory_space=pltpu.VMEM)

    def low(*shape):
        return pltpu.VMEM(shape, LOW)

    def full(*shape):
        return pltpu.VMEM(shape, F32)

    out_quarter = part_width // (4 * chips)
    scratch = [
        low(all_rows, hidden_width),
        low(all_rows, hidden_width),
        low(width, hidden_width),
        low(part_width, width),
        low(rows, width),
        low(all_rows, width),
        low(rows, part_width),
        low(rows, part_width),
        full(own_rows, width),
        full(own_rows, width),
        full(own_rows, width),
        low(own_rows, width),
        full(all_rows, 2 * BLOCK),
        low(all_rows - rows, 2 * part_width),
        full(4, VECTOR_ROWS, width),
        full(chips + 2, VECTOR_ROWS, width),
        low(2 * down_parts + up_parts, chips, 4, quarter, PART),
        low(chips, 4, out_quarter, width),
        low(pooled, 2, chips, quarter // 2, PART),
        low(2, chips, out_quarter // 2, width),
        low(pooled, chips, quarter, PART),
        low(chips, out_quarter, width),
        low(pooled, chips, quarter, PART),
        low(chips, out_quarter, width),
        low(pooled, chips - 1, quarter, PART),
        low(chips - 1, out_quarter, width),
        low(pooled, 4, quarter, PART),
        low(4, out_quarter, width),
        pltpu.SemaphoreType.DMA((240,)),
        pltpu.SemaphoreType.DMA((240,)),
        pltpu.SemaphoreType.DMA((16,)),
    ]
    out_shapes = [
        jax.ShapeDtypeStruct((2, width // (4 * chips), 6 * part_width), LOW),
        jax.ShapeDtypeStruct((4, out_quarter, width), LOW),
        jax.ShapeDtypeStruct((2, width // (4 * chips), 2 * hidden_width), LOW),
        jax.ShapeDtypeStruct((4, hidden_width // (4 * chips), width), LOW),
        jax.ShapeDtypeStruct((VECTOR_ROWS, width), F32),
        jax.ShapeDtypeStruct((own_rows, width), LOW),
    ]
    results = pl.pallas_call(
        partial(backward_kernel, chips, micro, blocks, blocks_of),
        out_shape=tuple(out_shapes),
        in_specs=[any_space] * 12 + [vmem] * 2,
        out_specs=tuple([vmem] * 6),
        scratch_shapes=scratch,
        compiler_params=pltpu.CompilerParams(
            collective_id=1, has_side_effects=True, vmem_limit_bytes=67_000_000
        ),
    )(*members, starts, gains)
    flat = [member.reshape(-1, member.shape[2]).astype(F32) for member in results[:4]]
    return flat, results[4], results[5]


def shards(
    chips,
    reps,
    tokens,
    cotangent,
    seq_lengths,
    dealing,
    attention_gain,
    attention_shift,
    input_weight,
    query_bias,
    value_bias,
    output_weight,
    output_bias,
    feed_gain,
    feed_shift,
    up_weight,
    up_bias,
    down_weight,
    down_bias,
):
    links = Links(chips, reps)
    core, chip = links.core, links.chip
    micro, tok_rows, width = tokens.shape
    shard_count = 2 * chips
    own_rows = micro * tok_rows
    blocks = 2 * tok_rows // BLOCK

    def own_of(values):
        return pick(values.reshape(micro, 2, tok_rows, -1), core, 1).reshape(own_rows, -1)

    def other_of(values):
        return pick(values.reshape(micro, 2, tok_rows, -1), 1 - core, 1).reshape(own_rows, -1)

    def pair_rows(own):
        came = links.swap(own, core=1)
        shape = (micro, 1, tok_rows, own.shape[-1])
        return links.by_core(own.reshape(shape), came.reshape(shape), 1).reshape(2 * own_rows, -1)

    def pair_sum(partial_values):
        return own_of(partial_values) + links.swap(other_of(partial_values), core=1)

    vectors = (
        attention_gain,
        attention_shift,
        query_bias,
        value_bias,
        output_bias,
        feed_gain,
        feed_shift,
        down_bias,
        up_bias,
    )
    lengths = [member.shape[0] for member in vectors]
    packed_length = sum(lengths)
    fast = reps == 4
    lines = -(-packed_length // (16 * BLOCK)) * 16

    def pad_lines(values):
        values = jnp.pad(values, ((0, 0), (0, lines * BLOCK - packed_length)))
        return values.reshape(-1, lines, BLOCK)

    packed_in = jnp.concatenate(vectors)
    if fast:
        table, input_part, output_part, up_part, down_part = gather_weights(
            pad_lines(packed_in[None])[0],
            (input_weight, output_weight, up_weight, down_weight),
            (3 * chips, None, chips, None),
            chips,
        )
        table = table.reshape(shard_count, -1)[:, :packed_length].astype(F32)
    else:
        table = links.gather_vectors(packed_in).astype(F32)
        input_part = links.gather(links.halves(input_weight, 3))
        output_part = links.gather(output_weight)
        up_part = links.gather(links.halves(up_weight, 1))
        down_part = links.gather(down_weight)
    wholes, at = [], 0
    for length in lengths:
        wholes.append(table[:, at : at + length])
        at += length

    def whole(index):
        return wholes[index].reshape(1, -1)

    def core_part(index):
        return pick(wholes[index].reshape(chips, 2, -1), core, 1).reshape(1, -1)

    inputs = tokens.reshape(own_rows, width).astype(F32)
    unit_one, inverse_one = normalize(inputs)
    normed = (unit_one * whole(0) + whole(1)).astype(LOW)
    chip_normed = pair_rows(normed)
    tail = chip_normed.reshape(micro, 2 * tok_rows, width)[:, 2 * tok_rows - BLOCK :]
    halo = links.shift(tail.reshape(micro * BLOCK, width), 1)
    all_normed = jnp.concatenate([chip_normed, halo], axis=0)
    down_low = pair_rows(cotangent.reshape(own_rows, width))
    first = chip * 2 * tok_rows
    starts = jnp.stack(
        [
            sequence_starts(seq_lengths[m, 0], dealing[m, 0], first, 2 * tok_rows)
            for m in range(micro)
        ]
    )
    block_first = first + jnp.arange(2 * tok_rows, dtype=jnp.int32) // BLOCK * BLOCK - BLOCK
    starts = (starts - block_first[None, :]).reshape(2 * own_rows, 1)

    half = width // 2
    bias = jnp.concatenate([core_part(2), jnp.zeros((1, half), F32), core_part(3)], axis=1)
    mixed = (dot(all_normed, input_part) + bias).astype(LOW)
    branch = attention(mixed, starts, blocks)
    middle = inputs + pair_sum(dot(branch, output_part)) + whole(4)
    unit_two, inverse_two = normalize(middle)
    normed_two = pair_rows((unit_two * whole(5) + whole(6)).astype(LOW))
    hidden = dot(normed_two, up_part) + core_part(8)
    activated, gelu_back = jax.vjp(gelu_tanh, hidden)
    activated = activated.astype(LOW)
    result = middle + pair_sum(dot(activated, down_part)) + whole(7)

    upstream = cotangent.reshape(own_rows, width).astype(F32)
    (hidden_grad,) = gelu_back(back_dot(down_low, down_part))
    hidden_low = hidden_grad.astype(LOW)
    if fast:
        grads, sums, input_grad = backward(
            chips,
            micro,
            blocks,
            (width // shard_count, None, up_part.shape[1] // chips, None),
            (
                activated,
                down_low,
                hidden_low,
                normed_two,
                up_part,
                output_part,
                input_part,
                branch,
                mixed,
                all_normed,
                middle,
                tokens.reshape(own_rows, width),
            ),
            starts,
            jnp.concatenate([whole(0), whole(5)], axis=0),
        )
        input_weight_grad, output_grad, up_grad, down_grad = grads
        shared = pick(sums[:8].reshape(8, shard_count, -1), chip * 2 + core, 1)
        sides = pick(sums[8].reshape(2, chips, -1), chip, 1)
        vector_grads = [
            shared[0],
            shared[1],
            sides[0],
            sides[1],
            shared[2],
            shared[3],
            shared[4],
            shared[5],
            pick(sums[9:].reshape(-1)[: up_part.shape[1]].reshape(chips, -1), chip),
        ]
    else:
        down_partial = rows_dot(activated, down_low).astype(LOW)
        up_partial = rows_dot(normed_two, hidden_low).astype(LOW)
        upper_two = pair_sum(back_dot(hidden_low, up_part))
        middle_grad = upstream + normalize_back(upper_two, whole(5), unit_two, inverse_two)
        output_own = middle_grad.astype(LOW)
        output_low = pair_rows(output_own)
        output_partial = rows_dot(branch, output_low).astype(LOW)
        attended = back_dot(output_low, output_part).astype(LOW)
        mixed_grad = attention_back(mixed, starts, attended, blocks)
        input_partial = rows_dot(all_normed, mixed_grad).astype(LOW)
        back_halo = links.shift(mixed_grad[2 * own_rows :, half:], -1)
        body = mixed_grad[: 2 * own_rows].reshape(micro, 2 * tok_rows, 3 * half)
        tail_grad = body[:, 2 * tok_rows - BLOCK :, half:].astype(F32) + back_halo.reshape(
            micro, BLOCK, width
        ).astype(F32)
        body = body.at[:, 2 * tok_rows - BLOCK :, half:].set(tail_grad.astype(LOW))
        upper_one = pair_sum(back_dot(body.reshape(2 * own_rows, 3 * half), input_part))
        input_grad = middle_grad + normalize_back(upper_one, whole(0), unit_one, inverse_one)

        def by_shard(values):
            return values.reshape(shard_count, -1)

        def by_core_shard(values):
            spread = values.reshape(chips, 1, -1)
            mask = jnp.arange(2, dtype=jnp.int32)[None, :, None] == core
            return jnp.where(mask, spread, 0.0).reshape(shard_count, -1)

        def column_sum(values):
            return jnp.sum(values.astype(F32), axis=0)

        packed = jnp.concatenate(
            [
                by_shard(column_sum(upper_one * unit_one)),
                by_shard(column_sum(upper_one)),
                by_core_shard(column_sum(mixed_grad[:, :half])),
                by_core_shard(column_sum(mixed_grad[:, width:])),
                by_shard(column_sum(output_own)),
                by_shard(column_sum(upper_two * unit_two)),
                by_shard(column_sum(upper_two)),
                by_shard(column_sum(upstream)),
                by_core_shard(column_sum(hidden_low)),
            ],
            axis=1,
        )
        sums = links.reduce_vectors(packed)
        input_weight_grad = links.unhalves(links.reduce(input_partial), 3).astype(F32)
        output_grad = links.reduce(output_partial).astype(F32)
        up_grad = links.unhalves(links.reduce(up_partial), 1).astype(F32)
        down_grad = links.reduce(down_partial).astype(F32)
        vector_grads, at = [], 0
        for length in lengths:
            vector_grads.append(sums[at : at + length])
            at += length
    return (
        result.astype(LOW).reshape(tokens.shape),
        input_grad.astype(LOW).reshape(tokens.shape),
        vector_grads[0],
        vector_grads[1],
        input_weight_grad,
        vector_grads[2],
        vector_grads[3],
        output_grad,
        vector_grads[4],
        vector_grads[5],
        vector_grads[6],
        up_grad,
        vector_grads[8],
        down_grad,
        vector_grads[7],
    )


def solution(mesh):
    rows_spec = P(None, ("shard", "rep"), None)
    vector, matrix = P("shard"), P("shard", None)
    weight_specs = (
        vector,
        vector,
        matrix,
        vector,
        vector,
        matrix,
        vector,
        vector,
        vector,
        matrix,
        vector,
        matrix,
        vector,
    )
    return jax.shard_map(
        partial(shards, mesh.shape["shard"] // 2, mesh.shape["rep"]),
        mesh=mesh,
        in_specs=(rows_spec, rows_spec, P(None, "rep", None, None), P(None, "rep", None))
        + weight_specs,
        out_specs=(rows_spec, rows_spec) + weight_specs,
        check_vma=False,
    )
```

```python
from functools import partial

import jax
import jax.numpy as jnp
from jax import lax
from jax.experimental import pallas as pl
from jax.experimental.pallas import tpu as pltpu
from jax.sharding import PartitionSpec as P

HD = 64
BLOCK = 128
EPSILON = 1e-05
MASKED = -1e30
AXES = ("shard", "rep")
F32 = jnp.float32
LOW = jnp.bfloat16


def dot(left, right):
    return jnp.dot(left, right, preferred_element_type=F32)


def rows_dot(left, right):
    return lax.dot_general(left, right, (((0,), (0,)), ((), ())), preferred_element_type=F32)


def back_dot(left, right):
    return lax.dot_general(left, right, (((1,), (1,)), ((), ())), preferred_element_type=F32)


def pick(stacked, index, axis=0):
    return lax.dynamic_index_in_dim(stacked, index, axis, keepdims=False)


def normalize(values):
    center = values - jnp.mean(values, axis=-1, keepdims=True)
    inverse = lax.rsqrt(jnp.mean(center * center, axis=-1, keepdims=True) + EPSILON)
    return center * inverse, inverse


def normalize_back(upper, gain, unit, inverse):
    scaled = upper * gain
    mean_scaled = jnp.mean(scaled, axis=-1, keepdims=True)
    mean_product = jnp.mean(scaled * unit, axis=-1, keepdims=True)
    return inverse * (scaled - mean_scaled - unit * mean_product)


def gelu_tanh(values):
    return jax.nn.gelu(values, approximate=True)


def sequence_starts(seq_lengths, dealing, first, rows):
    total = dealing.shape[0]
    numbers = jnp.arange(total, dtype=jnp.int32)
    matched = (dealing[:, None] == numbers[None, :]).astype(jnp.int32)
    packed_length = jnp.sum(matched * seq_lengths.reshape(total)[None, :], axis=1)
    before = (numbers[None, :] < numbers[:, None]).astype(jnp.int32)
    packed_start = jnp.sum(before * packed_length[None, :], axis=1)
    own = first + jnp.arange(rows, dtype=jnp.int32)
    return jnp.max(
        jnp.where(packed_start[None, :] <= own[:, None], packed_start[None, :], 0), axis=1
    )


def window(ref, row, previous, column):
    return jnp.concatenate(
        [
            ref[pl.ds(previous, BLOCK), column : column + BLOCK],
            ref[pl.ds(row, BLOCK), column : column + BLOCK],
        ],
        axis=0,
    )


def block_rows(step, blocks, body_rows):
    micro, block = step // blocks, step % blocks
    row = pl.multiple_of(step * BLOCK, BLOCK)
    previous = jnp.where(block == 0, body_rows + micro * BLOCK, row - BLOCK)
    return row, pl.multiple_of(previous, BLOCK)


def soft_weights(query_half, keys, allowed):
    scores = back_dot(query_half, keys) * float(HD) ** (-0.5)
    scores = jnp.where(allowed, scores, MASKED)
    top = jnp.max(scores, axis=1, keepdims=True)
    powers = jnp.exp(scores - top)
    return powers / jnp.sum(powers, axis=1, keepdims=True)


def allowed_keys(start_ref, row):
    places = lax.broadcasted_iota(jnp.int32, (BLOCK, 2 * BLOCK), 1)
    lines = lax.broadcasted_iota(jnp.int32, (BLOCK, 2 * BLOCK), 0)
    return (places >= start_ref[pl.ds(row, BLOCK), :]) & (places <= lines + BLOCK)


def attention_kernel(blocks, width, mixed_ref, start_ref, branch_ref):
    body_rows = branch_ref.shape[0]
    left = lax.broadcasted_iota(jnp.int32, (BLOCK, BLOCK), 1) < HD

    def step_body(step, _):
        row, previous = block_rows(step, blocks, body_rows)
        allowed = allowed_keys(start_ref, row)
        for column in range(0, width, BLOCK):
            queries = mixed_ref[pl.ds(row, BLOCK), column : column + BLOCK]
            keys = window(mixed_ref, row, previous, width + column)
            values = window(mixed_ref, row, previous, 2 * width + column)
            parts = []
            for half in (left, ~left):
                soft = soft_weights(jnp.where(half, queries, 0), keys, allowed)
                parts.append(dot(soft.astype(LOW), values))
            branch_ref[pl.ds(row, BLOCK), column : column + BLOCK] = jnp.where(
                left, parts[0], parts[1]
            ).astype(LOW)
        return 0

    lax.fori_loop(0, body_rows // BLOCK, step_body, 0)


def attention_back_kernel(blocks, width, mixed_ref, start_ref, upper_ref, grad_ref, sums_ref):
    body_rows = upper_ref.shape[0]
    left = lax.broadcasted_iota(jnp.int32, (BLOCK, BLOCK), 1) < HD
    left_tall = lax.broadcasted_iota(jnp.int32, (2 * BLOCK, BLOCK), 1) < HD
    scale = float(HD) ** (-0.5)
    sums_ref[...] = jnp.zeros_like(sums_ref)

    def step_body(step, _):
        row, previous = block_rows(step, blocks, body_rows)
        allowed = allowed_keys(start_ref, row)
        for column in range(0, width, BLOCK):
            queries = mixed_ref[pl.ds(row, BLOCK), column : column + BLOCK]
            keys = window(mixed_ref, row, previous, width + column)
            values = window(mixed_ref, row, previous, 2 * width + column)
            upper = upper_ref[pl.ds(row, BLOCK), column : column + BLOCK]
            parts = []
            for half in (left, ~left):
                soft = soft_weights(jnp.where(half, queries, 0), keys, allowed)
                soft_grad = back_dot(jnp.where(half, upper, 0), values)
                total = jnp.sum(soft * soft_grad, axis=1, keepdims=True)
                score_low = (soft * (soft_grad - total)).astype(LOW)
                parts.append(
                    (
                        dot(score_low, keys) * scale,
                        rows_dot(score_low, queries) * scale,
                        rows_dot(soft.astype(LOW), upper),
                    )
                )
            grad_ref[pl.ds(row, BLOCK), column : column + BLOCK] = jnp.where(
                left, parts[0][0], parts[1][0]
            ).astype(LOW)
            for slot in (1, 2):
                joined = jnp.where(left_tall, parts[0][slot], parts[1][slot])
                place = (slot - 1) * width + column
                sums_ref[pl.ds(previous, BLOCK), place : place + BLOCK] += joined[:BLOCK]
                sums_ref[pl.ds(row, BLOCK), place : place + BLOCK] += joined[BLOCK:]
        return 0

    lax.fori_loop(0, body_rows // BLOCK, step_body, 0)
    grad_ref[:, width:] = sums_ref[...].astype(LOW)
    grad_ref[body_rows:, :width] = jnp.zeros((grad_ref.shape[0] - body_rows, width), LOW)


def attention(mixed, starts, blocks):
    width = mixed.shape[1] // 3
    rows = starts.shape[0]
    vmem = pl.BlockSpec(memory_space=pltpu.VMEM)
    return pl.pallas_call(
        partial(attention_kernel, blocks, width),
        out_shape=jax.ShapeDtypeStruct((rows, width), LOW),
        in_specs=[vmem, vmem],
        out_specs=vmem,
        cost_estimate=pl.CostEstimate(
            flops=rows * width * BLOCK * 16, bytes_accessed=8 << 20, transcendentals=0
        ),
        compiler_params=pltpu.CompilerParams(vmem_limit_bytes=40 << 20),
    )(mixed, starts)


def attention_back(mixed, starts, upper, blocks):
    width = mixed.shape[1] // 3
    rows = starts.shape[0]
    vmem = pl.BlockSpec(memory_space=pltpu.VMEM)
    return pl.pallas_call(
        partial(attention_back_kernel, blocks, width),
        out_shape=jax.ShapeDtypeStruct(mixed.shape, LOW),
        in_specs=[vmem, vmem, vmem],
        out_specs=vmem,
        scratch_shapes=[pltpu.VMEM((mixed.shape[0], 2 * width), F32)],
        cost_estimate=pl.CostEstimate(
            flops=rows * width * BLOCK * 40, bytes_accessed=16 << 20, transcendentals=0
        ),
        compiler_params=pltpu.CompilerParams(vmem_limit_bytes=40 << 20),
    )(mixed, starts, upper)


class Links:
    def __init__(self, chips, reps):
        self.chips, self.reps = chips, reps
        shard = lax.axis_index("shard")
        self.chip, self.core, self.rep = shard // 2, shard % 2, lax.axis_index("rep")

    def flat(self, chip, core, rep):
        return (chip * 2 + core) * self.reps + rep

    def swap(self, values, chip=0, core=0, rep=0):
        pairs = [
            (self.flat(a, b, d), self.flat(a ^ chip, b ^ core, d ^ rep))
            for a in range(self.chips)
            for b in range(2)
            for d in range(self.reps)
        ]
        return lax.ppermute(values, AXES, pairs)

    def shift(self, values, by):
        pairs = [
            (self.flat(a, b, d), self.flat(a + by, b, d))
            for a in range(self.chips)
            if 0 <= a + by < self.chips
            for b in range(2)
            for d in range(self.reps)
        ]
        return lax.ppermute(values, AXES, pairs)

    def by_core(self, own, other, axis):
        first = jnp.where(self.core == 0, own, other)
        second = jnp.where(self.core == 0, other, own)
        return jnp.concatenate([first, second], axis=axis)

    def halves(self, matrix, parts):
        rows, columns = matrix.shape
        blocks = self.chips * parts
        view = matrix.reshape(rows, blocks, 2, columns // (2 * blocks))
        keep = pick(view, self.core, 2).reshape(rows, columns // 2)
        give = pick(view, 1 - self.core, 2).reshape(rows, columns // 2)
        return self.by_core(keep, self.swap(give, core=1), 0)

    def gather(self, chip_rows):
        rows, columns = chip_rows.shape
        quarter = rows // self.reps
        quarters = chip_rows.reshape(self.reps, quarter, columns)
        piece = pick(quarters, self.rep)
        pieces = jnp.stack([self.swap(piece, chip=j) for j in range(1, self.chips)])
        found = [pieces] + [None] * (self.reps - 1)
        if self.reps == 4:
            half = quarter // 2
            found[1] = self.swap(pieces, rep=1)
            found[2] = self.swap(pieces, rep=2)
            upper = self.swap(found[1][:, :half], rep=2)
            lower = self.swap(found[2][:, half:], rep=1)
            found[3] = jnp.concatenate([upper, lower], axis=1)
        else:
            for j in range(1, self.reps):
                found[j] = self.swap(pieces, rep=j)
        stacked = jnp.stack(
            [
                jnp.concatenate([pick(quarters, self.rep ^ j)[None], found[j]], axis=0)
                for j in range(self.reps)
            ]
        )
        ordered = []
        for chip in range(self.chips):
            for rep in range(self.reps):
                at = (self.rep ^ rep, self.chip ^ chip, 0, 0)
                ordered.append(
                    lax.dynamic_slice(stacked, at, (1, 1, quarter, columns)).reshape(
                        quarter, columns
                    )
                )
        return jnp.concatenate(ordered, axis=0)

    def reduce(self, grads):
        chips, reps = self.chips, self.reps
        rows, columns = grads.shape
        quarter = rows // (chips * reps)
        view = grads.astype(LOW).reshape(chips, reps, quarter, columns)
        mine = pick(view, self.rep, 1).astype(F32)
        if reps == 4:
            half = quarter // 2
            across = pick(view, self.rep ^ 3, 1)
            upper = self.swap(across[:, :half], rep=1)
            lower = self.swap(across[:, half:], rep=2)
            to_x = pick(view, self.rep ^ 1, 1)
            to_y = pick(view, self.rep ^ 2, 1)
            to_x = jnp.concatenate(
                [to_x[:, :half], (to_x[:, half:].astype(F32) + lower.astype(F32)).astype(LOW)],
                axis=1,
            )
            to_y = jnp.concatenate(
                [(to_y[:, :half].astype(F32) + upper.astype(F32)).astype(LOW), to_y[:, half:]],
                axis=1,
            )
            mine = (
                mine + self.swap(to_x, rep=1).astype(F32) + self.swap(to_y, rep=2).astype(F32)
            )
        else:
            for j in range(1, reps):
                mine = mine + self.swap(pick(view, self.rep ^ j, 1), rep=j).astype(F32)
        total = pick(mine, self.chip)
        sends = mine.astype(LOW)
        for j in range(1, chips):
            total = total + self.swap(pick(sends, self.chip ^ j), chip=j).astype(F32)
        return self.spread(total.astype(LOW))

    def spread(self, own):
        if self.reps == 4:
            half = own.shape[0] // 2
            from_x = self.swap(own, rep=1)
            from_y = self.swap(own, rep=2)
            upper = self.swap(from_x[:half], rep=2)
            lower = self.swap(from_y[half:], rep=1)
            found = [own, from_x, from_y, jnp.concatenate([upper, lower], axis=0)]
        else:
            found = [own] + [self.swap(own, rep=j) for j in range(1, self.reps)]
        stacked = jnp.stack(found)
        return jnp.concatenate([pick(stacked, self.rep ^ j) for j in range(self.reps)], axis=0)

    def unhalves(self, chip_rows, parts):
        rows, columns = chip_rows.shape
        view = chip_rows.reshape(2, rows // 2, columns)
        blocks = self.chips * parts
        keep = pick(view, self.core).reshape(rows // 2, blocks, 1, columns // blocks)
        came = self.swap(pick(view, 1 - self.core), core=1)
        came = came.reshape(rows // 2, blocks, 1, columns // blocks)
        return self.by_core(keep, came, 2).reshape(rows // 2, 2 * columns)

    def gather_vectors(self, packed):
        pair = self.by_core(packed[None], self.swap(packed, core=1)[None], 0)
        found = jnp.stack([pair] + [self.swap(pair, chip=j) for j in range(1, self.chips)])
        ordered = [pick(found, self.chip ^ j) for j in range(self.chips)]
        return jnp.concatenate(ordered, axis=0)

    def reduce_vectors(self, partial_sums):
        chips, reps = self.chips, self.reps
        view = partial_sums.reshape(chips, 2, -1)
        total = None
        for a in range(chips):
            for b in range(2):
                row = pick(pick(view, self.chip ^ a), self.core ^ b)
                row = row if a == b == 0 else self.swap(row, chip=a, core=b)
                total = row if total is None else total + row
        terms = [total] + [self.swap(total, rep=j) for j in range(1, reps)]
        while len(terms) > 1:
            terms = [terms[i] + terms[i + 1] for i in range(0, len(terms), 2)]
        return terms[0]

class Copies:
    def __init__(self, send, recv, links):
        self.send, self.recv, self.links = send, recv, links
        self.places, self.started = {}, []

    def make(self, name, source, target, device):
        place = self.places.setdefault(name, len(self.places))
        return pltpu.make_async_remote_copy(
            src_ref=source,
            dst_ref=target,
            send_sem=self.send.at[place],
            recv_sem=self.recv.at[place],
            device_id=device,
            device_id_type=pl.DeviceIdType.MESH,
        )

    def start(self, name, source, target, device, when=None):
        copy = self.make(name, source, target, device)
        run_when(when, copy.start)
        self.started.append((name, when, copy))

    def arrived(self, name, target, when=None):
        copy = self.make(name, target, target, self.links.other(x=1))
        run_when(when, copy.wait_recv)

    def sent(self, name):
        for item in [item for item in self.started if item[0] == name]:
            run_when(item[1], item[2].wait_send)
            self.started.remove(item)

    def finish(self):
        for _, when, copy in self.started:
            run_when(when, copy.wait_send)


def run_when(when, body):
    if when is None:
        body()
    else:
        pl.when(when)(body)


class Place:
    def __init__(self, chips):
        shard = lax.axis_index("shard")
        self.chips, self.shard = chips, shard
        self.chip, self.core, self.rep = shard // 2, lax.rem(shard, 2), lax.axis_index("rep")

    def flipped(self, bits):
        x, y = lax.rem(self.rep, 2), self.rep // 2
        x = 1 - x if bits & 1 else x
        y = 1 - y if bits & 2 else y
        return y * 2 + x

    def other(self, x=0, y=0, core=0, chip=None):
        chip = self.chip if chip is None else chip
        side = 1 - self.core if core else self.core
        return {"shard": chip * 2 + side, "rep": self.flipped(x + 2 * y)}

    def shard_at(self, step):
        return lax.rem(self.shard + step, 2 * self.chips)

    def greet(self, barrier_devices):
        barrier = pltpu.get_barrier_semaphore()
        for device in barrier_devices:
            pl.semaphore_signal(barrier, 1, device_id=device, device_id_type=pl.DeviceIdType.MESH)
        pl.semaphore_wait(barrier, len(barrier_devices))

    def neighbours(self):
        shards = [
            {"shard": self.shard_at(step), "rep": self.rep} for step in range(1, 2 * self.chips)
        ]
        return shards + [self.other(x=1), self.other(y=1)]


def forward_kernel(chips, micro, blocks, splits, *refs):
    vec_in, in_in, out_in, up_in, down_in, tokens_in, cotangent_in, starts = refs[:8]
    (
        in_out,
        out_out,
        up_out,
        down_out,
        mixed_out,
        branch_out,
        all_normed_out,
        normed_two_out,
        activated_out,
        hidden_out,
        middle_out,
        low_out,
        vectors,
    ) = refs[8:21]
    (
        in_whole,
        out_whole,
        up_whole,
        table,
        mixed_bias,
        up_bias,
        tokens,
        low,
        all_normed,
        mixed,
        branch,
        give,
        came,
        middle,
        normed_two,
        activated,
        hidden,
        send,
        recv,
        local,
    ) = refs[21:]
    shards_in = (in_in, out_in, up_in, down_in)
    wholes = (in_whole, out_whole, up_whole, down_out)
    at = Place(chips)
    core = at.core
    copies = Copies(send, recv, at)
    all_rows, width = all_normed.shape
    rows = low.shape[0]
    own_rows, micro_rows = rows // 2, rows // micro
    own_micro = micro_rows // 2
    part_width = branch.shape[1]
    moved, staged = [], []

    down_stage = activated.at[pl.ds(0, down_in.shape[0]), pl.ds(0, width)]

    def keep(source, target):
        copy = pltpu.make_async_copy(source, target, local.at[len(moved)])
        copy.start()
        moved.append(copy)
        return copy

    def own_place(row_side, step):
        return pl.ds(pl.multiple_of(step * micro_rows + row_side * own_micro, own_micro), own_micro)

    load_tokens = keep(tokens_in, tokens)
    at.greet(at.neighbours())
    partner = at.other(core=1)
    load_table = keep(vec_in, table.at[at.shard])
    for step in range(1, 2 * chips):
        copies.start(
            ("vec", step), vec_in, table.at[at.shard], {"shard": at.shard_at(step), "rep": at.rep}
        )
    kept = []
    for index, (source, whole, count) in enumerate(zip(shards_in, wholes, splits)):
        shard_rows = source.shape[0]
        first = len(moved)
        if index == 3:
            keep(source, down_stage)
        elif count is None:
            place = pl.ds(pl.multiple_of(at.chip * shard_rows, shard_rows), shard_rows)
            keep(source, whole.at[place])
        else:
            piece_width = source.shape[1] // (2 * count)
            place = pl.ds(pl.multiple_of(at.shard * shard_rows, shard_rows), shard_rows)
            for block in range(count):
                columns = pl.ds(block * piece_width, piece_width)

                def side(which):
                    start = pl.multiple_of((2 * block + which) * piece_width, piece_width)
                    return pl.ds(start, piece_width)

                copies.start(
                    ("pair", index, block),
                    source.at[:, side(1 - core)],
                    whole.at[place, columns],
                    partner,
                )
                keep(source.at[:, side(core)], whole.at[place, columns])
        kept.append(moved[first:])
    load_low = []
    for step in range(micro):
        source = cotangent_in.at[pl.ds(step * own_micro, own_micro)]
        load_low.append(keep(source, low.at[own_place(core, step)]))
        copies.start(("low", step), source, low.at[own_place(core, step)], partner)

    def piece(index, chip, bits=None, side=None):
        whole = wholes[index]
        chip_rows = whole.shape[0] // chips
        size = chip_rows // 4
        start = chip * chip_rows + (at.rep if bits is None else at.flipped(bits)) * size
        if side is not None:
            size = size // 2
            start = start + side * size
        return whole.at[pl.ds(pl.multiple_of(start, size), size)]

    ways = (("up", 1), ("down", -1))

    def neighbour(step):
        return at.other(chip=jnp.clip(at.chip + step, 0, chips - 1))

    def can_send(step):
        return at.chip < chips - 1 if step > 0 else at.chip > 0

    def origins(index, distance):
        for name, step in ways:
            when = at.chip >= distance if step > 0 else at.chip + distance < chips
            chip = jnp.clip(at.chip - step * distance, 0, chips - 1)
            yield (name, index, distance), step, when, chip

    def open_z(index):
        for copy in kept[index]:
            copy.wait()
        if splits[index] is not None:
            shard_rows = shards_in[index].shape[0]
            piece_width = shards_in[index].shape[1] // (2 * splits[index])
            place = (at.chip * 2 + 1 - core) * shard_rows
            place = pl.ds(pl.multiple_of(place, shard_rows), shard_rows)
            for block in range(splits[index]):
                columns = pl.ds(block * piece_width, piece_width)
                copies.arrived(("pair", index, block), wholes[index].at[place, columns])
        mine = target = piece(index, at.chip)
        if index == 3:
            place = pl.ds(pl.multiple_of(at.chip * down_in.shape[0], down_in.shape[0]), down_in.shape[0])
            staged.append(keep(down_stage, down_out.at[place]))
            quarter = down_in.shape[0] // 4
            mine = down_in.at[pl.ds(pl.multiple_of(at.rep * quarter, quarter), quarter)]
        for name, step in ways:
            copies.start((name, index, 1), mine, target, neighbour(step), can_send(step))

    def pass_on(index, distance):
        for key, step, when, chip in origins(index, distance):
            found = piece(index, chip)
            copies.arrived(key, found, when)
            if distance < chips - 1:
                copies.start(
                    (key[0], index, distance + 1),
                    found,
                    found,
                    neighbour(step),
                    when & can_send(step),
                )
            copies.start(("x",) + key, found, found, at.other(x=1), when)
            copies.start(("y",) + key, found, found, at.other(y=1), when)

    def across(index, distance):
        for key, step, when, chip in origins(index, distance):
            copies.arrived(("x",) + key, piece(index, chip, 1), when)
            upper = piece(index, chip, 1, 0)
            copies.start(("xy",) + key, upper, upper, at.other(y=1), when)
            copies.arrived(("y",) + key, piece(index, chip, 2), when)
            lower = piece(index, chip, 2, 1)
            copies.start(("yx",) + key, lower, lower, at.other(x=1), when)

    def close(index):
        for distance in range(1, chips):
            for key, step, when, chip in origins(index, distance):
                copies.arrived(("xy",) + key, piece(index, chip, 3, 0), when)
                copies.arrived(("yx",) + key, piece(index, chip, 3, 1), when)

    lines = 32

    def own_lines(step):
        place = pl.ds(pl.multiple_of(step * lines, lines), lines)
        chip_row = step // (own_micro // lines) * micro_rows + core * own_micro
        chip_row = chip_row + lax.rem(step, own_micro // lines) * lines
        return place, pl.ds(pl.multiple_of(chip_row, lines), lines)

    def spread_vectors():
        load_table.wait()
        for step in range(1, 2 * chips):
            copies.arrived(("vec", step), table.at[at.shard_at(2 * chips - step)])
        for shard in range(2 * chips):
            vectors[:, shard * BLOCK : (shard + 1) * BLOCK] = table[shard].astype(F32)
        mixed_bias[...] = jnp.zeros_like(mixed_bias)
        each = up_bias.shape[1] // (chips * BLOCK)
        for chip in range(chips):
            member = table[2 * chip + core].astype(F32)
            columns = pl.ds(chip * BLOCK, BLOCK)
            mixed_bias[:, columns] = member[2:3, :]
            mixed_bias[:, pl.ds(2 * part_width + chip * BLOCK, BLOCK)] = member[3:4, :]
            for j in range(each):
                up_bias[:, pl.ds((chip * each + j) * BLOCK, BLOCK)] = member[8 + j : 9 + j, :]

    def halo_place(step):
        return pl.ds(rows + step * BLOCK, BLOCK)

    def first_norm():
        def body(step):
            place, chip_place = own_lines(step)
            unit, _ = normalize(tokens[place, :].astype(F32))
            all_normed[chip_place, :] = (unit * vectors[0:1, :] + vectors[1:2, :]).astype(LOW)

        loop(own_rows // lines, body)
        for step in range(micro):
            mine = all_normed.at[own_place(core, step)]
            copies.start(("normed", step), mine, mine, partner)
            tail = all_normed.at[pl.ds((step + 1) * micro_rows - BLOCK, BLOCK)]
            copies.start(
                ("halo", step),
                tail,
                all_normed.at[halo_place(step)],
                neighbour(1),
                can_send(1) & (core == 1),
            )

        def clear():
            all_normed[rows:, :] = jnp.zeros((all_rows - rows, width), LOW)

        pl.when(at.chip == 0)(clear)

    def halo_on():
        for step in range(micro):
            found = all_normed.at[halo_place(step)]
            received = (at.chip > 0) & (core == 1)
            copies.arrived(("halo", step), found, received)
            copies.start(("halo on", step), found, found, partner, received)

    def all_normed_ready():
        for step in range(micro):
            copies.arrived(("normed", step), all_normed.at[own_place(1 - core, step)])
            copies.arrived(
                ("halo on", step), all_normed.at[halo_place(step)], (at.chip > 0) & (core == 0)
            )

    tile = 256

    def mix():
        def body(step):
            columns = pl.ds(pl.multiple_of(step * tile, tile), tile)
            result = dot(all_normed[...], in_whole[:, columns]) + mixed_bias[:, columns]
            mixed[:, columns] = result.astype(LOW)

        loop(3 * part_width // tile, body)

    left = lax.broadcasted_iota(jnp.int32, (BLOCK, BLOCK), 1) < HD

    def attend(column):
        def body(step):
            row, previous = block_rows(step, blocks, rows)
            allowed = allowed_keys(starts, row)
            queries = mixed[pl.ds(row, BLOCK), column : column + BLOCK]
            keys = window(mixed, row, previous, part_width + column)
            values = window(mixed, row, previous, 2 * part_width + column)
            parts = []
            for side in (left, ~left):
                soft = soft_weights(jnp.where(side, queries, 0), keys, allowed)
                parts.append(dot(soft.astype(LOW), values))
            branch[pl.ds(row, BLOCK), column : column + BLOCK] = jnp.where(
                left, parts[0], parts[1]
            ).astype(LOW)

        loop(rows // BLOCK, body)

    def project(side, target):
        for step in range(micro):
            place = pl.ds(step * own_micro, own_micro)
            left_rows = branch[own_place(side, step), :]

            def body(part):
                columns = pl.ds(pl.multiple_of(part * tile, tile), tile)
                target[place, columns] = dot(left_rows, out_whole[:, columns])

            loop(width // tile, body)

    def second_norm():
        copies.arrived(("partial",), came)

        def body(step):
            place, chip_place = own_lines(step)
            total = tokens[place, :].astype(F32) + (middle[place, :] + came[place, :])
            total = total + vectors[4:5, :]
            middle[place, :] = total
            unit, _ = normalize(total)
            normed_two[chip_place, :] = (unit * vectors[5:6, :] + vectors[6:7, :]).astype(LOW)

        loop(own_rows // lines, body)
        for step in range(micro):
            mine = normed_two.at[own_place(core, step)]
            copies.start(("normed two", step), mine, mine, partner)

    def feed(first, last):
        def body(step):
            columns = pl.ds(pl.multiple_of((first + step) * tile, tile), tile)
            result = dot(normed_two[...], up_whole[:, columns]) + up_bias[:, columns]
            hidden[:, columns] = result
            activated[:, columns] = gelu_tanh(result).astype(LOW)

        loop(last - first, body)

    open_z(0)
    load_tokens.wait()
    spread_vectors()
    first_norm()
    open_z(1)
    pass_on(0, 1)
    pass_on(0, 2)
    across(0, 1)
    open_z(2)
    pass_on(0, 3)
    halo_on()
    across(0, 2)
    for distance in range(1, chips):
        pass_on(1, distance)
    across(0, 3)
    for distance in range(1, chips):
        across(1, distance)
    all_normed_ready()
    pass_on(2, 1)
    open_z(3)
    close(0)
    pass_on(2, 2)
    keep(in_whole, in_out)
    keep(all_normed, all_normed_out)
    mix()
    keep(mixed, mixed_out)
    across(2, 1)
    attend(0)
    attend(BLOCK)
    pass_on(2, 3)
    across(2, 2)
    attend(2 * BLOCK)
    pass_on(3, 1)
    attend(3 * BLOCK)
    keep(branch, branch_out)
    across(2, 3)
    close(1)
    keep(out_whole, out_out)
    project(1 - core, give)
    copies.start(("partial",), give, came, partner)
    project(core, middle)
    pass_on(3, 2)
    across(3, 1)
    second_norm()
    keep(middle, middle_out)
    for copy in load_low:
        copy.wait()
    for step in range(micro):
        copies.arrived(("low", step), low.at[own_place(1 - core, step)])
    keep(low, low_out)
    close(2)
    keep(up_whole, up_out)
    for step in range(micro):
        copies.arrived(("normed two", step), normed_two.at[own_place(1 - core, step)])
    keep(normed_two, normed_two_out)
    tiles = activated.shape[1] // tile
    staged[0].wait()
    feed(0, tiles // 2)
    pass_on(3, 3)
    across(3, 2)
    feed(tiles // 2, tiles)
    keep(activated, activated_out)
    keep(hidden, hidden_out)
    across(3, 3)
    close(3)
    for copy in moved[sum(len(group) for group in kept) + 2 + len(load_low) :]:
        if copy is not staged[0]:
            copy.wait()
    copies.finish()


def forward(chips, micro, blocks, splits, packed, matrices, tokens, cotangent, starts):
    any_space = pl.BlockSpec(memory_space=pl.ANY)
    vmem = pl.BlockSpec(memory_space=pltpu.VMEM)
    own_rows, width = tokens.shape
    rows, half = 2 * own_rows, width // 2
    all_rows = rows + micro * BLOCK
    shapes = []
    for matrix, count in zip(matrices, splits):
        shard_rows, columns = matrix.shape
        whole = (chips * shard_rows, columns)
        shapes.append(whole if count is None else (2 * chips * shard_rows, columns // 2))
    hidden_width = shapes[2][1]

    def low(*shape):
        return jax.ShapeDtypeStruct(shape, LOW)

    def full(*shape):
        return jax.ShapeDtypeStruct(shape, F32)

    outs = [low(*shape) for shape in shapes] + [
        low(all_rows, 3 * half),
        low(rows, half),
        low(all_rows, width),
        low(rows, width),
        low(rows, hidden_width),
        full(rows, hidden_width),
        full(own_rows, width),
        low(rows, width),
        full(packed.shape[0], width),
    ]
    scratch = [pltpu.VMEM(shape, LOW) for shape in shapes[:3]] + [
        pltpu.VMEM((2 * chips,) + packed.shape, LOW),
        pltpu.VMEM((1, 3 * half), F32),
        pltpu.VMEM((1, hidden_width), F32),
        pltpu.VMEM((own_rows, width), LOW),
        pltpu.VMEM((rows, width), LOW),
        pltpu.VMEM((all_rows, width), LOW),
        pltpu.VMEM((all_rows, 3 * half), LOW),
        pltpu.VMEM((rows, half), LOW),
        pltpu.VMEM((own_rows, width), F32),
        pltpu.VMEM((own_rows, width), F32),
        pltpu.VMEM((own_rows, width), F32),
        pltpu.VMEM((rows, width), LOW),
        pltpu.VMEM((rows, hidden_width), LOW),
        pltpu.VMEM((rows, hidden_width), F32),
        pltpu.SemaphoreType.DMA((180,)),
        pltpu.SemaphoreType.DMA((180,)),
        pltpu.SemaphoreType.DMA((48,)),
    ]
    return pl.pallas_call(
        partial(forward_kernel, chips, micro, blocks, splits),
        out_shape=tuple(outs),
        in_specs=[any_space] * 7 + [vmem],
        out_specs=tuple([any_space] * 12 + [vmem]),
        scratch_shapes=scratch,
        compiler_params=pltpu.CompilerParams(
            collective_id=0, has_side_effects=True, vmem_limit_bytes=63_000_000
        ),
    )(packed, *matrices, tokens, cotangent, starts)


class Reduction:
    def __init__(self, at, copies, blocks_of, outs):
        self.at, self.copies, self.blocks_of, self.outs = at, copies, blocks_of, outs
        self.x_side, self.y_side = at.other(x=1), at.other(y=1)
        self.rep_x, self.rep_y, self.rep_xy = at.flipped(1), at.flipped(2), at.flipped(3)
        self.chunks = []

    def add(self, index, line, first, grad, across, from_x, from_y, from_z, totals):
        self.chunks.append((index, line, first, grad, across, from_x, from_y, from_z, totals))

    def send_across(self, n):
        _, _, _, grad, across, from_x, from_y, _, _ = self.chunks[n]
        half = grad.shape[2] // 2
        upper, lower = pl.ds(0, half), pl.ds(half, half)
        start = self.copies.start
        start(("ax", n), grad.at[:, self.rep_xy, upper], across.at[0], self.x_side)
        start(("ay", n), grad.at[:, self.rep_xy, lower], across.at[1], self.y_side)
        start(("bx", n), grad.at[:, self.rep_x, upper], from_x.at[:, upper], self.x_side)
        start(("by", n), grad.at[:, self.rep_y, lower], from_y.at[:, lower], self.y_side)

    def add_across(self, n):
        _, _, _, grad, across, from_x, from_y, _, _ = self.chunks[n]
        half = grad.shape[2] // 2
        upper, lower = pl.ds(0, half), pl.ds(half, half)
        self.copies.arrived(("ay", n), across.at[1])
        across[1] = (
            across[1].astype(F32) + grad[:, self.rep_x, half : 2 * half].astype(F32)
        ).astype(LOW)
        self.copies.start(("cx", n), across.at[1], from_x.at[:, lower], self.x_side)
        self.copies.arrived(("ax", n), across.at[0])
        across[0] = (across[0].astype(F32) + grad[:, self.rep_y, 0:half].astype(F32)).astype(LOW)
        self.copies.start(("cy", n), across.at[0], from_y.at[:, upper], self.y_side)

    def add_reps(self, n):
        _, _, _, grad, _, from_x, from_y, from_z, _ = self.chunks[n]
        at, half = self.at, grad.shape[2] // 2
        upper, lower = pl.ds(0, half), pl.ds(half, half)
        self.copies.arrived(("bx", n), from_x.at[:, upper])
        self.copies.arrived(("by", n), from_y.at[:, lower])
        self.copies.arrived(("cx", n), from_x.at[:, lower])
        self.copies.arrived(("cy", n), from_y.at[:, upper])
        from_x[...] = (
            grad[:, at.rep].astype(F32) + from_x[...].astype(F32) + from_y[...].astype(F32)
        ).astype(LOW)
        for step in range(1, at.chips):
            chip = lax.rem(at.chip + step, at.chips)
            self.copies.start(
                ("z", n, step), from_x.at[chip], from_z.at[step - 1], at.other(chip=chip)
            )

    def add_chips(self, n):
        _, _, _, grad, _, from_x, _, from_z, totals = self.chunks[n]
        at = self.at
        total = from_x[at.chip].astype(F32)
        for step in range(1, at.chips):
            self.copies.arrived(("z", n, step), from_z.at[step - 1])
            total = total + from_z[step - 1].astype(F32)
        totals[at.rep] = total.astype(LOW)
        own = totals.at[at.rep]
        self.copies.start(("ex", n), own, own, self.x_side)
        self.copies.start(("ey", n), own, own, self.y_side)

    def spread(self, n):
        totals = self.chunks[n][-1]
        half = totals.shape[1] // 2
        self.copies.arrived(("ex", n), totals.at[self.rep_x])
        part = totals.at[self.rep_x, pl.ds(0, half)]
        self.copies.start(("exy", n), part, part, self.y_side)
        self.copies.arrived(("ey", n), totals.at[self.rep_y])
        part = totals.at[self.rep_y, pl.ds(half, half)]
        self.copies.start(("eyx", n), part, part, self.x_side)

    def sides(self, n):
        index, first, width = self.chunks[n][0], self.chunks[n][2], self.chunks[n][-1].shape[2]
        block = self.blocks_of[index]
        for start in range(0, width, block):
            yield start, ((first + start) // block) * 2, block

    def deliver(self, n):
        index, line, first, totals = *self.chunks[n][:3], self.chunks[n][-1]
        quarter, width = totals.shape[1:]
        half, at = quarter // 2, self.at
        self.copies.arrived(("exy", n), totals.at[self.rep_xy, pl.ds(0, half)])
        self.copies.arrived(("eyx", n), totals.at[self.rep_xy, pl.ds(half, half)])
        out = self.outs[index]
        if self.blocks_of[index] is None:
            out[:, line : line + quarter, first : first + width] = totals[...]
            return
        for start, place, block in self.sides(n):
            columns = pl.ds(pl.multiple_of((place + at.core) * block, block), block)
            self.copies.start(
                ("pair", n, start),
                totals.at[pl.ds(2 * (1 - at.core), 2), :, pl.ds(start, block)],
                out.at[:, :, columns],
                at.other(core=1),
            )
            out[:, :, columns] = totals[pl.ds(2 * at.core, 2), :, start : start + block]

    def receive(self, n):
        index = self.chunks[n][0]
        if self.blocks_of[index] is None:
            return
        for start, place, block in self.sides(n):
            columns = pl.ds(pl.multiple_of((place + 1 - self.at.core) * block, block), block)
            self.copies.arrived(("pair", n, start), self.outs[index].at[:, :, columns])

    def tick(self, time):
        stages = (
            self.send_across,
            self.add_across,
            self.add_reps,
            self.add_chips,
            self.spread,
            self.deliver,
            self.receive,
        )
        for stage, offset in zip(stages, OFFSETS):
            if 0 <= time - offset < len(self.chunks):
                stage(time - offset)


OFFSETS = (0, 1, 2, 3, 5, 6, 7)
PART = 512
VECTOR_ROWS = 16


def gelu_slope(values):
    slope = float(2.0 / 3.141592653589793) ** 0.5
    square = values * values
    bend = jnp.tanh(slope * (values + 0.044715 * (values * square)))
    return 0.5 * (1.0 + bend) + 0.5 * values * (1.0 - bend * bend) * slope * (
        1.0 + 0.134145 * square
    )


def loop(count, body):
    def step(index, carry):
        body(index)
        return carry

    lax.fori_loop(0, count, step, 0)


def backward_kernel(chips, micro, blocks, blocks_of, *refs):
    (
        activated_in,
        down_low_in,
        hidden_in,
        normed_two_in,
        up_in,
        out_in,
        in_in,
        down_in,
        branch_in,
        mixed_in,
        all_normed_in,
        middle_in,
        tokens_in,
        starts,
        gains,
    ) = refs[:15]
    outs, vectors_out, input_grad_out, block_out = refs[15:19], refs[19], refs[20], refs[21]
    refs = refs[22:]
    (
        wide,
        deep,
        matrix,
        out_matrix,
        low,
        normed,
        branch,
        attended,
        give,
        came,
        middle,
        tokens,
        key_sums,
        halo,
        vectors,
        vectors_came,
    ) = refs[:16]
    credit, send, recv, local = refs[-4:]
    pools = refs[16:-4]
    at = Place(chips)
    core = at.core
    width = down_low_in.shape[1]
    rows = down_low_in.shape[0]
    body_rows, all_rows = rows, mixed_in.shape[0]
    part_width = mixed_in.shape[1] // 3
    hidden_width = hidden_in.shape[1]
    own_rows, micro_rows = rows // 2, rows // micro
    own_micro = micro_rows // 2
    copies = Copies(send, recv, at)

    loads = []

    def load(source, target):
        copy = pltpu.make_async_copy(source, target, local.at[len(loads)])
        copy.start()
        loads.append(copy)
        return copy

    half_give = own_rows // 2
    tile_sems = local.at[pl.ds(24, 2)]
    activated = wide.at[pl.ds(0, rows)]
    hidden_low = deep.at[pl.ds(0, rows)]
    mixed = wide.at[:, pl.ds(0, 3 * part_width)]
    mixed_grad = deep.at[:, pl.ds(0, 3 * part_width)]
    in_matrix = matrix.at[:, pl.ds(0, 3 * part_width)]
    normed_two = normed.at[pl.ds(0, rows)]
    load_first = [load(activated_in, activated), load(down_low_in, low)]
    down_matrix_rows = matrix.shape[1]
    load_down = [
        load(down_in.at[pl.ds(side * width, width)], matrix.at[:, pl.ds(side * width, width)])
        for side in range(down_matrix_rows // width)
    ]
    load_up = [load(normed_two_in, normed_two), load(middle_in, middle)]
    load_three = [load(out_in, out_matrix), load(branch_in, branch), load(tokens_in, tokens)]
    vectors[...] = jnp.zeros_like(vectors)
    at.greet(at.neighbours())

    reduction = Reduction(at, copies, blocks_of, outs)
    (
        grad_pool,
        grad_pool_out,
        across_pool,
        across_out,
        x_pool,
        x_out,
        y_pool,
        y_out,
        z_pool,
        z_out,
        t_pool,
        t_out,
    ) = pools
    quarter = PART // 8

    def pooled(n, grad_place, index, line, first):
        reduction.add(
            index,
            line,
            first,
            grad_pool.at[grad_place],
            across_pool.at[n],
            x_pool.at[n],
            y_pool.at[n],
            z_pool.at[n],
            t_pool.at[n],
        )

    down_parts, up_parts, in_parts = width // PART, hidden_width // PART, 3 * part_width // PART
    for part in range(down_parts):
        for line in range(2):
            n = 2 * part + line
            pooled(n, n, 3, line * quarter, part * PART)
    for part in range(up_parts):
        n = 2 * down_parts + part
        pooled(n, n, 2, 0, part * PART)
    reduction.add(1, 0, 0, grad_pool_out, across_out, x_out, y_out, z_out, t_out)
    first_in = len(reduction.chunks)
    for part in range(in_parts):
        pooled(first_in - 1 + part, part, 0, 0, part * PART)

    def own_place(row_side, step):
        return pl.ds(pl.multiple_of(step * micro_rows + row_side * own_micro, own_micro), own_micro)

    def dot_down(part):
        block = activated_in.shape[1] // chips

        def body(chip):
            left = activated[:, pl.ds(pl.multiple_of(chip * block, block), block)]
            result = rows_dot(left, low[:, part * PART : (part + 1) * PART]).astype(LOW)
            result = result.reshape(4, 2, quarter, PART)
            grad_pool[2 * part, chip] = result[:, 0]
            grad_pool[2 * part + 1, chip] = result[:, 1]

        loop(chips, body)

    def dot_pair(place, left, right, part):
        block = width // chips

        def body(chip):
            columns = left[:, pl.ds(pl.multiple_of(chip * block, block), block)]
            result = rows_dot(columns, right[:, part * PART : (part + 1) * PART]).astype(LOW)
            grad_pool[place, chip] = result.reshape(4, quarter, PART)

        loop(chips, body)

    def dot_up(part):
        dot_pair(2 * down_parts + part, normed_two, hidden_low, part)

    def dot_in(part):
        for key in ("ax", "ay", "bx", "by"):
            copies.sent((key, part))
        dot_pair(part, normed, mixed_grad, part)

    def dot_out():
        block = part_width // chips

        def body(chip):
            left = branch[:, pl.ds(pl.multiple_of(chip * block, block), block)]
            grad_pool_out[chip] = rows_dot(left, low[...]).astype(LOW).reshape(4, block // 4, width)

        loop(chips, body)

    def back_product(left, left_rows, right, target, target_rows, adding):
        tile = 256

        def body(step):
            columns = pl.ds(pl.multiple_of(step * tile, tile), tile)
            result = back_dot(left[left_rows, :], right[columns, :])
            if adding:
                result = result + target[target_rows, columns]
            target[target_rows, columns] = result.astype(target.dtype)

        loop(right.shape[0] // tile, body)

    def hidden_tile(row, side, slot):
        return pltpu.make_async_copy(
            hidden_in.at[
                pl.ds(pl.multiple_of(row * half_give, half_give), half_give),
                pl.ds(side * width, width),
            ],
            give.at[pl.ds(slot * half_give, half_give)],
            tile_sems.at[slot],
        )

    def hidden_gradient():
        count = rows // half_give
        for side in range(2):
            hidden_tile(0, side, side).start()

        def body(row):
            place = pl.ds(pl.multiple_of(row * half_give, half_give), half_give)
            for side in range(2):
                hidden_tile(row, side, side).wait()

                def strip(part):
                    start = side * width + part * 256
                    columns = pl.ds(pl.multiple_of(start, 256), 256)
                    from_place = pl.ds(pl.multiple_of(part * 256, 256), 256)
                    values = give[side * half_give : (side + 1) * half_give, from_place]
                    product = back_dot(low[place, :], matrix[from_place, side * width : (side + 1) * width])
                    hidden_low[place, columns] = (product * gelu_slope(values)).astype(LOW)

                loop(width // 256, strip)

                def following():
                    hidden_tile(row + 1, side, side).start()

                pl.when(row + 1 < count)(following)

        loop(count, body)

    def down_product(left_rows, target_rows, finish):
        def body(step):
            columns = pl.ds(pl.multiple_of(step * 256, 256), 256)
            result = None
            for side in range(2):
                start = pl.multiple_of(side * width + step * 256, 256)
                term = dot(
                    activated[left_rows, side * width : (side + 1) * width],
                    matrix[:, pl.ds(start, 256)],
                )
                result = term if result is None else result + term
            finish(target_rows, columns, result)

        loop(width // 256, body)

    def give_result():
        def finish(place, columns, result):
            give[place, columns] = result

        for step in range(micro):
            place = pl.ds(step * own_micro, own_micro)
            down_product(own_place(1 - core, step), place, finish)
        copies.start(("result",), give, came, at.other(core=1))

    def own_result():
        copies.arrived(("result",), came)

        def finish(place, columns, result):
            total = middle[place, columns] + (result + came[place, columns])
            block_out[place, columns] = (total + gains[7:8, columns]).astype(LOW)

        for step in range(micro):
            place = pl.ds(step * own_micro, own_micro)
            down_product(own_place(core, step), place, finish)
        pl.semaphore_signal(
            credit, 1, device_id=at.other(core=1), device_id_type=pl.DeviceIdType.MESH
        )

    def give_partial(name, left, right):
        for step in range(micro):
            place = pl.ds(step * own_micro, own_micro)
            back_product(left, own_place(1 - core, step), right, give, place, False)
        copies.start(name, give, came, at.other(core=1))

    def own_partial(name, left, right):
        copies.arrived(name, came)
        for step in range(micro):
            place = pl.ds(step * own_micro, own_micro)
            back_product(left, own_place(core, step), right, came, place, True)

    def column_sum(row, values):
        vectors[0, row : row + 1, :] += jnp.sum(values, axis=0, keepdims=True)

    lines = 32

    def second_norm_back():
        gain = gains[5:6, :]

        def body(step):
            place = pl.ds(pl.multiple_of(step * lines, lines), lines)
            chip_row = step // (own_micro // lines) * micro_rows + core * own_micro
            chip_row = chip_row + lax.rem(step, own_micro // lines) * lines
            chip_place = pl.ds(pl.multiple_of(chip_row, lines), lines)
            unit, inverse = normalize(middle[place, :])
            upper = came[place, :]
            upstream = low[chip_place, :].astype(F32)
            total = upstream + normalize_back(upper, gain, unit, inverse)
            middle[place, :] = total
            rounded = total.astype(LOW)
            low[chip_place, :] = rounded
            column_sum(2, rounded.astype(F32))
            column_sum(3, upper * unit)
            column_sum(4, upper)
            column_sum(5, upstream)

        loop(own_rows // lines, body)
        for step in range(micro):
            place = low.at[own_place(core, step)]
            copies.start(("low", step), place, place, at.other(core=1))

    def first_norm_back():
        gain = gains[0:1, :]

        def body(step):
            place = pl.ds(pl.multiple_of(step * lines, lines), lines)
            unit, inverse = normalize(tokens[place, :].astype(F32))
            upper = came[place, :]
            total = middle[place, :] + normalize_back(upper, gain, unit, inverse)
            input_grad_out[place, :] = total.astype(LOW)
            column_sum(0, upper * unit)
            column_sum(1, upper)

        loop(own_rows // lines, body)

    def hidden_sums():
        def body(step):
            place = pl.ds(pl.multiple_of(step * lines, lines), lines)
            for side in range(hidden_width // width):
                column_sum(
                    9 + side, hidden_low[place, side * width : (side + 1) * width].astype(F32)
                )

        loop(rows // lines, body)

    def mixed_sums():
        def body(step):
            place = pl.ds(pl.multiple_of(step * lines, lines), lines)
            joined = jnp.concatenate(
                [
                    mixed_grad[place, 0:part_width].astype(F32),
                    mixed_grad[place, 2 * part_width : 3 * part_width].astype(F32),
                ],
                axis=1,
            )
            column_sum(8, joined)

        loop(all_rows // lines, body)

    left = lax.broadcasted_iota(jnp.int32, (BLOCK, BLOCK), 1) < HD
    left_tall = lax.broadcasted_iota(jnp.int32, (2 * BLOCK, BLOCK), 1) < HD
    scale = float(HD) ** (-0.5)

    def attention_group(column):
        key_sums[...] = jnp.zeros_like(key_sums)

        def body(step):
            row, previous = block_rows(step, blocks, body_rows)
            allowed = allowed_keys(starts, row)
            queries = mixed[pl.ds(row, BLOCK), column : column + BLOCK]
            keys = window(mixed, row, previous, part_width + column)
            values = window(mixed, row, previous, 2 * part_width + column)
            upper = attended[pl.ds(row, BLOCK), column : column + BLOCK]
            parts = []
            for side in (left, ~left):
                soft = soft_weights(jnp.where(side, queries, 0), keys, allowed)
                soft_grad = back_dot(jnp.where(side, upper, 0), values)
                total = jnp.sum(soft * soft_grad, axis=1, keepdims=True)
                score_low = (soft * (soft_grad - total)).astype(LOW)
                parts.append(
                    (
                        dot(score_low, keys) * scale,
                        rows_dot(score_low, queries) * scale,
                        rows_dot(soft.astype(LOW), upper),
                    )
                )
            mixed_grad[pl.ds(row, BLOCK), column : column + BLOCK] = jnp.where(
                left, parts[0][0], parts[1][0]
            ).astype(LOW)
            for slot in (1, 2):
                joined = jnp.where(left_tall, parts[0][slot], parts[1][slot])
                place = (slot - 1) * BLOCK
                key_sums[pl.ds(previous, BLOCK), place : place + BLOCK] += joined[:BLOCK]
                key_sums[pl.ds(row, BLOCK), place : place + BLOCK] += joined[BLOCK:]

        loop(body_rows // BLOCK, body)
        for slot in (1, 2):
            place = (slot - 1) * BLOCK
            mixed_grad[:, slot * part_width + column : slot * part_width + column + BLOCK] = (
                key_sums[:, place : place + BLOCK].astype(LOW)
            )
        mixed_grad[body_rows:, column : column + BLOCK] = jnp.zeros(
            (all_rows - body_rows, BLOCK), LOW
        )

    lower_chip = at.other(chip=jnp.maximum(at.chip - 1, 0))

    def send_halo():
        copies.start(
            ("halo",),
            mixed_grad.at[pl.ds(body_rows, all_rows - body_rows), pl.ds(part_width, 2 * part_width)],
            halo,
            lower_chip,
            at.chip > 0,
        )

    def add_halo():
        copies.arrived(("halo",), halo, at.chip < chips - 1)

        def body():
            for step in range(micro):
                place = pl.ds((step + 1) * micro_rows - BLOCK, BLOCK)
                mixed_grad[place, part_width : 3 * part_width] = (
                    mixed_grad[place, part_width : 3 * part_width].astype(F32)
                    + halo[step * BLOCK : (step + 1) * BLOCK, :].astype(F32)
                ).astype(LOW)

        pl.when(at.chip < chips - 1)(body)

    time = iter(range(100))

    def tick():
        reduction.tick(next(time))

    def wait_for(members):
        for member in members:
            member.wait()

    wait_for(load_first)
    dot_down(0)
    tick()
    for part in range(1, down_parts):
        dot_down(part)
    tick()
    wait_for(load_down)
    hidden_gradient()
    tick()
    wait_for(load_up)
    give_result()
    for part in range(up_parts // 2):
        dot_up(part)
    own_result()
    load_two = [load(up_in, matrix), load(mixed_in, mixed)]
    tick()
    for part in range(up_parts // 2, up_parts):
        dot_up(part)
    hidden_sums()
    wait_for(load_two)
    copies.sent(("result",))
    pl.semaphore_wait(credit, 1)
    give_partial(("partial", 0), hidden_low, matrix)
    load_normed = [load(all_normed_in, normed)]
    own_partial(("partial", 0), hidden_low, matrix)
    load_last = [load(in_in, in_matrix)] + load_normed
    second_norm_back()
    tick()
    wait_for(load_three)
    for step in range(micro):
        back_product(
            low, own_place(core, step), out_matrix, attended, own_place(core, step), False
        )
    for step in range(micro):
        copies.arrived(("low", step), low.at[own_place(1 - core, step)])
        back_product(
            low, own_place(1 - core, step), out_matrix, attended, own_place(1 - core, step), False
        )
    dot_out()
    for column in range(0, part_width, BLOCK):
        attention_group(column)
        tick()
    send_halo()
    wait_for(load_last)
    dot_in(0)
    tick()
    for part in range(1, in_parts):
        dot_in(part)
        if part == in_parts - 1:
            mixed_sums()
            copies.sent(("halo",))
            add_halo()
            copies.sent(("partial", 0))
            give_partial(("partial", 1), mixed_grad, in_matrix)
        tick()
    own_partial(("partial", 1), mixed_grad, in_matrix)
    tick()
    first_norm_back()
    copies.start(("sum", "core"), vectors.at[0, pl.ds(0, 8)], vectors_came.at[0, pl.ds(0, 8)], at.other(core=1))
    tick()
    copies.arrived(("sum", "core"), vectors_came.at[0, pl.ds(0, 8)])
    vectors[1, 0:8, :] = vectors[0, 0:8, :] + vectors_came[0, 0:8, :]
    vectors[1, 8:16, :] = vectors[0, 8:16, :]
    copies.start(("sum", "x"), vectors.at[1], vectors_came.at[1], at.other(x=1))
    tick()
    copies.arrived(("sum", "x"), vectors_came.at[1])
    vectors[2] = vectors[1] + vectors_came[1]
    copies.start(("sum", "y"), vectors.at[2], vectors_came.at[2], at.other(y=1))
    tick()
    copies.arrived(("sum", "y"), vectors_came.at[2])
    vectors[3] = vectors[2] + vectors_came[2]
    for step in range(1, chips):
        copies.start(
            ("sum", "z", step),
            vectors.at[3],
            vectors_came.at[2 + step],
            at.other(chip=lax.rem(at.chip + step, chips)),
        )
    tick()
    total = vectors[3]
    for step in range(1, chips):
        copies.arrived(("sum", "z", step), vectors_came.at[2 + step])
        total = total + vectors_came[2 + step]
    vectors_out[...] = total
    for _ in range(OFFSETS[-1]):
        tick()
    copies.finish()


def backward(chips, micro, blocks, blocks_of, members, starts, gains):
    down_low, hidden_low, branch, mixed = members[1], members[2], members[8], members[9]
    rows, width = down_low.shape
    all_rows, hidden_width, part_width = mixed.shape[0], hidden_low.shape[1], branch.shape[1]
    own_rows = rows // 2
    quarter = PART // 8
    down_parts, up_parts, in_parts = width // PART, hidden_width // PART, 3 * part_width // PART
    pooled = 2 * down_parts + up_parts + in_parts
    any_space = pl.BlockSpec(memory_space=pl.ANY)
    vmem = pl.BlockSpec(memory_space=pltpu.VMEM)

    def low(*shape):
        return pltpu.VMEM(shape, LOW)

    def full(*shape):
        return pltpu.VMEM(shape, F32)

    out_quarter = part_width // (4 * chips)
    scratch = [
        low(all_rows, hidden_width),
        low(all_rows, hidden_width),
        low(width, hidden_width),
        low(part_width, width),
        low(rows, width),
        low(all_rows, width),
        low(rows, part_width),
        low(rows, part_width),
        full(own_rows, width),
        full(own_rows, width),
        full(own_rows, width),
        low(own_rows, width),
        full(all_rows, 2 * BLOCK),
        low(all_rows - rows, 2 * part_width),
        full(4, VECTOR_ROWS, width),
        full(chips + 2, VECTOR_ROWS, width),
        low(2 * down_parts + up_parts, chips, 4, quarter, PART),
        low(chips, 4, out_quarter, width),
        low(pooled, 2, chips, quarter // 2, PART),
        low(2, chips, out_quarter // 2, width),
        low(pooled, chips, quarter, PART),
        low(chips, out_quarter, width),
        low(pooled, chips, quarter, PART),
        low(chips, out_quarter, width),
        low(pooled, chips - 1, quarter, PART),
        low(chips - 1, out_quarter, width),
        low(pooled, 4, quarter, PART),
        low(4, out_quarter, width),
        pltpu.SemaphoreType.REGULAR,
        pltpu.SemaphoreType.DMA((240,)),
        pltpu.SemaphoreType.DMA((240,)),
        pltpu.SemaphoreType.DMA((26,)),
    ]
    out_shapes = [
        jax.ShapeDtypeStruct((2, width // (4 * chips), 6 * part_width), LOW),
        jax.ShapeDtypeStruct((4, out_quarter, width), LOW),
        jax.ShapeDtypeStruct((2, width // (4 * chips), 2 * hidden_width), LOW),
        jax.ShapeDtypeStruct((4, hidden_width // (4 * chips), width), LOW),
        jax.ShapeDtypeStruct((VECTOR_ROWS, width), F32),
        jax.ShapeDtypeStruct((own_rows, width), LOW),
        jax.ShapeDtypeStruct((own_rows, width), LOW),
    ]
    results = pl.pallas_call(
        partial(backward_kernel, chips, micro, blocks, blocks_of),
        out_shape=tuple(out_shapes),
        in_specs=[any_space] * 13 + [vmem] * 2,
        out_specs=tuple([vmem] * 7),
        scratch_shapes=scratch,
        compiler_params=pltpu.CompilerParams(
            collective_id=1, has_side_effects=True, vmem_limit_bytes=67_000_000
        ),
    )(*members, starts, gains)
    flat = [member.reshape(-1, member.shape[2]).astype(F32) for member in results[:4]]
    return flat, results[4], results[5], results[6]


def shards_general(
    chips,
    reps,
    tokens,
    cotangent,
    seq_lengths,
    dealing,
    attention_gain,
    attention_shift,
    input_weight,
    query_bias,
    value_bias,
    output_weight,
    output_bias,
    feed_gain,
    feed_shift,
    up_weight,
    up_bias,
    down_weight,
    down_bias,
):
    links = Links(chips, reps)
    core, chip = links.core, links.chip
    micro, tok_rows, width = tokens.shape
    shard_count = 2 * chips
    own_rows = micro * tok_rows
    blocks = 2 * tok_rows // BLOCK

    def own_of(values):
        return pick(values.reshape(micro, 2, tok_rows, -1), core, 1).reshape(own_rows, -1)

    def other_of(values):
        return pick(values.reshape(micro, 2, tok_rows, -1), 1 - core, 1).reshape(own_rows, -1)

    def pair_rows(own):
        came = links.swap(own, core=1)
        shape = (micro, 1, tok_rows, own.shape[-1])
        return links.by_core(own.reshape(shape), came.reshape(shape), 1).reshape(2 * own_rows, -1)

    def pair_sum(partial_values):
        return own_of(partial_values) + links.swap(other_of(partial_values), core=1)

    vectors = (
        attention_gain,
        attention_shift,
        query_bias,
        value_bias,
        output_bias,
        feed_gain,
        feed_shift,
        down_bias,
        up_bias,
    )
    lengths = [member.shape[0] for member in vectors]
    table = links.gather_vectors(jnp.concatenate(vectors)).astype(F32)
    wholes, at = [], 0
    for length in lengths:
        wholes.append(table[:, at : at + length])
        at += length

    def whole(index):
        return wholes[index].reshape(1, -1)

    def core_part(index):
        return pick(wholes[index].reshape(chips, 2, -1), core, 1).reshape(1, -1)

    input_part = links.gather(links.halves(input_weight, 3))
    output_part = links.gather(output_weight)
    up_part = links.gather(links.halves(up_weight, 1))
    down_part = links.gather(down_weight)

    inputs = tokens.reshape(own_rows, width).astype(F32)
    unit_one, inverse_one = normalize(inputs)
    normed = (unit_one * whole(0) + whole(1)).astype(LOW)
    chip_normed = pair_rows(normed)
    tail = chip_normed.reshape(micro, 2 * tok_rows, width)[:, 2 * tok_rows - BLOCK :]
    halo = links.shift(tail.reshape(micro * BLOCK, width), 1)
    all_normed = jnp.concatenate([chip_normed, halo], axis=0)
    down_low = pair_rows(cotangent.reshape(own_rows, width))
    first = chip * 2 * tok_rows
    starts = jnp.stack(
        [
            sequence_starts(seq_lengths[m, 0], dealing[m, 0], first, 2 * tok_rows)
            for m in range(micro)
        ]
    )
    block_first = first + jnp.arange(2 * tok_rows, dtype=jnp.int32) // BLOCK * BLOCK - BLOCK
    starts = (starts - block_first[None, :]).reshape(2 * own_rows, 1)

    half = width // 2
    bias = jnp.concatenate([core_part(2), jnp.zeros((1, half), F32), core_part(3)], axis=1)
    mixed = (dot(all_normed, input_part) + bias).astype(LOW)
    branch = attention(mixed, starts, blocks)
    middle = inputs + pair_sum(dot(branch, output_part)) + whole(4)
    unit_two, inverse_two = normalize(middle)
    normed_two = pair_rows((unit_two * whole(5) + whole(6)).astype(LOW))
    hidden = dot(normed_two, up_part) + core_part(8)
    activated, gelu_back = jax.vjp(gelu_tanh, hidden)
    activated = activated.astype(LOW)
    down_grad = links.reduce(rows_dot(activated, down_low)).astype(F32)
    result = middle + pair_sum(dot(activated, down_part)) + whole(7)

    upstream = cotangent.reshape(own_rows, width).astype(F32)
    (hidden_grad,) = gelu_back(back_dot(down_low, down_part))
    hidden_low = hidden_grad.astype(LOW)
    up_grad = links.unhalves(links.reduce(rows_dot(normed_two, hidden_low)), 1).astype(F32)
    upper_two = pair_sum(back_dot(hidden_low, up_part))
    middle_grad = upstream + normalize_back(upper_two, whole(5), unit_two, inverse_two)
    output_own = middle_grad.astype(LOW)
    output_low = pair_rows(output_own)
    output_grad = links.reduce(rows_dot(branch, output_low)).astype(F32)
    attended = back_dot(output_low, output_part).astype(LOW)
    mixed_grad = attention_back(mixed, starts, attended, blocks)
    input_weight_grad = links.unhalves(links.reduce(rows_dot(all_normed, mixed_grad)), 3).astype(F32)
    back_halo = links.shift(mixed_grad[2 * own_rows :, half:], -1)
    body = mixed_grad[: 2 * own_rows].reshape(micro, 2 * tok_rows, 3 * half)
    tail_grad = body[:, 2 * tok_rows - BLOCK :, half:].astype(F32) + back_halo.reshape(
        micro, BLOCK, width
    ).astype(F32)
    body = body.at[:, 2 * tok_rows - BLOCK :, half:].set(tail_grad.astype(LOW))
    upper_one = pair_sum(back_dot(body.reshape(2 * own_rows, 3 * half), input_part))
    input_grad = middle_grad + normalize_back(upper_one, whole(0), unit_one, inverse_one)

    def by_shard(values):
        return values.reshape(shard_count, -1)

    def by_core_shard(values):
        spread = values.reshape(chips, 1, -1)
        mask = jnp.arange(2, dtype=jnp.int32)[None, :, None] == core
        return jnp.where(mask, spread, 0.0).reshape(shard_count, -1)

    def column_sum(values):
        return jnp.sum(values.astype(F32), axis=0)

    packed = jnp.concatenate(
        [
            by_shard(column_sum(upper_one * unit_one)),
            by_shard(column_sum(upper_one)),
            by_core_shard(column_sum(mixed_grad[:, :half])),
            by_core_shard(column_sum(mixed_grad[:, width:])),
            by_shard(column_sum(output_own)),
            by_shard(column_sum(upper_two * unit_two)),
            by_shard(column_sum(upper_two)),
            by_shard(column_sum(upstream)),
            by_core_shard(column_sum(hidden_low)),
        ],
        axis=1,
    )
    sums = links.reduce_vectors(packed)
    vector_grads, at = [], 0
    for length in lengths:
        vector_grads.append(sums[at : at + length])
        at += length
    return (
        result.astype(LOW).reshape(tokens.shape),
        input_grad.astype(LOW).reshape(tokens.shape),
        vector_grads[0],
        vector_grads[1],
        input_weight_grad,
        vector_grads[2],
        vector_grads[3],
        output_grad,
        vector_grads[4],
        vector_grads[5],
        vector_grads[6],
        up_grad,
        vector_grads[8],
        down_grad,
        vector_grads[7],
    )


def shards(
    chips,
    reps,
    tokens,
    cotangent,
    seq_lengths,
    dealing,
    *weights,
):
    if chips != 4 or reps != 4:
        return shards_general(chips, reps, tokens, cotangent, seq_lengths, dealing, *weights)
    (
        attention_gain,
        attention_shift,
        input_weight,
        query_bias,
        value_bias,
        output_weight,
        output_bias,
        feed_gain,
        feed_shift,
        up_weight,
        up_bias,
        down_weight,
        down_bias,
    ) = weights
    shard = lax.axis_index("shard")
    chip = shard // 2
    micro, tok_rows, width = tokens.shape
    shard_count, half = 2 * chips, width // 2
    own_rows = micro * tok_rows
    blocks = 2 * tok_rows // BLOCK
    hidden_half = up_weight.shape[1] // 2

    packed = jnp.concatenate(
        [
            attention_gain,
            attention_shift,
            query_bias,
            value_bias,
            output_bias,
            feed_gain,
            feed_shift,
            down_bias,
            up_bias,
        ]
    )
    packed = jnp.pad(packed, (0, VECTOR_ROWS * BLOCK - packed.shape[0]))
    first = chip * 2 * tok_rows
    starts = jnp.stack(
        [
            sequence_starts(seq_lengths[m, 0], dealing[m, 0], first, 2 * tok_rows)
            for m in range(micro)
        ]
    )
    block_first = first + jnp.arange(2 * tok_rows, dtype=jnp.int32) // BLOCK * BLOCK - BLOCK
    starts = (starts - block_first[None, :]).reshape(2 * own_rows, 1)
    own_tokens = tokens.reshape(own_rows, width)
    (
        input_part,
        output_part,
        up_part,
        down_part,
        mixed,
        branch,
        all_normed,
        normed_two,
        activated,
        hidden,
        middle,
        down_low,
        vectors,
    ) = forward(
        chips,
        micro,
        blocks,
        (3 * chips, None, chips, None),
        packed.reshape(VECTOR_ROWS, BLOCK),
        (input_weight, output_weight, up_weight, down_weight),
        own_tokens,
        cotangent.reshape(own_rows, width),
        starts,
    )
    grads, sums, input_grad, block_out = backward(
        chips,
        micro,
        blocks,
        (width // shard_count, None, hidden_half // chips, None),
        (
            activated,
            down_low,
            hidden,
            normed_two,
            up_part,
            output_part,
            input_part,
            down_part,
            branch,
            mixed,
            all_normed,
            middle,
            own_tokens,
        ),
        starts,
        vectors,
    )
    input_weight_grad, output_grad, up_grad, down_grad = grads
    shared = pick(sums[:8].reshape(8, shard_count, -1), shard, 1)
    sides = pick(sums[8].reshape(2, chips, -1), chip, 1)
    up_sum = pick(sums[9:].reshape(-1)[:hidden_half].reshape(chips, -1), chip)
    return (
        block_out.reshape(tokens.shape),
        input_grad.reshape(tokens.shape),
        shared[0],
        shared[1],
        input_weight_grad,
        sides[0],
        sides[1],
        output_grad,
        shared[2],
        shared[3],
        shared[4],
        up_grad,
        up_sum,
        down_grad,
        shared[5],
    )


def solution(mesh):
    rows_spec = P(None, ("shard", "rep"), None)
    vector, matrix = P("shard"), P("shard", None)
    weight_specs = (
        vector,
        vector,
        matrix,
        vector,
        vector,
        matrix,
        vector,
        vector,
        vector,
        matrix,
        vector,
        matrix,
        vector,
    )
    return jax.shard_map(
        partial(shards, mesh.shape["shard"] // 2, mesh.shape["rep"]),
        mesh=mesh,
        in_specs=(rows_spec, rows_spec, P(None, "rep", None, None), P(None, "rep", None))
        + weight_specs,
        out_specs=(rows_spec, rows_spec) + weight_specs,
        check_vma=False,
    )
```

```python
from functools import partial

import jax
import jax.numpy as jnp
from jax import lax
from jax.experimental import pallas as pl
from jax.experimental.pallas import tpu as pltpu
from jax.sharding import PartitionSpec as P

HD = 64
BLOCK = 128
EPSILON = 1e-05
MASKED = -1e30
AXES = ("shard", "rep")
F32 = jnp.float32
LOW = jnp.bfloat16


def dot(left, right):
    return jnp.dot(left, right, preferred_element_type=F32)


def rows_dot(left, right):
    return lax.dot_general(left, right, (((0,), (0,)), ((), ())), preferred_element_type=F32)


def back_dot(left, right):
    return lax.dot_general(left, right, (((1,), (1,)), ((), ())), preferred_element_type=F32)


def pick(stacked, index, axis=0):
    return lax.dynamic_index_in_dim(stacked, index, axis, keepdims=False)


def normalize(values):
    center = values - jnp.mean(values, axis=-1, keepdims=True)
    inverse = lax.rsqrt(jnp.mean(center * center, axis=-1, keepdims=True) + EPSILON)
    return center * inverse, inverse


def normalize_back(upper, gain, unit, inverse):
    scaled = upper * gain
    mean_scaled = jnp.mean(scaled, axis=-1, keepdims=True)
    mean_product = jnp.mean(scaled * unit, axis=-1, keepdims=True)
    return inverse * (scaled - mean_scaled - unit * mean_product)


def gelu_tanh(values):
    return jax.nn.gelu(values, approximate=True)


def sequence_starts(seq_lengths, dealing, first, rows):
    total = dealing.shape[0]
    numbers = jnp.arange(total, dtype=jnp.int32)
    matched = (dealing[:, None] == numbers[None, :]).astype(jnp.int32)
    packed_length = jnp.sum(matched * seq_lengths.reshape(total)[None, :], axis=1)
    before = (numbers[None, :] < numbers[:, None]).astype(jnp.int32)
    packed_start = jnp.sum(before * packed_length[None, :], axis=1)
    own = first + jnp.arange(rows, dtype=jnp.int32)
    return jnp.max(
        jnp.where(packed_start[None, :] <= own[:, None], packed_start[None, :], 0), axis=1
    )


def window(ref, row, previous, column):
    return jnp.concatenate(
        [
            ref[pl.ds(previous, BLOCK), column : column + BLOCK],
            ref[pl.ds(row, BLOCK), column : column + BLOCK],
        ],
        axis=0,
    )


def block_rows(step, blocks, body_rows):
    micro, block = step // blocks, step % blocks
    row = pl.multiple_of(step * BLOCK, BLOCK)
    previous = jnp.where(block == 0, body_rows + micro * BLOCK, row - BLOCK)
    return row, pl.multiple_of(previous, BLOCK)


def soft_weights(query_half, keys, allowed):
    scores = back_dot(query_half, keys) * float(HD) ** (-0.5)
    scores = jnp.where(allowed, scores, MASKED)
    top = jnp.max(scores, axis=1, keepdims=True)
    powers = jnp.exp(scores - top)
    return powers / jnp.sum(powers, axis=1, keepdims=True)


def allowed_keys(start_ref, row):
    places = lax.broadcasted_iota(jnp.int32, (BLOCK, 2 * BLOCK), 1)
    lines = lax.broadcasted_iota(jnp.int32, (BLOCK, 2 * BLOCK), 0)
    return (places >= start_ref[pl.ds(row, BLOCK), :]) & (places <= lines + BLOCK)


def attention_kernel(blocks, width, mixed_ref, start_ref, branch_ref):
    body_rows = branch_ref.shape[0]
    left = lax.broadcasted_iota(jnp.int32, (BLOCK, BLOCK), 1) < HD

    def step_body(step, _):
        row, previous = block_rows(step, blocks, body_rows)
        allowed = allowed_keys(start_ref, row)
        for column in range(0, width, BLOCK):
            queries = mixed_ref[pl.ds(row, BLOCK), column : column + BLOCK]
            keys = window(mixed_ref, row, previous, width + column)
            values = window(mixed_ref, row, previous, 2 * width + column)
            parts = []
            for half in (left, ~left):
                soft = soft_weights(jnp.where(half, queries, 0), keys, allowed)
                parts.append(dot(soft.astype(LOW), values))
            branch_ref[pl.ds(row, BLOCK), column : column + BLOCK] = jnp.where(
                left, parts[0], parts[1]
            ).astype(LOW)
        return 0

    lax.fori_loop(0, body_rows // BLOCK, step_body, 0)


def attention_back_kernel(blocks, width, mixed_ref, start_ref, upper_ref, grad_ref, sums_ref):
    body_rows = upper_ref.shape[0]
    left = lax.broadcasted_iota(jnp.int32, (BLOCK, BLOCK), 1) < HD
    left_tall = lax.broadcasted_iota(jnp.int32, (2 * BLOCK, BLOCK), 1) < HD
    scale = float(HD) ** (-0.5)
    sums_ref[...] = jnp.zeros_like(sums_ref)

    def step_body(step, _):
        row, previous = block_rows(step, blocks, body_rows)
        allowed = allowed_keys(start_ref, row)
        for column in range(0, width, BLOCK):
            queries = mixed_ref[pl.ds(row, BLOCK), column : column + BLOCK]
            keys = window(mixed_ref, row, previous, width + column)
            values = window(mixed_ref, row, previous, 2 * width + column)
            upper = upper_ref[pl.ds(row, BLOCK), column : column + BLOCK]
            parts = []
            for half in (left, ~left):
                soft = soft_weights(jnp.where(half, queries, 0), keys, allowed)
                soft_grad = back_dot(jnp.where(half, upper, 0), values)
                total = jnp.sum(soft * soft_grad, axis=1, keepdims=True)
                score_low = (soft * (soft_grad - total)).astype(LOW)
                parts.append(
                    (
                        dot(score_low, keys) * scale,
                        rows_dot(score_low, queries) * scale,
                        rows_dot(soft.astype(LOW), upper),
                    )
                )
            grad_ref[pl.ds(row, BLOCK), column : column + BLOCK] = jnp.where(
                left, parts[0][0], parts[1][0]
            ).astype(LOW)
            for slot in (1, 2):
                joined = jnp.where(left_tall, parts[0][slot], parts[1][slot])
                place = (slot - 1) * width + column
                sums_ref[pl.ds(previous, BLOCK), place : place + BLOCK] += joined[:BLOCK]
                sums_ref[pl.ds(row, BLOCK), place : place + BLOCK] += joined[BLOCK:]
        return 0

    lax.fori_loop(0, body_rows // BLOCK, step_body, 0)
    grad_ref[:, width:] = sums_ref[...].astype(LOW)
    grad_ref[body_rows:, :width] = jnp.zeros((grad_ref.shape[0] - body_rows, width), LOW)


def attention(mixed, starts, blocks):
    width = mixed.shape[1] // 3
    rows = starts.shape[0]
    vmem = pl.BlockSpec(memory_space=pltpu.VMEM)
    return pl.pallas_call(
        partial(attention_kernel, blocks, width),
        out_shape=jax.ShapeDtypeStruct((rows, width), LOW),
        in_specs=[vmem, vmem],
        out_specs=vmem,
        cost_estimate=pl.CostEstimate(
            flops=rows * width * BLOCK * 16, bytes_accessed=8 << 20, transcendentals=0
        ),
        compiler_params=pltpu.CompilerParams(vmem_limit_bytes=40 << 20),
    )(mixed, starts)


def attention_back(mixed, starts, upper, blocks):
    width = mixed.shape[1] // 3
    rows = starts.shape[0]
    vmem = pl.BlockSpec(memory_space=pltpu.VMEM)
    return pl.pallas_call(
        partial(attention_back_kernel, blocks, width),
        out_shape=jax.ShapeDtypeStruct(mixed.shape, LOW),
        in_specs=[vmem, vmem, vmem],
        out_specs=vmem,
        scratch_shapes=[pltpu.VMEM((mixed.shape[0], 2 * width), F32)],
        cost_estimate=pl.CostEstimate(
            flops=rows * width * BLOCK * 40, bytes_accessed=16 << 20, transcendentals=0
        ),
        compiler_params=pltpu.CompilerParams(vmem_limit_bytes=40 << 20),
    )(mixed, starts, upper)


class Links:
    def __init__(self, chips, reps):
        self.chips, self.reps = chips, reps
        shard = lax.axis_index("shard")
        self.chip, self.core, self.rep = shard // 2, shard % 2, lax.axis_index("rep")

    def flat(self, chip, core, rep):
        return (chip * 2 + core) * self.reps + rep

    def swap(self, values, chip=0, core=0, rep=0):
        pairs = [
            (self.flat(a, b, d), self.flat(a ^ chip, b ^ core, d ^ rep))
            for a in range(self.chips)
            for b in range(2)
            for d in range(self.reps)
        ]
        return lax.ppermute(values, AXES, pairs)

    def shift(self, values, by):
        pairs = [
            (self.flat(a, b, d), self.flat(a + by, b, d))
            for a in range(self.chips)
            if 0 <= a + by < self.chips
            for b in range(2)
            for d in range(self.reps)
        ]
        return lax.ppermute(values, AXES, pairs)

    def by_core(self, own, other, axis):
        first = jnp.where(self.core == 0, own, other)
        second = jnp.where(self.core == 0, other, own)
        return jnp.concatenate([first, second], axis=axis)

    def halves(self, matrix, parts):
        rows, columns = matrix.shape
        blocks = self.chips * parts
        view = matrix.reshape(rows, blocks, 2, columns // (2 * blocks))
        keep = pick(view, self.core, 2).reshape(rows, columns // 2)
        give = pick(view, 1 - self.core, 2).reshape(rows, columns // 2)
        return self.by_core(keep, self.swap(give, core=1), 0)

    def gather(self, chip_rows):
        rows, columns = chip_rows.shape
        quarter = rows // self.reps
        quarters = chip_rows.reshape(self.reps, quarter, columns)
        piece = pick(quarters, self.rep)
        pieces = jnp.stack([self.swap(piece, chip=j) for j in range(1, self.chips)])
        found = [pieces] + [None] * (self.reps - 1)
        if self.reps == 4:
            half = quarter // 2
            found[1] = self.swap(pieces, rep=1)
            found[2] = self.swap(pieces, rep=2)
            upper = self.swap(found[1][:, :half], rep=2)
            lower = self.swap(found[2][:, half:], rep=1)
            found[3] = jnp.concatenate([upper, lower], axis=1)
        else:
            for j in range(1, self.reps):
                found[j] = self.swap(pieces, rep=j)
        stacked = jnp.stack(
            [
                jnp.concatenate([pick(quarters, self.rep ^ j)[None], found[j]], axis=0)
                for j in range(self.reps)
            ]
        )
        ordered = []
        for chip in range(self.chips):
            for rep in range(self.reps):
                at = (self.rep ^ rep, self.chip ^ chip, 0, 0)
                ordered.append(
                    lax.dynamic_slice(stacked, at, (1, 1, quarter, columns)).reshape(
                        quarter, columns
                    )
                )
        return jnp.concatenate(ordered, axis=0)

    def reduce(self, grads):
        chips, reps = self.chips, self.reps
        rows, columns = grads.shape
        quarter = rows // (chips * reps)
        view = grads.astype(LOW).reshape(chips, reps, quarter, columns)
        mine = pick(view, self.rep, 1).astype(F32)
        if reps == 4:
            half = quarter // 2
            across = pick(view, self.rep ^ 3, 1)
            upper = self.swap(across[:, :half], rep=1)
            lower = self.swap(across[:, half:], rep=2)
            to_x = pick(view, self.rep ^ 1, 1)
            to_y = pick(view, self.rep ^ 2, 1)
            to_x = jnp.concatenate(
                [to_x[:, :half], (to_x[:, half:].astype(F32) + lower.astype(F32)).astype(LOW)],
                axis=1,
            )
            to_y = jnp.concatenate(
                [(to_y[:, :half].astype(F32) + upper.astype(F32)).astype(LOW), to_y[:, half:]],
                axis=1,
            )
            mine = (
                mine + self.swap(to_x, rep=1).astype(F32) + self.swap(to_y, rep=2).astype(F32)
            )
        else:
            for j in range(1, reps):
                mine = mine + self.swap(pick(view, self.rep ^ j, 1), rep=j).astype(F32)
        total = pick(mine, self.chip)
        sends = mine.astype(LOW)
        for j in range(1, chips):
            total = total + self.swap(pick(sends, self.chip ^ j), chip=j).astype(F32)
        return self.spread(total.astype(LOW))

    def spread(self, own):
        if self.reps == 4:
            half = own.shape[0] // 2
            from_x = self.swap(own, rep=1)
            from_y = self.swap(own, rep=2)
            upper = self.swap(from_x[:half], rep=2)
            lower = self.swap(from_y[half:], rep=1)
            found = [own, from_x, from_y, jnp.concatenate([upper, lower], axis=0)]
        else:
            found = [own] + [self.swap(own, rep=j) for j in range(1, self.reps)]
        stacked = jnp.stack(found)
        return jnp.concatenate([pick(stacked, self.rep ^ j) for j in range(self.reps)], axis=0)

    def unhalves(self, chip_rows, parts):
        rows, columns = chip_rows.shape
        view = chip_rows.reshape(2, rows // 2, columns)
        blocks = self.chips * parts
        keep = pick(view, self.core).reshape(rows // 2, blocks, 1, columns // blocks)
        came = self.swap(pick(view, 1 - self.core), core=1)
        came = came.reshape(rows // 2, blocks, 1, columns // blocks)
        return self.by_core(keep, came, 2).reshape(rows // 2, 2 * columns)

    def gather_vectors(self, packed):
        pair = self.by_core(packed[None], self.swap(packed, core=1)[None], 0)
        found = jnp.stack([pair] + [self.swap(pair, chip=j) for j in range(1, self.chips)])
        ordered = [pick(found, self.chip ^ j) for j in range(self.chips)]
        return jnp.concatenate(ordered, axis=0)

    def reduce_vectors(self, partial_sums):
        chips, reps = self.chips, self.reps
        view = partial_sums.reshape(chips, 2, -1)
        total = None
        for a in range(chips):
            for b in range(2):
                row = pick(pick(view, self.chip ^ a), self.core ^ b)
                row = row if a == b == 0 else self.swap(row, chip=a, core=b)
                total = row if total is None else total + row
        terms = [total] + [self.swap(total, rep=j) for j in range(1, reps)]
        while len(terms) > 1:
            terms = [terms[i] + terms[i + 1] for i in range(0, len(terms), 2)]
        return terms[0]

class Copies:
    def __init__(self, send, recv, links):
        self.send, self.recv, self.links = send, recv, links
        self.places, self.started = {}, []

    def make(self, name, source, target, device):
        place = self.places.setdefault(name, len(self.places))
        return pltpu.make_async_remote_copy(
            src_ref=source,
            dst_ref=target,
            send_sem=self.send.at[place],
            recv_sem=self.recv.at[place],
            device_id=device,
            device_id_type=pl.DeviceIdType.MESH,
        )

    def start(self, name, source, target, device, when=None):
        copy = self.make(name, source, target, device)
        run_when(when, copy.start)
        self.started.append((name, when, copy))

    def arrived(self, name, target, when=None):
        copy = self.make(name, target, target, self.links.other(x=1))
        run_when(when, copy.wait_recv)

    def sent(self, name):
        for item in [item for item in self.started if item[0] == name]:
            run_when(item[1], item[2].wait_send)
            self.started.remove(item)

    def finish(self):
        for _, when, copy in self.started:
            run_when(when, copy.wait_send)


def run_when(when, body):
    if when is None:
        body()
    else:
        pl.when(when)(body)


class Place:
    def __init__(self, chips):
        shard = lax.axis_index("shard")
        self.chips, self.shard = chips, shard
        self.chip, self.core, self.rep = shard // 2, lax.rem(shard, 2), lax.axis_index("rep")

    def flipped(self, bits):
        x, y = lax.rem(self.rep, 2), self.rep // 2
        x = 1 - x if bits & 1 else x
        y = 1 - y if bits & 2 else y
        return y * 2 + x

    def other(self, x=0, y=0, core=0, chip=None):
        chip = self.chip if chip is None else chip
        side = 1 - self.core if core else self.core
        return {"shard": chip * 2 + side, "rep": self.flipped(x + 2 * y)}

    def shard_at(self, step):
        return lax.rem(self.shard + step, 2 * self.chips)

    def greet(self, barrier_devices):
        barrier = pltpu.get_barrier_semaphore()
        for device in barrier_devices:
            pl.semaphore_signal(barrier, 1, device_id=device, device_id_type=pl.DeviceIdType.MESH)
        pl.semaphore_wait(barrier, len(barrier_devices))

    def neighbours(self):
        shards = [
            {"shard": self.shard_at(step), "rep": self.rep} for step in range(1, 2 * self.chips)
        ]
        return shards + [self.other(x=1), self.other(y=1)]


def forward_kernel(chips, micro, blocks, splits, *refs):
    vec_in, in_in, out_in, up_in, down_in, tokens_in, cotangent_in, starts = refs[:8]
    (
        in_out,
        out_out,
        up_out,
        down_out,
        mixed_out,
        branch_out,
        all_normed_out,
        normed_two_out,
        activated_out,
        hidden_out,
        middle_out,
        low_out,
        vectors,
    ) = refs[8:21]
    (
        in_whole,
        out_whole,
        up_whole,
        table,
        mixed_bias,
        up_bias,
        tokens,
        low,
        all_normed,
        mixed,
        branch,
        give,
        came,
        middle,
        normed_two,
        activated,
        hidden,
        send,
        recv,
        local,
    ) = refs[21:]
    shards_in = (in_in, out_in, up_in, down_in)
    wholes = (in_whole, out_whole, up_whole, down_out)
    at = Place(chips)
    core = at.core
    copies = Copies(send, recv, at)
    all_rows, width = all_normed.shape
    rows = low.shape[0]
    own_rows, micro_rows = rows // 2, rows // micro
    own_micro = micro_rows // 2
    part_width = branch.shape[1]
    moved, staged = [], []

    down_stage = activated.at[pl.ds(0, down_in.shape[0]), pl.ds(0, width)]

    def keep(source, target):
        copy = pltpu.make_async_copy(source, target, local.at[len(moved)])
        copy.start()
        moved.append(copy)
        return copy

    def own_place(row_side, step):
        return pl.ds(pl.multiple_of(step * micro_rows + row_side * own_micro, own_micro), own_micro)

    load_tokens = keep(tokens_in, tokens)
    at.greet(at.neighbours())
    partner = at.other(core=1)
    load_table = keep(vec_in, table.at[at.shard])
    for step in range(1, 2 * chips):
        copies.start(
            ("vec", step), vec_in, table.at[at.shard], {"shard": at.shard_at(step), "rep": at.rep}
        )
    kept = []
    for index, (source, whole, count) in enumerate(zip(shards_in, wholes, splits)):
        shard_rows = source.shape[0]
        first = len(moved)
        if index == 3:
            keep(source, down_stage)
        elif count is None:
            place = pl.ds(pl.multiple_of(at.chip * shard_rows, shard_rows), shard_rows)
            keep(source, whole.at[place])
        else:
            piece_width = source.shape[1] // (2 * count)
            place = pl.ds(pl.multiple_of(at.shard * shard_rows, shard_rows), shard_rows)
            for block in range(count):
                columns = pl.ds(block * piece_width, piece_width)

                def side(which):
                    start = pl.multiple_of((2 * block + which) * piece_width, piece_width)
                    return pl.ds(start, piece_width)

                copies.start(
                    ("pair", index, block),
                    source.at[:, side(1 - core)],
                    whole.at[place, columns],
                    partner,
                )
                keep(source.at[:, side(core)], whole.at[place, columns])
        kept.append(moved[first:])
    load_low = []
    for step in range(micro):
        source = cotangent_in.at[pl.ds(step * own_micro, own_micro)]
        load_low.append(keep(source, low.at[own_place(core, step)]))
        copies.start(("low", step), source, low.at[own_place(core, step)], partner)

    def piece(index, chip, bits=None, side=None):
        whole = wholes[index]
        chip_rows = whole.shape[0] // chips
        size = chip_rows // 4
        start = chip * chip_rows + (at.rep if bits is None else at.flipped(bits)) * size
        if side is not None:
            size = size // 2
            start = start + side * size
        return whole.at[pl.ds(pl.multiple_of(start, size), size)]

    ways = (("up", 1), ("down", -1))

    def neighbour(step):
        return at.other(chip=jnp.clip(at.chip + step, 0, chips - 1))

    def can_send(step):
        return at.chip < chips - 1 if step > 0 else at.chip > 0

    def origins(index, distance):
        for name, step in ways:
            when = at.chip >= distance if step > 0 else at.chip + distance < chips
            chip = jnp.clip(at.chip - step * distance, 0, chips - 1)
            yield (name, index, distance), step, when, chip

    def open_z(index):
        for copy in kept[index]:
            copy.wait()
        if splits[index] is not None:
            shard_rows = shards_in[index].shape[0]
            piece_width = shards_in[index].shape[1] // (2 * splits[index])
            place = (at.chip * 2 + 1 - core) * shard_rows
            place = pl.ds(pl.multiple_of(place, shard_rows), shard_rows)
            for block in range(splits[index]):
                columns = pl.ds(block * piece_width, piece_width)
                copies.arrived(("pair", index, block), wholes[index].at[place, columns])
        mine = target = piece(index, at.chip)
        if index == 3:
            place = pl.ds(pl.multiple_of(at.chip * down_in.shape[0], down_in.shape[0]), down_in.shape[0])
            staged.append(keep(down_stage, down_out.at[place]))
            quarter = down_in.shape[0] // 4
            mine = down_in.at[pl.ds(pl.multiple_of(at.rep * quarter, quarter), quarter)]
        for name, step in ways:
            copies.start((name, index, 1), mine, target, neighbour(step), can_send(step))

    def pass_on(index, distance):
        for key, step, when, chip in origins(index, distance):
            found = piece(index, chip)
            copies.arrived(key, found, when)
            if distance < chips - 1:
                copies.start(
                    (key[0], index, distance + 1),
                    found,
                    found,
                    neighbour(step),
                    when & can_send(step),
                )
            copies.start(("x",) + key, found, found, at.other(x=1), when)
            copies.start(("y",) + key, found, found, at.other(y=1), when)

    def across(index, distance):
        for key, step, when, chip in origins(index, distance):
            copies.arrived(("x",) + key, piece(index, chip, 1), when)
            upper = piece(index, chip, 1, 0)
            copies.start(("xy",) + key, upper, upper, at.other(y=1), when)
            copies.arrived(("y",) + key, piece(index, chip, 2), when)
            lower = piece(index, chip, 2, 1)
            copies.start(("yx",) + key, lower, lower, at.other(x=1), when)

    def close(index):
        for distance in range(1, chips):
            for key, step, when, chip in origins(index, distance):
                copies.arrived(("xy",) + key, piece(index, chip, 3, 0), when)
                copies.arrived(("yx",) + key, piece(index, chip, 3, 1), when)

    lines = 32

    def own_lines(step):
        place = pl.ds(pl.multiple_of(step * lines, lines), lines)
        chip_row = step // (own_micro // lines) * micro_rows + core * own_micro
        chip_row = chip_row + lax.rem(step, own_micro // lines) * lines
        return place, pl.ds(pl.multiple_of(chip_row, lines), lines)

    def spread_vectors():
        load_table.wait()
        for step in range(1, 2 * chips):
            copies.arrived(("vec", step), table.at[at.shard_at(2 * chips - step)])
        for shard in range(2 * chips):
            vectors[:, shard * BLOCK : (shard + 1) * BLOCK] = table[shard].astype(F32)
        mixed_bias[...] = jnp.zeros_like(mixed_bias)
        each = up_bias.shape[1] // (chips * BLOCK)
        for chip in range(chips):
            member = table[2 * chip + core].astype(F32)
            columns = pl.ds(chip * BLOCK, BLOCK)
            mixed_bias[:, columns] = member[2:3, :]
            mixed_bias[:, pl.ds(2 * part_width + chip * BLOCK, BLOCK)] = member[3:4, :]
            for j in range(each):
                up_bias[:, pl.ds((chip * each + j) * BLOCK, BLOCK)] = member[8 + j : 9 + j, :]

    def halo_place(step):
        return pl.ds(rows + step * BLOCK, BLOCK)

    def first_norm():
        def body(step):
            place, chip_place = own_lines(step)
            unit, _ = normalize(tokens[place, :].astype(F32))
            all_normed[chip_place, :] = (unit * vectors[0:1, :] + vectors[1:2, :]).astype(LOW)

        loop(own_rows // lines, body)
        for step in range(micro):
            mine = all_normed.at[own_place(core, step)]
            copies.start(("normed", step), mine, mine, partner)
            tail = all_normed.at[pl.ds((step + 1) * micro_rows - BLOCK, BLOCK)]
            copies.start(
                ("halo", step),
                tail,
                all_normed.at[halo_place(step)],
                neighbour(1),
                can_send(1) & (core == 1),
            )

        def clear():
            all_normed[rows:, :] = jnp.zeros((all_rows - rows, width), LOW)

        pl.when(at.chip == 0)(clear)

    def halo_on():
        for step in range(micro):
            found = all_normed.at[halo_place(step)]
            received = (at.chip > 0) & (core == 1)
            copies.arrived(("halo", step), found, received)
            copies.start(("halo on", step), found, found, partner, received)

    def all_normed_ready():
        for step in range(micro):
            copies.arrived(("normed", step), all_normed.at[own_place(1 - core, step)])
            copies.arrived(
                ("halo on", step), all_normed.at[halo_place(step)], (at.chip > 0) & (core == 0)
            )

    tile = 256

    def mix():
        def body(step):
            columns = pl.ds(pl.multiple_of(step * tile, tile), tile)
            result = dot(all_normed[...], in_whole[:, columns]) + mixed_bias[:, columns]
            mixed[:, columns] = result.astype(LOW)

        loop(3 * part_width // tile, body)

    left = lax.broadcasted_iota(jnp.int32, (BLOCK, BLOCK), 1) < HD

    def attend(column):
        def body(step):
            row, previous = block_rows(step, blocks, rows)
            allowed = allowed_keys(starts, row)
            queries = mixed[pl.ds(row, BLOCK), column : column + BLOCK]
            keys = window(mixed, row, previous, part_width + column)
            values = window(mixed, row, previous, 2 * part_width + column)
            parts = []
            for side in (left, ~left):
                soft = soft_weights(jnp.where(side, queries, 0), keys, allowed)
                parts.append(dot(soft.astype(LOW), values))
            branch[pl.ds(row, BLOCK), column : column + BLOCK] = jnp.where(
                left, parts[0], parts[1]
            ).astype(LOW)

        loop(rows // BLOCK, body)

    def project(side, target):
        for step in range(micro):
            place = pl.ds(step * own_micro, own_micro)
            left_rows = branch[own_place(side, step), :]

            def body(part):
                columns = pl.ds(pl.multiple_of(part * tile, tile), tile)
                target[place, columns] = dot(left_rows, out_whole[:, columns])

            loop(width // tile, body)

    def second_norm():
        copies.arrived(("partial",), came)

        def body(step):
            place, chip_place = own_lines(step)
            total = tokens[place, :].astype(F32) + (middle[place, :] + came[place, :])
            total = total + vectors[4:5, :]
            middle[place, :] = total
            unit, _ = normalize(total)
            normed_two[chip_place, :] = (unit * vectors[5:6, :] + vectors[6:7, :]).astype(LOW)

        loop(own_rows // lines, body)
        for step in range(micro):
            mine = normed_two.at[own_place(core, step)]
            copies.start(("normed two", step), mine, mine, partner)

    def feed(first, last):
        def body(step):
            columns = pl.ds(pl.multiple_of((first + step) * tile, tile), tile)
            result = dot(normed_two[...], up_whole[:, columns]) + up_bias[:, columns]
            hidden[:, columns] = result
            activated[:, columns] = gelu_tanh(result).astype(LOW)

        loop(last - first, body)

    open_z(0)
    load_tokens.wait()
    spread_vectors()
    pass_on(0, 1)
    open_z(1)
    first_norm()
    pass_on(0, 2)
    across(0, 1)
    open_z(2)
    pass_on(0, 3)
    halo_on()
    across(0, 2)
    for distance in range(1, chips):
        pass_on(1, distance)
    across(0, 3)
    for distance in range(1, chips):
        across(1, distance)
    all_normed_ready()
    pass_on(2, 1)
    open_z(3)
    close(0)
    pass_on(2, 2)
    keep(in_whole, in_out)
    keep(all_normed, all_normed_out)
    mix()
    keep(mixed, mixed_out)
    across(2, 1)
    attend(0)
    attend(BLOCK)
    pass_on(2, 3)
    across(2, 2)
    attend(2 * BLOCK)
    pass_on(3, 1)
    attend(3 * BLOCK)
    keep(branch, branch_out)
    across(2, 3)
    close(1)
    keep(out_whole, out_out)
    project(1 - core, give)
    copies.start(("partial",), give, came, partner)
    project(core, middle)
    pass_on(3, 2)
    pass_on(3, 3)
    second_norm()
    across(3, 1)
    keep(middle, middle_out)
    for copy in load_low:
        copy.wait()
    for step in range(micro):
        copies.arrived(("low", step), low.at[own_place(1 - core, step)])
    keep(low, low_out)
    close(2)
    keep(up_whole, up_out)
    for step in range(micro):
        copies.arrived(("normed two", step), normed_two.at[own_place(1 - core, step)])
    keep(normed_two, normed_two_out)
    tiles = activated.shape[1] // tile
    staged[0].wait()
    feed(0, tiles // 2)
    across(3, 2)
    feed(tiles // 2, tiles)
    keep(activated, activated_out)
    keep(hidden, hidden_out)
    across(3, 3)
    close(3)
    for copy in moved[sum(len(group) for group in kept) + 2 + len(load_low) :]:
        if copy is not staged[0]:
            copy.wait()
    copies.finish()


def forward(chips, micro, blocks, splits, packed, matrices, tokens, cotangent, starts):
    any_space = pl.BlockSpec(memory_space=pl.ANY)
    vmem = pl.BlockSpec(memory_space=pltpu.VMEM)
    own_rows, width = tokens.shape
    rows, half = 2 * own_rows, width // 2
    all_rows = rows + micro * BLOCK
    shapes = []
    for matrix, count in zip(matrices, splits):
        shard_rows, columns = matrix.shape
        whole = (chips * shard_rows, columns)
        shapes.append(whole if count is None else (2 * chips * shard_rows, columns // 2))
    hidden_width = shapes[2][1]

    def low(*shape):
        return jax.ShapeDtypeStruct(shape, LOW)

    def full(*shape):
        return jax.ShapeDtypeStruct(shape, F32)

    outs = [low(*shape) for shape in shapes] + [
        low(all_rows, 3 * half),
        low(rows, half),
        low(all_rows, width),
        low(rows, width),
        low(rows, hidden_width),
        full(rows, hidden_width),
        full(own_rows, width),
        low(rows, width),
        full(packed.shape[0], width),
    ]
    scratch = [pltpu.VMEM(shape, LOW) for shape in shapes[:3]] + [
        pltpu.VMEM((2 * chips,) + packed.shape, LOW),
        pltpu.VMEM((1, 3 * half), F32),
        pltpu.VMEM((1, hidden_width), F32),
        pltpu.VMEM((own_rows, width), LOW),
        pltpu.VMEM((rows, width), LOW),
        pltpu.VMEM((all_rows, width), LOW),
        pltpu.VMEM((all_rows, 3 * half), LOW),
        pltpu.VMEM((rows, half), LOW),
        pltpu.VMEM((own_rows, width), F32),
        pltpu.VMEM((own_rows, width), F32),
        pltpu.VMEM((own_rows, width), F32),
        pltpu.VMEM((rows, width), LOW),
        pltpu.VMEM((rows, hidden_width), LOW),
        pltpu.VMEM((rows, hidden_width), F32),
        pltpu.SemaphoreType.DMA((180,)),
        pltpu.SemaphoreType.DMA((180,)),
        pltpu.SemaphoreType.DMA((48,)),
    ]
    return pl.pallas_call(
        partial(forward_kernel, chips, micro, blocks, splits),
        out_shape=tuple(outs),
        in_specs=[any_space] * 7 + [vmem],
        out_specs=tuple([any_space] * 12 + [vmem]),
        scratch_shapes=scratch,
        compiler_params=pltpu.CompilerParams(
            collective_id=0, has_side_effects=True, vmem_limit_bytes=63_000_000
        ),
    )(packed, *matrices, tokens, cotangent, starts)


class Reduction:
    def __init__(self, at, copies, blocks_of, outs):
        self.at, self.copies, self.blocks_of, self.outs = at, copies, blocks_of, outs
        self.x_side, self.y_side = at.other(x=1), at.other(y=1)
        self.rep_x, self.rep_y, self.rep_xy = at.flipped(1), at.flipped(2), at.flipped(3)
        self.chunks = []

    def add(self, index, line, first, grad, across, from_x, from_y, from_z, totals):
        self.chunks.append((index, line, first, grad, across, from_x, from_y, from_z, totals))

    def send_across(self, n):
        _, _, _, grad, across, from_x, from_y, _, _ = self.chunks[n]
        half = grad.shape[2] // 2
        upper, lower = pl.ds(0, half), pl.ds(half, half)
        start = self.copies.start
        start(("ax", n), grad.at[:, self.rep_xy, upper], across.at[0], self.x_side)
        start(("ay", n), grad.at[:, self.rep_xy, lower], across.at[1], self.y_side)
        start(("bx", n), grad.at[:, self.rep_x, upper], from_x.at[:, upper], self.x_side)
        start(("by", n), grad.at[:, self.rep_y, lower], from_y.at[:, lower], self.y_side)

    def add_across(self, n):
        _, _, _, grad, across, from_x, from_y, _, _ = self.chunks[n]
        half = grad.shape[2] // 2
        upper, lower = pl.ds(0, half), pl.ds(half, half)
        self.copies.arrived(("ay", n), across.at[1])
        across[1] = (
            across[1].astype(F32) + grad[:, self.rep_x, half : 2 * half].astype(F32)
        ).astype(LOW)
        self.copies.start(("cx", n), across.at[1], from_x.at[:, lower], self.x_side)
        self.copies.arrived(("ax", n), across.at[0])
        across[0] = (across[0].astype(F32) + grad[:, self.rep_y, 0:half].astype(F32)).astype(LOW)
        self.copies.start(("cy", n), across.at[0], from_y.at[:, upper], self.y_side)

    def add_reps(self, n):
        _, _, _, grad, _, from_x, from_y, from_z, _ = self.chunks[n]
        at, half = self.at, grad.shape[2] // 2
        upper, lower = pl.ds(0, half), pl.ds(half, half)
        self.copies.arrived(("bx", n), from_x.at[:, upper])
        self.copies.arrived(("by", n), from_y.at[:, lower])
        self.copies.arrived(("cx", n), from_x.at[:, lower])
        self.copies.arrived(("cy", n), from_y.at[:, upper])
        from_x[...] = (
            grad[:, at.rep].astype(F32) + from_x[...].astype(F32) + from_y[...].astype(F32)
        ).astype(LOW)
        for step in range(1, at.chips):
            chip = lax.rem(at.chip + step, at.chips)
            self.copies.start(
                ("z", n, step), from_x.at[chip], from_z.at[step - 1], at.other(chip=chip)
            )

    def add_chips(self, n):
        _, _, _, grad, _, from_x, _, from_z, totals = self.chunks[n]
        at = self.at
        total = from_x[at.chip].astype(F32)
        for step in range(1, at.chips):
            self.copies.arrived(("z", n, step), from_z.at[step - 1])
            total = total + from_z[step - 1].astype(F32)
        totals[at.rep] = total.astype(LOW)
        own = totals.at[at.rep]
        self.copies.start(("ex", n), own, own, self.x_side)
        self.copies.start(("ey", n), own, own, self.y_side)

    def spread(self, n):
        totals = self.chunks[n][-1]
        half = totals.shape[1] // 2
        self.copies.arrived(("ex", n), totals.at[self.rep_x])
        part = totals.at[self.rep_x, pl.ds(0, half)]
        self.copies.start(("exy", n), part, part, self.y_side)
        self.copies.arrived(("ey", n), totals.at[self.rep_y])
        part = totals.at[self.rep_y, pl.ds(half, half)]
        self.copies.start(("eyx", n), part, part, self.x_side)

    def sides(self, n):
        index, first, width = self.chunks[n][0], self.chunks[n][2], self.chunks[n][-1].shape[2]
        block = self.blocks_of[index]
        for start in range(0, width, block):
            yield start, ((first + start) // block) * 2, block

    def deliver(self, n):
        index, line, first, totals = *self.chunks[n][:3], self.chunks[n][-1]
        quarter, width = totals.shape[1:]
        half, at = quarter // 2, self.at
        self.copies.arrived(("exy", n), totals.at[self.rep_xy, pl.ds(0, half)])
        self.copies.arrived(("eyx", n), totals.at[self.rep_xy, pl.ds(half, half)])
        out = self.outs[index]
        if self.blocks_of[index] is None:
            out[:, line : line + quarter, first : first + width] = totals[...]
            return
        for start, place, block in self.sides(n):
            columns = pl.ds(pl.multiple_of((place + at.core) * block, block), block)
            self.copies.start(
                ("pair", n, start),
                totals.at[pl.ds(2 * (1 - at.core), 2), :, pl.ds(start, block)],
                out.at[:, :, columns],
                at.other(core=1),
            )
            out[:, :, columns] = totals[pl.ds(2 * at.core, 2), :, start : start + block]

    def receive(self, n):
        index = self.chunks[n][0]
        if self.blocks_of[index] is None:
            return
        for start, place, block in self.sides(n):
            columns = pl.ds(pl.multiple_of((place + 1 - self.at.core) * block, block), block)
            self.copies.arrived(("pair", n, start), self.outs[index].at[:, :, columns])

    def tick(self, time):
        stages = (
            self.add_across,
            self.send_across,
            self.add_reps,
            self.add_chips,
            self.spread,
            self.deliver,
            self.receive,
        )
        for stage, offset in zip(stages, OFFSETS):
            if 0 <= time - offset < len(self.chunks):
                stage(time - offset)


OFFSETS = (1, 0, 2, 3, 5, 6, 7)
PART = 512
VECTOR_ROWS = 16


def gelu_slope(values):
    slope = float(2.0 / 3.141592653589793) ** 0.5
    square = values * values
    bend = jnp.tanh(slope * (values + 0.044715 * (values * square)))
    return 0.5 * (1.0 + bend) + 0.5 * values * (1.0 - bend * bend) * slope * (
        1.0 + 0.134145 * square
    )


def loop(count, body):
    def step(index, carry):
        body(index)
        return carry

    lax.fori_loop(0, count, step, 0)


def backward_kernel(chips, micro, blocks, blocks_of, *refs):
    (
        activated_in,
        down_low_in,
        hidden_in,
        normed_two_in,
        up_in,
        out_in,
        in_in,
        down_in,
        branch_in,
        mixed_in,
        all_normed_in,
        middle_in,
        tokens_in,
        starts,
        gains,
    ) = refs[:15]
    outs, vectors_out, input_grad_out, block_out = refs[15:19], refs[19], refs[20], refs[21]
    refs = refs[22:]
    (
        wide,
        deep,
        matrix,
        out_matrix,
        low,
        normed,
        branch,
        attended,
        give,
        came,
        middle,
        tokens,
        key_sums,
        halo,
        vectors,
        vectors_came,
    ) = refs[:16]
    credit, send, recv, local = refs[-4:]
    pools = refs[16:-4]
    at = Place(chips)
    core = at.core
    width = down_low_in.shape[1]
    rows = down_low_in.shape[0]
    body_rows, all_rows = rows, mixed_in.shape[0]
    part_width = mixed_in.shape[1] // 3
    hidden_width = hidden_in.shape[1]
    own_rows, micro_rows = rows // 2, rows // micro
    own_micro = micro_rows // 2
    copies = Copies(send, recv, at)

    loads = []

    def load(source, target):
        copy = pltpu.make_async_copy(source, target, local.at[len(loads)])
        copy.start()
        loads.append(copy)
        return copy

    half_give = own_rows // 2
    tile_sems = local.at[pl.ds(24, 2)]
    activated = wide.at[pl.ds(0, rows)]
    hidden_low = deep.at[pl.ds(0, rows)]
    mixed = wide.at[:, pl.ds(0, 3 * part_width)]
    mixed_grad = deep.at[:, pl.ds(0, 3 * part_width)]
    in_matrix = matrix.at[:, pl.ds(0, 3 * part_width)]
    normed_two = normed.at[pl.ds(0, rows)]
    load_first = [load(activated_in, activated), load(down_low_in, low)]
    down_matrix_rows = matrix.shape[1]
    load_down = [
        load(down_in.at[pl.ds(side * width, width)], matrix.at[:, pl.ds(side * width, width)])
        for side in range(down_matrix_rows // width)
    ]
    load_up = [load(normed_two_in, normed_two), load(middle_in, middle)]
    load_three = [load(out_in, out_matrix), load(branch_in, branch), load(tokens_in, tokens)]
    vectors[...] = jnp.zeros_like(vectors)
    at.greet(at.neighbours())

    reduction = Reduction(at, copies, blocks_of, outs)
    (
        grad_pool,
        grad_pool_out,
        across_pool,
        across_out,
        x_pool,
        x_out,
        y_pool,
        y_out,
        z_pool,
        z_out,
        t_pool,
        t_out,
    ) = pools
    quarter = PART // 8

    def pooled(n, grad_place, index, line, first):
        reduction.add(
            index,
            line,
            first,
            grad_pool.at[grad_place],
            across_pool.at[n],
            x_pool.at[n],
            y_pool.at[n],
            z_pool.at[n],
            t_pool.at[n],
        )

    down_parts, up_parts, in_parts = width // PART, hidden_width // PART, 3 * part_width // PART
    for part in range(down_parts):
        for line in range(2):
            n = 2 * part + line
            pooled(n, n, 3, line * quarter, part * PART)
    for part in range(up_parts):
        n = 2 * down_parts + part
        pooled(n, n, 2, 0, part * PART)
    reduction.add(1, 0, 0, grad_pool_out, across_out, x_out, y_out, z_out, t_out)
    first_in = len(reduction.chunks)
    for part in range(in_parts):
        pooled(first_in - 1 + part, part, 0, 0, part * PART)

    def own_place(row_side, step):
        return pl.ds(pl.multiple_of(step * micro_rows + row_side * own_micro, own_micro), own_micro)

    def dot_down(part):
        block = activated_in.shape[1] // chips

        def body(chip):
            left = activated[:, pl.ds(pl.multiple_of(chip * block, block), block)]
            result = rows_dot(left, low[:, part * PART : (part + 1) * PART]).astype(LOW)
            result = result.reshape(4, 2, quarter, PART)
            grad_pool[2 * part, chip] = result[:, 0]
            grad_pool[2 * part + 1, chip] = result[:, 1]

        loop(chips, body)

    def dot_pair(place, left, right, part):
        block = width // chips

        def body(chip):
            columns = left[:, pl.ds(pl.multiple_of(chip * block, block), block)]
            result = rows_dot(columns, right[:, part * PART : (part + 1) * PART]).astype(LOW)
            grad_pool[place, chip] = result.reshape(4, quarter, PART)

        loop(chips, body)

    def dot_up(part):
        dot_pair(2 * down_parts + part, normed_two, hidden_low, part)

    def dot_in(part):
        for key in ("ax", "ay", "bx", "by"):
            copies.sent((key, part))
        dot_pair(part, normed, mixed_grad, part)

    def dot_out():
        block = part_width // chips

        def body(chip):
            left = branch[:, pl.ds(pl.multiple_of(chip * block, block), block)]
            grad_pool_out[chip] = rows_dot(left, low[...]).astype(LOW).reshape(4, block // 4, width)

        loop(chips, body)

    def back_product(left, left_rows, right, target, target_rows, adding):
        tile = 256

        def body(step):
            columns = pl.ds(pl.multiple_of(step * tile, tile), tile)
            result = back_dot(left[left_rows, :], right[columns, :])
            if adding:
                result = result + target[target_rows, columns]
            target[target_rows, columns] = result.astype(target.dtype)

        loop(right.shape[0] // tile, body)

    def hidden_tile(row, side, slot):
        return pltpu.make_async_copy(
            hidden_in.at[
                pl.ds(pl.multiple_of(row * half_give, half_give), half_give),
                pl.ds(side * width, width),
            ],
            give.at[pl.ds(slot * half_give, half_give)],
            tile_sems.at[slot],
        )

    def hidden_gradient():
        count = rows // half_give
        for side in range(2):
            hidden_tile(0, side, side).start()

        def body(row):
            place = pl.ds(pl.multiple_of(row * half_give, half_give), half_give)
            for side in range(2):
                hidden_tile(row, side, side).wait()

                def strip(part):
                    start = side * width + part * 256
                    columns = pl.ds(pl.multiple_of(start, 256), 256)
                    from_place = pl.ds(pl.multiple_of(part * 256, 256), 256)
                    values = give[side * half_give : (side + 1) * half_give, from_place]
                    product = back_dot(low[place, :], matrix[from_place, side * width : (side + 1) * width])
                    hidden_low[place, columns] = (product * gelu_slope(values)).astype(LOW)

                loop(width // 256, strip)

                def following():
                    hidden_tile(row + 1, side, side).start()

                pl.when(row + 1 < count)(following)

        loop(count, body)

    def down_product(left_rows, target_rows, finish):
        def body(step):
            columns = pl.ds(pl.multiple_of(step * 256, 256), 256)
            result = None
            for side in range(2):
                start = pl.multiple_of(side * width + step * 256, 256)
                term = dot(
                    activated[left_rows, side * width : (side + 1) * width],
                    matrix[:, pl.ds(start, 256)],
                )
                result = term if result is None else result + term
            finish(target_rows, columns, result)

        loop(width // 256, body)

    def give_result():
        def finish(place, columns, result):
            give[place, columns] = result

        for step in range(micro):
            place = pl.ds(step * own_micro, own_micro)
            down_product(own_place(1 - core, step), place, finish)
        copies.start(("result",), give, came, at.other(core=1))

    def own_result():
        copies.arrived(("result",), came)

        def finish(place, columns, result):
            total = middle[place, columns] + (result + came[place, columns])
            block_out[place, columns] = (total + gains[7:8, columns]).astype(LOW)

        for step in range(micro):
            place = pl.ds(step * own_micro, own_micro)
            down_product(own_place(core, step), place, finish)
        pl.semaphore_signal(
            credit, 1, device_id=at.other(core=1), device_id_type=pl.DeviceIdType.MESH
        )

    def give_partial(name, left, right):
        for step in range(micro):
            place = pl.ds(step * own_micro, own_micro)
            back_product(left, own_place(1 - core, step), right, give, place, False)
        copies.start(name, give, came, at.other(core=1))

    def own_partial(name, left, right):
        copies.arrived(name, came)
        for step in range(micro):
            place = pl.ds(step * own_micro, own_micro)
            back_product(left, own_place(core, step), right, came, place, True)

    def column_sum(row, values):
        vectors[0, row : row + 1, :] += jnp.sum(values, axis=0, keepdims=True)

    lines = 32

    def second_norm_back():
        gain = gains[5:6, :]

        def body(step):
            place = pl.ds(pl.multiple_of(step * lines, lines), lines)
            chip_row = step // (own_micro // lines) * micro_rows + core * own_micro
            chip_row = chip_row + lax.rem(step, own_micro // lines) * lines
            chip_place = pl.ds(pl.multiple_of(chip_row, lines), lines)
            unit, inverse = normalize(middle[place, :])
            upper = came[place, :]
            upstream = low[chip_place, :].astype(F32)
            total = upstream + normalize_back(upper, gain, unit, inverse)
            middle[place, :] = total
            rounded = total.astype(LOW)
            low[chip_place, :] = rounded
            column_sum(2, rounded.astype(F32))
            column_sum(3, upper * unit)
            column_sum(4, upper)
            column_sum(5, upstream)

        loop(own_rows // lines, body)
        for step in range(micro):
            place = low.at[own_place(core, step)]
            copies.start(("low", step), place, place, at.other(core=1))

    def first_norm_back():
        gain = gains[0:1, :]

        def body(step):
            place = pl.ds(pl.multiple_of(step * lines, lines), lines)
            unit, inverse = normalize(tokens[place, :].astype(F32))
            upper = came[place, :]
            total = middle[place, :] + normalize_back(upper, gain, unit, inverse)
            input_grad_out[place, :] = total.astype(LOW)
            column_sum(0, upper * unit)
            column_sum(1, upper)

        loop(own_rows // lines, body)

    def hidden_sums():
        def body(step):
            place = pl.ds(pl.multiple_of(step * lines, lines), lines)
            for side in range(hidden_width // width):
                column_sum(
                    9 + side, hidden_low[place, side * width : (side + 1) * width].astype(F32)
                )

        loop(rows // lines, body)

    def mixed_sums():
        def body(step):
            place = pl.ds(pl.multiple_of(step * lines, lines), lines)
            joined = jnp.concatenate(
                [
                    mixed_grad[place, 0:part_width].astype(F32),
                    mixed_grad[place, 2 * part_width : 3 * part_width].astype(F32),
                ],
                axis=1,
            )
            column_sum(8, joined)

        loop(all_rows // lines, body)

    left = lax.broadcasted_iota(jnp.int32, (BLOCK, BLOCK), 1) < HD
    left_tall = lax.broadcasted_iota(jnp.int32, (2 * BLOCK, BLOCK), 1) < HD
    scale = float(HD) ** (-0.5)

    def attention_group(column):
        key_sums[...] = jnp.zeros_like(key_sums)

        def body(step):
            row, previous = block_rows(step, blocks, body_rows)
            allowed = allowed_keys(starts, row)
            queries = mixed[pl.ds(row, BLOCK), column : column + BLOCK]
            keys = window(mixed, row, previous, part_width + column)
            values = window(mixed, row, previous, 2 * part_width + column)
            upper = attended[pl.ds(row, BLOCK), column : column + BLOCK]
            parts = []
            for side in (left, ~left):
                soft = soft_weights(jnp.where(side, queries, 0), keys, allowed)
                soft_grad = back_dot(jnp.where(side, upper, 0), values)
                total = jnp.sum(soft * soft_grad, axis=1, keepdims=True)
                score_low = (soft * (soft_grad - total)).astype(LOW)
                parts.append(
                    (
                        dot(score_low, keys) * scale,
                        rows_dot(score_low, queries) * scale,
                        rows_dot(soft.astype(LOW), upper),
                    )
                )
            mixed_grad[pl.ds(row, BLOCK), column : column + BLOCK] = jnp.where(
                left, parts[0][0], parts[1][0]
            ).astype(LOW)
            for slot in (1, 2):
                joined = jnp.where(left_tall, parts[0][slot], parts[1][slot])
                place = (slot - 1) * BLOCK
                key_sums[pl.ds(previous, BLOCK), place : place + BLOCK] += joined[:BLOCK]
                key_sums[pl.ds(row, BLOCK), place : place + BLOCK] += joined[BLOCK:]

        loop(body_rows // BLOCK, body)
        for slot in (1, 2):
            place = (slot - 1) * BLOCK
            mixed_grad[:, slot * part_width + column : slot * part_width + column + BLOCK] = (
                key_sums[:, place : place + BLOCK].astype(LOW)
            )
        mixed_grad[body_rows:, column : column + BLOCK] = jnp.zeros(
            (all_rows - body_rows, BLOCK), LOW
        )

    lower_chip = at.other(chip=jnp.maximum(at.chip - 1, 0))

    def send_halo():
        copies.start(
            ("halo",),
            mixed_grad.at[pl.ds(body_rows, all_rows - body_rows), pl.ds(part_width, 2 * part_width)],
            halo,
            lower_chip,
            at.chip > 0,
        )

    def add_halo():
        copies.arrived(("halo",), halo, at.chip < chips - 1)

        def body():
            for step in range(micro):
                place = pl.ds((step + 1) * micro_rows - BLOCK, BLOCK)
                mixed_grad[place, part_width : 3 * part_width] = (
                    mixed_grad[place, part_width : 3 * part_width].astype(F32)
                    + halo[step * BLOCK : (step + 1) * BLOCK, :].astype(F32)
                ).astype(LOW)

        pl.when(at.chip < chips - 1)(body)

    time = iter(range(100))

    def tick():
        reduction.tick(next(time))

    def wait_for(members):
        for member in members:
            member.wait()

    wait_for(load_first)
    dot_down(0)
    tick()
    for part in range(1, down_parts):
        dot_down(part)
    tick()
    wait_for(load_down)
    hidden_gradient()
    tick()
    wait_for(load_up)
    give_result()
    for part in range(up_parts // 2):
        dot_up(part)
    own_result()
    load_two = [load(up_in, matrix), load(mixed_in, mixed)]
    tick()
    for part in range(up_parts // 2, up_parts):
        dot_up(part)
    hidden_sums()
    wait_for(load_two)
    copies.sent(("result",))
    pl.semaphore_wait(credit, 1)
    give_partial(("partial", 0), hidden_low, matrix)
    load_normed = [load(all_normed_in, normed)]
    own_partial(("partial", 0), hidden_low, matrix)
    load_last = [load(in_in, in_matrix)] + load_normed
    second_norm_back()
    tick()
    wait_for(load_three)
    for step in range(micro):
        back_product(
            low, own_place(core, step), out_matrix, attended, own_place(core, step), False
        )
    for step in range(micro):
        copies.arrived(("low", step), low.at[own_place(1 - core, step)])
        back_product(
            low, own_place(1 - core, step), out_matrix, attended, own_place(1 - core, step), False
        )
    dot_out()
    for column in range(0, part_width, BLOCK):
        attention_group(column)
        tick()
    send_halo()
    wait_for(load_last)
    dot_in(0)
    tick()
    for part in range(1, in_parts):
        dot_in(part)
        if part == in_parts - 1:
            mixed_sums()
            copies.sent(("halo",))
            add_halo()
            copies.sent(("partial", 0))
            give_partial(("partial", 1), mixed_grad, in_matrix)
        tick()
    own_partial(("partial", 1), mixed_grad, in_matrix)
    tick()
    first_norm_back()
    copies.start(("sum", "core"), vectors.at[0, pl.ds(0, 8)], vectors_came.at[0, pl.ds(0, 8)], at.other(core=1))
    tick()
    copies.arrived(("sum", "core"), vectors_came.at[0, pl.ds(0, 8)])
    vectors[1, 0:8, :] = vectors[0, 0:8, :] + vectors_came[0, 0:8, :]
    vectors[1, 8:16, :] = vectors[0, 8:16, :]
    copies.start(("sum", "x"), vectors.at[1], vectors_came.at[1], at.other(x=1))
    tick()
    copies.arrived(("sum", "x"), vectors_came.at[1])
    vectors[2] = vectors[1] + vectors_came[1]
    copies.start(("sum", "y"), vectors.at[2], vectors_came.at[2], at.other(y=1))
    tick()
    copies.arrived(("sum", "y"), vectors_came.at[2])
    vectors[3] = vectors[2] + vectors_came[2]
    for step in range(1, chips):
        copies.start(
            ("sum", "z", step),
            vectors.at[3],
            vectors_came.at[2 + step],
            at.other(chip=lax.rem(at.chip + step, chips)),
        )
    tick()
    total = vectors[3]
    for step in range(1, chips):
        copies.arrived(("sum", "z", step), vectors_came.at[2 + step])
        total = total + vectors_came[2 + step]
    vectors_out[...] = total
    for _ in range(7):
        tick()
    copies.finish()


def backward(chips, micro, blocks, blocks_of, members, starts, gains):
    down_low, hidden_low, branch, mixed = members[1], members[2], members[8], members[9]
    rows, width = down_low.shape
    all_rows, hidden_width, part_width = mixed.shape[0], hidden_low.shape[1], branch.shape[1]
    own_rows = rows // 2
    quarter = PART // 8
    down_parts, up_parts, in_parts = width // PART, hidden_width // PART, 3 * part_width // PART
    pooled = 2 * down_parts + up_parts + in_parts
    any_space = pl.BlockSpec(memory_space=pl.ANY)
    vmem = pl.BlockSpec(memory_space=pltpu.VMEM)

    def low(*shape):
        return pltpu.VMEM(shape, LOW)

    def full(*shape):
        return pltpu.VMEM(shape, F32)

    out_quarter = part_width // (4 * chips)
    scratch = [
        low(all_rows, hidden_width),
        low(all_rows, hidden_width),
        low(width, hidden_width),
        low(part_width, width),
        low(rows, width),
        low(all_rows, width),
        low(rows, part_width),
        low(rows, part_width),
        full(own_rows, width),
        full(own_rows, width),
        full(own_rows, width),
        low(own_rows, width),
        full(all_rows, 2 * BLOCK),
        low(all_rows - rows, 2 * part_width),
        full(4, VECTOR_ROWS, width),
        full(chips + 2, VECTOR_ROWS, width),
        low(2 * down_parts + up_parts, chips, 4, quarter, PART),
        low(chips, 4, out_quarter, width),
        low(pooled, 2, chips, quarter // 2, PART),
        low(2, chips, out_quarter // 2, width),
        low(pooled, chips, quarter, PART),
        low(chips, out_quarter, width),
        low(pooled, chips, quarter, PART),
        low(chips, out_quarter, width),
        low(pooled, chips - 1, quarter, PART),
        low(chips - 1, out_quarter, width),
        low(pooled, 4, quarter, PART),
        low(4, out_quarter, width),
        pltpu.SemaphoreType.REGULAR,
        pltpu.SemaphoreType.DMA((240,)),
        pltpu.SemaphoreType.DMA((240,)),
        pltpu.SemaphoreType.DMA((26,)),
    ]
    out_shapes = [
        jax.ShapeDtypeStruct((2, width // (4 * chips), 6 * part_width), LOW),
        jax.ShapeDtypeStruct((4, out_quarter, width), LOW),
        jax.ShapeDtypeStruct((2, width // (4 * chips), 2 * hidden_width), LOW),
        jax.ShapeDtypeStruct((4, hidden_width // (4 * chips), width), LOW),
        jax.ShapeDtypeStruct((VECTOR_ROWS, width), F32),
        jax.ShapeDtypeStruct((own_rows, width), LOW),
        jax.ShapeDtypeStruct((own_rows, width), LOW),
    ]
    results = pl.pallas_call(
        partial(backward_kernel, chips, micro, blocks, blocks_of),
        out_shape=tuple(out_shapes),
        in_specs=[any_space] * 13 + [vmem] * 2,
        out_specs=tuple([vmem] * 7),
        scratch_shapes=scratch,
        compiler_params=pltpu.CompilerParams(
            collective_id=1, has_side_effects=True, vmem_limit_bytes=67_000_000
        ),
    )(*members, starts, gains)
    return results


def shards_general(
    chips,
    reps,
    tokens,
    cotangent,
    seq_lengths,
    dealing,
    attention_gain,
    attention_shift,
    input_weight,
    query_bias,
    value_bias,
    output_weight,
    output_bias,
    feed_gain,
    feed_shift,
    up_weight,
    up_bias,
    down_weight,
    down_bias,
):
    links = Links(chips, reps)
    core, chip = links.core, links.chip
    micro, tok_rows, width = tokens.shape
    shard_count = 2 * chips
    own_rows = micro * tok_rows
    blocks = 2 * tok_rows // BLOCK

    def own_of(values):
        return pick(values.reshape(micro, 2, tok_rows, -1), core, 1).reshape(own_rows, -1)

    def other_of(values):
        return pick(values.reshape(micro, 2, tok_rows, -1), 1 - core, 1).reshape(own_rows, -1)

    def pair_rows(own):
        came = links.swap(own, core=1)
        shape = (micro, 1, tok_rows, own.shape[-1])
        return links.by_core(own.reshape(shape), came.reshape(shape), 1).reshape(2 * own_rows, -1)

    def pair_sum(partial_values):
        return own_of(partial_values) + links.swap(other_of(partial_values), core=1)

    vectors = (
        attention_gain,
        attention_shift,
        query_bias,
        value_bias,
        output_bias,
        feed_gain,
        feed_shift,
        down_bias,
        up_bias,
    )
    lengths = [member.shape[0] for member in vectors]
    table = links.gather_vectors(jnp.concatenate(vectors)).astype(F32)
    wholes, at = [], 0
    for length in lengths:
        wholes.append(table[:, at : at + length])
        at += length

    def whole(index):
        return wholes[index].reshape(1, -1)

    def core_part(index):
        return pick(wholes[index].reshape(chips, 2, -1), core, 1).reshape(1, -1)

    input_part = links.gather(links.halves(input_weight, 3))
    output_part = links.gather(output_weight)
    up_part = links.gather(links.halves(up_weight, 1))
    down_part = links.gather(down_weight)

    inputs = tokens.reshape(own_rows, width).astype(F32)
    unit_one, inverse_one = normalize(inputs)
    normed = (unit_one * whole(0) + whole(1)).astype(LOW)
    chip_normed = pair_rows(normed)
    tail = chip_normed.reshape(micro, 2 * tok_rows, width)[:, 2 * tok_rows - BLOCK :]
    halo = links.shift(tail.reshape(micro * BLOCK, width), 1)
    all_normed = jnp.concatenate([chip_normed, halo], axis=0)
    down_low = pair_rows(cotangent.reshape(own_rows, width))
    first = chip * 2 * tok_rows
    starts = jnp.stack(
        [
            sequence_starts(seq_lengths[m, 0], dealing[m, 0], first, 2 * tok_rows)
            for m in range(micro)
        ]
    )
    block_first = first + jnp.arange(2 * tok_rows, dtype=jnp.int32) // BLOCK * BLOCK - BLOCK
    starts = (starts - block_first[None, :]).reshape(2 * own_rows, 1)

    half = width // 2
    bias = jnp.concatenate([core_part(2), jnp.zeros((1, half), F32), core_part(3)], axis=1)
    mixed = (dot(all_normed, input_part) + bias).astype(LOW)
    branch = attention(mixed, starts, blocks)
    middle = inputs + pair_sum(dot(branch, output_part)) + whole(4)
    unit_two, inverse_two = normalize(middle)
    normed_two = pair_rows((unit_two * whole(5) + whole(6)).astype(LOW))
    hidden = dot(normed_two, up_part) + core_part(8)
    activated, gelu_back = jax.vjp(gelu_tanh, hidden)
    activated = activated.astype(LOW)
    down_grad = links.reduce(rows_dot(activated, down_low)).astype(F32)
    result = middle + pair_sum(dot(activated, down_part)) + whole(7)

    upstream = cotangent.reshape(own_rows, width).astype(F32)
    (hidden_grad,) = gelu_back(back_dot(down_low, down_part))
    hidden_low = hidden_grad.astype(LOW)
    up_grad = links.unhalves(links.reduce(rows_dot(normed_two, hidden_low)), 1).astype(F32)
    upper_two = pair_sum(back_dot(hidden_low, up_part))
    middle_grad = upstream + normalize_back(upper_two, whole(5), unit_two, inverse_two)
    output_own = middle_grad.astype(LOW)
    output_low = pair_rows(output_own)
    output_grad = links.reduce(rows_dot(branch, output_low)).astype(F32)
    attended = back_dot(output_low, output_part).astype(LOW)
    mixed_grad = attention_back(mixed, starts, attended, blocks)
    input_weight_grad = links.unhalves(links.reduce(rows_dot(all_normed, mixed_grad)), 3).astype(F32)
    back_halo = links.shift(mixed_grad[2 * own_rows :, half:], -1)
    body = mixed_grad[: 2 * own_rows].reshape(micro, 2 * tok_rows, 3 * half)
    tail_grad = body[:, 2 * tok_rows - BLOCK :, half:].astype(F32) + back_halo.reshape(
        micro, BLOCK, width
    ).astype(F32)
    body = body.at[:, 2 * tok_rows - BLOCK :, half:].set(tail_grad.astype(LOW))
    upper_one = pair_sum(back_dot(body.reshape(2 * own_rows, 3 * half), input_part))
    input_grad = middle_grad + normalize_back(upper_one, whole(0), unit_one, inverse_one)

    def by_shard(values):
        return values.reshape(shard_count, -1)

    def by_core_shard(values):
        spread = values.reshape(chips, 1, -1)
        mask = jnp.arange(2, dtype=jnp.int32)[None, :, None] == core
        return jnp.where(mask, spread, 0.0).reshape(shard_count, -1)

    def column_sum(values):
        return jnp.sum(values.astype(F32), axis=0)

    packed = jnp.concatenate(
        [
            by_shard(column_sum(upper_one * unit_one)),
            by_shard(column_sum(upper_one)),
            by_core_shard(column_sum(mixed_grad[:, :half])),
            by_core_shard(column_sum(mixed_grad[:, width:])),
            by_shard(column_sum(output_own)),
            by_shard(column_sum(upper_two * unit_two)),
            by_shard(column_sum(upper_two)),
            by_shard(column_sum(upstream)),
            by_core_shard(column_sum(hidden_low)),
        ],
        axis=1,
    )
    sums = links.reduce_vectors(packed)
    vector_grads, at = [], 0
    for length in lengths:
        vector_grads.append(sums[at : at + length])
        at += length
    return (
        result.astype(LOW).reshape(tokens.shape),
        input_grad.astype(LOW).reshape(tokens.shape),
        vector_grads[0],
        vector_grads[1],
        input_weight_grad,
        vector_grads[2],
        vector_grads[3],
        output_grad,
        vector_grads[4],
        vector_grads[5],
        vector_grads[6],
        up_grad,
        vector_grads[8],
        down_grad,
        vector_grads[7],
    )


def finish_kernel(chips, parts, *refs):
    sums, vectors = refs[parts], refs[2 * parts + 1 :]
    for source, target in zip(refs[:parts], refs[parts + 1 : 2 * parts + 1]):
        target[...] = source[...].astype(target.dtype)

    def own_vectors():
        shard = lax.axis_index("shard")
        chip = shard // 2
        own = pl.ds(pl.multiple_of(shard * BLOCK, BLOCK), BLOCK)
        for row in range(6):
            vectors[row][...] = sums[row : row + 1, own]
        half = sums.shape[1] // 2
        for side in range(2):
            place = pl.multiple_of(side * half + chip * BLOCK, BLOCK)
            vectors[6 + side][...] = sums[8:9, pl.ds(place, BLOCK)]
        length = vectors[8].shape[1]
        each = sums.shape[1] // length
        for at in range(chips):

            def copy():
                row, place = 9 + at // each, at % each * length
                vectors[8][...] = sums[row : row + 1, place : place + length]

            pl.when(chip == at)(copy)

    pl.when(pl.program_id(0) == 0)(own_vectors)


def finish(chips, grads, sums, rows):
    steps = 4
    members = list(grads) + list(rows)
    specs = [
        pl.BlockSpec((member.shape[0] // steps, member.shape[1]), lambda step: (step, 0))
        for member in members
    ]
    lengths = [BLOCK] * 8 + [grads[2].shape[1] // (2 * chips)]
    out_shapes = (
        [jax.ShapeDtypeStruct(member.shape, F32) for member in grads]
        + [jax.ShapeDtypeStruct(member.shape, LOW) for member in rows]
        + [jax.ShapeDtypeStruct((1, length), F32) for length in lengths]
    )
    small = [pl.BlockSpec((1, length), lambda step: (0, 0)) for length in lengths]
    return pl.pallas_call(
        partial(finish_kernel, chips, len(members)),
        grid=(steps,),
        out_shape=tuple(out_shapes),
        in_specs=specs + [pl.BlockSpec(sums.shape, lambda step: (0, 0))],
        out_specs=tuple(specs + small),
        compiler_params=pltpu.CompilerParams(vmem_limit_bytes=67_000_000),
    )(*members, sums)


def shards(
    chips,
    reps,
    tokens,
    cotangent,
    seq_lengths,
    dealing,
    *weights,
):
    if chips != 4 or reps != 4:
        return shards_general(chips, reps, tokens, cotangent, seq_lengths, dealing, *weights)
    (
        attention_gain,
        attention_shift,
        input_weight,
        query_bias,
        value_bias,
        output_weight,
        output_bias,
        feed_gain,
        feed_shift,
        up_weight,
        up_bias,
        down_weight,
        down_bias,
    ) = weights
    shard = lax.axis_index("shard")
    chip = shard // 2
    micro, tok_rows, width = tokens.shape
    shard_count, half = 2 * chips, width // 2
    own_rows = micro * tok_rows
    blocks = 2 * tok_rows // BLOCK
    hidden_half = up_weight.shape[1] // 2

    members = [
        attention_gain,
        attention_shift,
        query_bias,
        value_bias,
        output_bias,
        feed_gain,
        feed_shift,
        down_bias,
    ] + [up_bias[at : at + BLOCK] for at in range(0, up_bias.shape[0], BLOCK)]
    line = lax.broadcasted_iota(jnp.int32, (VECTOR_ROWS, BLOCK), 0)
    packed = jnp.zeros((VECTOR_ROWS, BLOCK), LOW)
    for index, member in enumerate(members):
        packed = jnp.where(line == index, member[None, :], packed)
    first = chip * 2 * tok_rows
    starts = jnp.stack(
        [
            sequence_starts(seq_lengths[m, 0], dealing[m, 0], first, 2 * tok_rows)
            for m in range(micro)
        ]
    )
    block_first = first + jnp.arange(2 * tok_rows, dtype=jnp.int32) // BLOCK * BLOCK - BLOCK
    starts = (starts - block_first[None, :]).reshape(2 * own_rows, 1)
    own_tokens = tokens.reshape(own_rows, width)
    (
        input_part,
        output_part,
        up_part,
        down_part,
        mixed,
        branch,
        all_normed,
        normed_two,
        activated,
        hidden,
        middle,
        down_low,
        vectors,
    ) = forward(
        chips,
        micro,
        blocks,
        (3 * chips, None, chips, None),
        packed,
        (input_weight, output_weight, up_weight, down_weight),
        own_tokens,
        cotangent.reshape(own_rows, width),
        starts,
    )
    results = backward(
        chips,
        micro,
        blocks,
        (width // shard_count, None, hidden_half // chips, None),
        (
            activated,
            down_low,
            hidden,
            normed_two,
            up_part,
            output_part,
            input_part,
            down_part,
            branch,
            mixed,
            all_normed,
            middle,
            own_tokens,
        ),
        starts,
        vectors,
    )
    flat = [member.reshape(-1, member.shape[2]) for member in results[:4]]
    finished = finish(chips, flat, results[4], results[5:])
    vector_grads = [member.reshape(-1) for member in finished[6:]]
    return (
        finished[5].reshape(tokens.shape),
        finished[4].reshape(tokens.shape),
        vector_grads[0],
        vector_grads[1],
        finished[0],
        vector_grads[6],
        vector_grads[7],
        finished[1],
        vector_grads[2],
        vector_grads[3],
        vector_grads[4],
        finished[2],
        vector_grads[8],
        finished[3],
        vector_grads[5],
    )


def solution(mesh):
    rows_spec = P(None, ("shard", "rep"), None)
    vector, matrix = P("shard"), P("shard", None)
    weight_specs = (
        vector,
        vector,
        matrix,
        vector,
        vector,
        matrix,
        vector,
        vector,
        vector,
        matrix,
        vector,
        matrix,
        vector,
    )
    return jax.shard_map(
        partial(shards, mesh.shape["shard"] // 2, mesh.shape["rep"]),
        mesh=mesh,
        in_specs=(rows_spec, rows_spec, P(None, "rep", None, None), P(None, "rep", None))
        + weight_specs,
        out_specs=(rows_spec, rows_spec) + weight_specs,
        check_vma=False,
    )
```

```python
from functools import partial

import jax
import jax.numpy as jnp
from jax import lax
from jax.experimental import pallas as pl
from jax.experimental.pallas import tpu as pltpu
from jax.sharding import PartitionSpec as P

HD = 64
BLOCK = 128
EPSILON = 1e-05
MASKED = -1e30
AXES = ("shard", "rep")
F32 = jnp.float32
LOW = jnp.bfloat16


def dot(left, right):
    return jnp.dot(left, right, preferred_element_type=F32)


def rows_dot(left, right):
    return lax.dot_general(left, right, (((0,), (0,)), ((), ())), preferred_element_type=F32)


def back_dot(left, right):
    return lax.dot_general(left, right, (((1,), (1,)), ((), ())), preferred_element_type=F32)


def pick(stacked, index, axis=0):
    return lax.dynamic_index_in_dim(stacked, index, axis, keepdims=False)


def normalize(values):
    center = values - jnp.mean(values, axis=-1, keepdims=True)
    inverse = lax.rsqrt(jnp.mean(center * center, axis=-1, keepdims=True) + EPSILON)
    return center * inverse, inverse


def normalize_back(upper, gain, unit, inverse):
    scaled = upper * gain
    mean_scaled = jnp.mean(scaled, axis=-1, keepdims=True)
    mean_product = jnp.mean(scaled * unit, axis=-1, keepdims=True)
    return inverse * (scaled - mean_scaled - unit * mean_product)


def gelu_tanh(values):
    return jax.nn.gelu(values, approximate=True)


def sequence_starts(seq_lengths, dealing, first, rows):
    total = dealing.shape[0]
    numbers = jnp.arange(total, dtype=jnp.int32)
    matched = (dealing[:, None] == numbers[None, :]).astype(jnp.int32)
    packed_length = jnp.sum(matched * seq_lengths.reshape(total)[None, :], axis=1)
    before = (numbers[None, :] < numbers[:, None]).astype(jnp.int32)
    packed_start = jnp.sum(before * packed_length[None, :], axis=1)
    own = first + jnp.arange(rows, dtype=jnp.int32)
    return jnp.max(
        jnp.where(packed_start[None, :] <= own[:, None], packed_start[None, :], 0), axis=1
    )


def window(ref, row, previous, column):
    return jnp.concatenate(
        [
            ref[pl.ds(previous, BLOCK), column : column + BLOCK],
            ref[pl.ds(row, BLOCK), column : column + BLOCK],
        ],
        axis=0,
    )


def block_rows(step, blocks, body_rows):
    micro, block = step // blocks, step % blocks
    row = pl.multiple_of(step * BLOCK, BLOCK)
    previous = jnp.where(block == 0, body_rows + micro * BLOCK, row - BLOCK)
    return row, pl.multiple_of(previous, BLOCK)


def soft_weights(query_half, keys, allowed):
    scores = back_dot(query_half, keys) * float(HD) ** (-0.5)
    scores = jnp.where(allowed, scores, MASKED)
    top = jnp.max(scores, axis=1, keepdims=True)
    powers = jnp.exp(scores - top)
    return powers / jnp.sum(powers, axis=1, keepdims=True)


def allowed_keys(start_ref, row):
    places = lax.broadcasted_iota(jnp.int32, (BLOCK, 2 * BLOCK), 1)
    lines = lax.broadcasted_iota(jnp.int32, (BLOCK, 2 * BLOCK), 0)
    return (places >= start_ref[pl.ds(row, BLOCK), :]) & (places <= lines + BLOCK)


def attention_kernel(blocks, width, mixed_ref, start_ref, branch_ref):
    body_rows = branch_ref.shape[0]
    left = lax.broadcasted_iota(jnp.int32, (BLOCK, BLOCK), 1) < HD

    def step_body(step, _):
        row, previous = block_rows(step, blocks, body_rows)
        allowed = allowed_keys(start_ref, row)
        for column in range(0, width, BLOCK):
            queries = mixed_ref[pl.ds(row, BLOCK), column : column + BLOCK]
            keys = window(mixed_ref, row, previous, width + column)
            values = window(mixed_ref, row, previous, 2 * width + column)
            parts = []
            for half in (left, ~left):
                soft = soft_weights(jnp.where(half, queries, 0), keys, allowed)
                parts.append(dot(soft.astype(LOW), values))
            branch_ref[pl.ds(row, BLOCK), column : column + BLOCK] = jnp.where(
                left, parts[0], parts[1]
            ).astype(LOW)
        return 0

    lax.fori_loop(0, body_rows // BLOCK, step_body, 0)


def attention_back_kernel(blocks, width, mixed_ref, start_ref, upper_ref, grad_ref, sums_ref):
    body_rows = upper_ref.shape[0]
    left = lax.broadcasted_iota(jnp.int32, (BLOCK, BLOCK), 1) < HD
    left_tall = lax.broadcasted_iota(jnp.int32, (2 * BLOCK, BLOCK), 1) < HD
    scale = float(HD) ** (-0.5)
    sums_ref[...] = jnp.zeros_like(sums_ref)

    def step_body(step, _):
        row, previous = block_rows(step, blocks, body_rows)
        allowed = allowed_keys(start_ref, row)
        for column in range(0, width, BLOCK):
            queries = mixed_ref[pl.ds(row, BLOCK), column : column + BLOCK]
            keys = window(mixed_ref, row, previous, width + column)
            values = window(mixed_ref, row, previous, 2 * width + column)
            upper = upper_ref[pl.ds(row, BLOCK), column : column + BLOCK]
            parts = []
            for half in (left, ~left):
                soft = soft_weights(jnp.where(half, queries, 0), keys, allowed)
                soft_grad = back_dot(jnp.where(half, upper, 0), values)
                total = jnp.sum(soft * soft_grad, axis=1, keepdims=True)
                score_low = (soft * (soft_grad - total)).astype(LOW)
                parts.append(
                    (
                        dot(score_low, keys) * scale,
                        rows_dot(score_low, queries) * scale,
                        rows_dot(soft.astype(LOW), upper),
                    )
                )
            grad_ref[pl.ds(row, BLOCK), column : column + BLOCK] = jnp.where(
                left, parts[0][0], parts[1][0]
            ).astype(LOW)
            for slot in (1, 2):
                joined = jnp.where(left_tall, parts[0][slot], parts[1][slot])
                place = (slot - 1) * width + column
                sums_ref[pl.ds(previous, BLOCK), place : place + BLOCK] += joined[:BLOCK]
                sums_ref[pl.ds(row, BLOCK), place : place + BLOCK] += joined[BLOCK:]
        return 0

    lax.fori_loop(0, body_rows // BLOCK, step_body, 0)
    grad_ref[:, width:] = sums_ref[...].astype(LOW)
    grad_ref[body_rows:, :width] = jnp.zeros((grad_ref.shape[0] - body_rows, width), LOW)


def attention(mixed, starts, blocks):
    width = mixed.shape[1] // 3
    rows = starts.shape[0]
    vmem = pl.BlockSpec(memory_space=pltpu.VMEM)
    return pl.pallas_call(
        partial(attention_kernel, blocks, width),
        out_shape=jax.ShapeDtypeStruct((rows, width), LOW),
        in_specs=[vmem, vmem],
        out_specs=vmem,
        cost_estimate=pl.CostEstimate(
            flops=rows * width * BLOCK * 16, bytes_accessed=8 << 20, transcendentals=0
        ),
        compiler_params=pltpu.CompilerParams(vmem_limit_bytes=40 << 20),
    )(mixed, starts)


def attention_back(mixed, starts, upper, blocks):
    width = mixed.shape[1] // 3
    rows = starts.shape[0]
    vmem = pl.BlockSpec(memory_space=pltpu.VMEM)
    return pl.pallas_call(
        partial(attention_back_kernel, blocks, width),
        out_shape=jax.ShapeDtypeStruct(mixed.shape, LOW),
        in_specs=[vmem, vmem, vmem],
        out_specs=vmem,
        scratch_shapes=[pltpu.VMEM((mixed.shape[0], 2 * width), F32)],
        cost_estimate=pl.CostEstimate(
            flops=rows * width * BLOCK * 40, bytes_accessed=16 << 20, transcendentals=0
        ),
        compiler_params=pltpu.CompilerParams(vmem_limit_bytes=40 << 20),
    )(mixed, starts, upper)


class Links:
    def __init__(self, chips, reps):
        self.chips, self.reps = chips, reps
        shard = lax.axis_index("shard")
        self.chip, self.core, self.rep = shard // 2, shard % 2, lax.axis_index("rep")

    def flat(self, chip, core, rep):
        return (chip * 2 + core) * self.reps + rep

    def swap(self, values, chip=0, core=0, rep=0):
        pairs = [
            (self.flat(a, b, d), self.flat(a ^ chip, b ^ core, d ^ rep))
            for a in range(self.chips)
            for b in range(2)
            for d in range(self.reps)
        ]
        return lax.ppermute(values, AXES, pairs)

    def shift(self, values, by):
        pairs = [
            (self.flat(a, b, d), self.flat(a + by, b, d))
            for a in range(self.chips)
            if 0 <= a + by < self.chips
            for b in range(2)
            for d in range(self.reps)
        ]
        return lax.ppermute(values, AXES, pairs)

    def by_core(self, own, other, axis):
        first = jnp.where(self.core == 0, own, other)
        second = jnp.where(self.core == 0, other, own)
        return jnp.concatenate([first, second], axis=axis)

    def halves(self, matrix, parts):
        rows, columns = matrix.shape
        blocks = self.chips * parts
        view = matrix.reshape(rows, blocks, 2, columns // (2 * blocks))
        keep = pick(view, self.core, 2).reshape(rows, columns // 2)
        give = pick(view, 1 - self.core, 2).reshape(rows, columns // 2)
        return self.by_core(keep, self.swap(give, core=1), 0)

    def gather(self, chip_rows):
        rows, columns = chip_rows.shape
        quarter = rows // self.reps
        quarters = chip_rows.reshape(self.reps, quarter, columns)
        piece = pick(quarters, self.rep)
        pieces = jnp.stack([self.swap(piece, chip=j) for j in range(1, self.chips)])
        found = [pieces] + [None] * (self.reps - 1)
        if self.reps == 4:
            half = quarter // 2
            found[1] = self.swap(pieces, rep=1)
            found[2] = self.swap(pieces, rep=2)
            upper = self.swap(found[1][:, :half], rep=2)
            lower = self.swap(found[2][:, half:], rep=1)
            found[3] = jnp.concatenate([upper, lower], axis=1)
        else:
            for j in range(1, self.reps):
                found[j] = self.swap(pieces, rep=j)
        stacked = jnp.stack(
            [
                jnp.concatenate([pick(quarters, self.rep ^ j)[None], found[j]], axis=0)
                for j in range(self.reps)
            ]
        )
        ordered = []
        for chip in range(self.chips):
            for rep in range(self.reps):
                at = (self.rep ^ rep, self.chip ^ chip, 0, 0)
                ordered.append(
                    lax.dynamic_slice(stacked, at, (1, 1, quarter, columns)).reshape(
                        quarter, columns
                    )
                )
        return jnp.concatenate(ordered, axis=0)

    def reduce(self, grads):
        chips, reps = self.chips, self.reps
        rows, columns = grads.shape
        quarter = rows // (chips * reps)
        view = grads.astype(LOW).reshape(chips, reps, quarter, columns)
        mine = pick(view, self.rep, 1).astype(F32)
        if reps == 4:
            half = quarter // 2
            across = pick(view, self.rep ^ 3, 1)
            upper = self.swap(across[:, :half], rep=1)
            lower = self.swap(across[:, half:], rep=2)
            to_x = pick(view, self.rep ^ 1, 1)
            to_y = pick(view, self.rep ^ 2, 1)
            to_x = jnp.concatenate(
                [to_x[:, :half], (to_x[:, half:].astype(F32) + lower.astype(F32)).astype(LOW)],
                axis=1,
            )
            to_y = jnp.concatenate(
                [(to_y[:, :half].astype(F32) + upper.astype(F32)).astype(LOW), to_y[:, half:]],
                axis=1,
            )
            mine = (
                mine + self.swap(to_x, rep=1).astype(F32) + self.swap(to_y, rep=2).astype(F32)
            )
        else:
            for j in range(1, reps):
                mine = mine + self.swap(pick(view, self.rep ^ j, 1), rep=j).astype(F32)
        total = pick(mine, self.chip)
        sends = mine.astype(LOW)
        for j in range(1, chips):
            total = total + self.swap(pick(sends, self.chip ^ j), chip=j).astype(F32)
        return self.spread(total.astype(LOW))

    def spread(self, own):
        if self.reps == 4:
            half = own.shape[0] // 2
            from_x = self.swap(own, rep=1)
            from_y = self.swap(own, rep=2)
            upper = self.swap(from_x[:half], rep=2)
            lower = self.swap(from_y[half:], rep=1)
            found = [own, from_x, from_y, jnp.concatenate([upper, lower], axis=0)]
        else:
            found = [own] + [self.swap(own, rep=j) for j in range(1, self.reps)]
        stacked = jnp.stack(found)
        return jnp.concatenate([pick(stacked, self.rep ^ j) for j in range(self.reps)], axis=0)

    def unhalves(self, chip_rows, parts):
        rows, columns = chip_rows.shape
        view = chip_rows.reshape(2, rows // 2, columns)
        blocks = self.chips * parts
        keep = pick(view, self.core).reshape(rows // 2, blocks, 1, columns // blocks)
        came = self.swap(pick(view, 1 - self.core), core=1)
        came = came.reshape(rows // 2, blocks, 1, columns // blocks)
        return self.by_core(keep, came, 2).reshape(rows // 2, 2 * columns)

    def gather_vectors(self, packed):
        pair = self.by_core(packed[None], self.swap(packed, core=1)[None], 0)
        found = jnp.stack([pair] + [self.swap(pair, chip=j) for j in range(1, self.chips)])
        ordered = [pick(found, self.chip ^ j) for j in range(self.chips)]
        return jnp.concatenate(ordered, axis=0)

    def reduce_vectors(self, partial_sums):
        chips, reps = self.chips, self.reps
        view = partial_sums.reshape(chips, 2, -1)
        total = None
        for a in range(chips):
            for b in range(2):
                row = pick(pick(view, self.chip ^ a), self.core ^ b)
                row = row if a == b == 0 else self.swap(row, chip=a, core=b)
                total = row if total is None else total + row
        terms = [total] + [self.swap(total, rep=j) for j in range(1, reps)]
        while len(terms) > 1:
            terms = [terms[i] + terms[i + 1] for i in range(0, len(terms), 2)]
        return terms[0]

class Copies:
    def __init__(self, send, recv, links):
        self.send, self.recv, self.links = send, recv, links
        self.places, self.started = {}, []

    def make(self, name, source, target, device):
        place = self.places.setdefault(name, len(self.places))
        return pltpu.make_async_remote_copy(
            src_ref=source,
            dst_ref=target,
            send_sem=self.send.at[place],
            recv_sem=self.recv.at[place],
            device_id=device,
            device_id_type=pl.DeviceIdType.MESH,
        )

    def start(self, name, source, target, device, when=None):
        copy = self.make(name, source, target, device)
        run_when(when, copy.start)
        self.started.append((name, when, copy))

    def arrived(self, name, target, when=None):
        copy = self.make(name, target, target, self.links.other(x=1))
        run_when(when, copy.wait_recv)

    def sent(self, name):
        for item in [item for item in self.started if item[0] == name]:
            run_when(item[1], item[2].wait_send)
            self.started.remove(item)

    def finish(self):
        for _, when, copy in self.started:
            run_when(when, copy.wait_send)


def run_when(when, body):
    if when is None:
        body()
    else:
        pl.when(when)(body)


class Place:
    def __init__(self, chips):
        shard = lax.axis_index("shard")
        self.chips, self.shard = chips, shard
        self.chip, self.core, self.rep = shard // 2, lax.rem(shard, 2), lax.axis_index("rep")

    def flipped(self, bits):
        x, y = lax.rem(self.rep, 2), self.rep // 2
        x = 1 - x if bits & 1 else x
        y = 1 - y if bits & 2 else y
        return y * 2 + x

    def other(self, x=0, y=0, core=0, chip=None):
        chip = self.chip if chip is None else chip
        side = 1 - self.core if core else self.core
        return {"shard": chip * 2 + side, "rep": self.flipped(x + 2 * y)}

    def shard_at(self, step):
        return lax.rem(self.shard + step, 2 * self.chips)

    def greet(self, barrier_devices):
        barrier = pltpu.get_barrier_semaphore()
        for device in barrier_devices:
            pl.semaphore_signal(barrier, 1, device_id=device, device_id_type=pl.DeviceIdType.MESH)
        pl.semaphore_wait(barrier, len(barrier_devices))

    def neighbours(self):
        shards = [
            {"shard": self.shard_at(step), "rep": self.rep} for step in range(1, 2 * self.chips)
        ]
        return shards + [self.other(x=1), self.other(y=1)]


def forward_kernel(chips, micro, blocks, splits, *refs):
    vec_in, in_in, out_in, up_in, down_in, tokens_in, cotangent_in, starts = refs[:8]
    (
        in_out,
        out_out,
        up_out,
        down_out,
        mixed_out,
        branch_out,
        all_normed_out,
        normed_two_out,
        activated_out,
        hidden_out,
        middle_out,
        low_out,
        vectors,
    ) = refs[8:21]
    (
        in_whole,
        out_whole,
        up_whole,
        table,
        mixed_bias,
        up_bias,
        tokens,
        low,
        all_normed,
        mixed,
        branch,
        give,
        came,
        middle,
        normed_two,
        activated,
        hidden,
        send,
        recv,
        local,
    ) = refs[21:]
    shards_in = (in_in, out_in, up_in, down_in)
    wholes = (in_whole, out_whole, up_whole, down_out)
    at = Place(chips)
    core = at.core
    copies = Copies(send, recv, at)
    all_rows, width = all_normed.shape
    rows = low.shape[0]
    own_rows, micro_rows = rows // 2, rows // micro
    own_micro = micro_rows // 2
    part_width = branch.shape[1]
    moved, staged = [], []

    down_stage = activated.at[pl.ds(0, down_in.shape[0]), pl.ds(0, width)]

    def keep(source, target):
        copy = pltpu.make_async_copy(source, target, local.at[len(moved)])
        copy.start()
        moved.append(copy)
        return copy

    def own_place(row_side, step):
        return pl.ds(pl.multiple_of(step * micro_rows + row_side * own_micro, own_micro), own_micro)

    load_tokens = keep(tokens_in, tokens)
    at.greet(at.neighbours())
    partner = at.other(core=1)
    load_table = keep(vec_in, table.at[at.shard])
    for step in range(1, 2 * chips):
        copies.start(
            ("vec", step), vec_in, table.at[at.shard], {"shard": at.shard_at(step), "rep": at.rep}
        )
    kept = []
    for index, (source, whole, count) in enumerate(zip(shards_in, wholes, splits)):
        shard_rows = source.shape[0]
        first = len(moved)
        if index == 3:
            keep(source, down_stage)
        elif count is None:
            place = pl.ds(pl.multiple_of(at.chip * shard_rows, shard_rows), shard_rows)
            keep(source, whole.at[place])
        else:
            piece_width = source.shape[1] // (2 * count)
            place = pl.ds(pl.multiple_of(at.shard * shard_rows, shard_rows), shard_rows)
            for block in range(count):
                columns = pl.ds(block * piece_width, piece_width)

                def side(which):
                    start = pl.multiple_of((2 * block + which) * piece_width, piece_width)
                    return pl.ds(start, piece_width)

                copies.start(
                    ("pair", index, block),
                    source.at[:, side(1 - core)],
                    whole.at[place, columns],
                    partner,
                )
                keep(source.at[:, side(core)], whole.at[place, columns])
        kept.append(moved[first:])
    load_low = []
    for step in range(micro):
        source = cotangent_in.at[pl.ds(step * own_micro, own_micro)]
        load_low.append(keep(source, low.at[own_place(core, step)]))
        copies.start(("low", step), source, low.at[own_place(core, step)], partner)

    def piece(index, chip, bits=None, side=None):
        whole = wholes[index]
        chip_rows = whole.shape[0] // chips
        size = chip_rows // 4
        start = chip * chip_rows + (at.rep if bits is None else at.flipped(bits)) * size
        if side is not None:
            size = size // 2
            start = start + side * size
        return whole.at[pl.ds(pl.multiple_of(start, size), size)]

    ways = (("up", 1), ("down", -1))

    def neighbour(step):
        return at.other(chip=jnp.clip(at.chip + step, 0, chips - 1))

    def can_send(step):
        return at.chip < chips - 1 if step > 0 else at.chip > 0

    def origins(index, distance):
        for name, step in ways:
            when = at.chip >= distance if step > 0 else at.chip + distance < chips
            chip = jnp.clip(at.chip - step * distance, 0, chips - 1)
            yield (name, index, distance), step, when, chip

    def open_z(index):
        for copy in kept[index]:
            copy.wait()
        if splits[index] is not None:
            shard_rows = shards_in[index].shape[0]
            piece_width = shards_in[index].shape[1] // (2 * splits[index])
            place = (at.chip * 2 + 1 - core) * shard_rows
            place = pl.ds(pl.multiple_of(place, shard_rows), shard_rows)
            for block in range(splits[index]):
                columns = pl.ds(block * piece_width, piece_width)
                copies.arrived(("pair", index, block), wholes[index].at[place, columns])
        mine = target = piece(index, at.chip)
        if index == 3:
            place = pl.ds(pl.multiple_of(at.chip * down_in.shape[0], down_in.shape[0]), down_in.shape[0])
            staged.append(keep(down_stage, down_out.at[place]))
            quarter = down_in.shape[0] // 4
            mine = down_in.at[pl.ds(pl.multiple_of(at.rep * quarter, quarter), quarter)]
        for name, step in ways:
            copies.start((name, index, 1), mine, target, neighbour(step), can_send(step))

    def pass_on(index, distance):
        for key, step, when, chip in origins(index, distance):
            found = piece(index, chip)
            copies.arrived(key, found, when)
            if distance < chips - 1:
                copies.start(
                    (key[0], index, distance + 1),
                    found,
                    found,
                    neighbour(step),
                    when & can_send(step),
                )
            copies.start(("x",) + key, found, found, at.other(x=1), when)
            copies.start(("y",) + key, found, found, at.other(y=1), when)

    def across(index, distance):
        for key, step, when, chip in origins(index, distance):
            copies.arrived(("x",) + key, piece(index, chip, 1), when)
            upper = piece(index, chip, 1, 0)
            copies.start(("xy",) + key, upper, upper, at.other(y=1), when)
            copies.arrived(("y",) + key, piece(index, chip, 2), when)
            lower = piece(index, chip, 2, 1)
            copies.start(("yx",) + key, lower, lower, at.other(x=1), when)

    def close(index):
        for distance in range(1, chips):
            for key, step, when, chip in origins(index, distance):
                copies.arrived(("xy",) + key, piece(index, chip, 3, 0), when)
                copies.arrived(("yx",) + key, piece(index, chip, 3, 1), when)

    lines = 32

    def own_lines(step):
        place = pl.ds(pl.multiple_of(step * lines, lines), lines)
        chip_row = step // (own_micro // lines) * micro_rows + core * own_micro
        chip_row = chip_row + lax.rem(step, own_micro // lines) * lines
        return place, pl.ds(pl.multiple_of(chip_row, lines), lines)

    def spread_vectors():
        load_table.wait()
        for step in range(1, 2 * chips):
            copies.arrived(("vec", step), table.at[at.shard_at(2 * chips - step)])
        for shard in range(2 * chips):
            vectors[:, shard * BLOCK : (shard + 1) * BLOCK] = table[shard].astype(F32)
        mixed_bias[...] = jnp.zeros_like(mixed_bias)
        each = up_bias.shape[1] // (chips * BLOCK)
        for chip in range(chips):
            member = table[2 * chip + core].astype(F32)
            columns = pl.ds(chip * BLOCK, BLOCK)
            mixed_bias[:, columns] = member[2:3, :]
            mixed_bias[:, pl.ds(2 * part_width + chip * BLOCK, BLOCK)] = member[3:4, :]
            for j in range(each):
                up_bias[:, pl.ds((chip * each + j) * BLOCK, BLOCK)] = member[8 + j : 9 + j, :]

    def halo_place(step):
        return pl.ds(rows + step * BLOCK, BLOCK)

    def first_norm():
        def body(step):
            place, chip_place = own_lines(step)
            unit, _ = normalize(tokens[place, :].astype(F32))
            all_normed[chip_place, :] = (unit * vectors[0:1, :] + vectors[1:2, :]).astype(LOW)

        loop(own_rows // lines, body)
        for step in range(micro):
            mine = all_normed.at[own_place(core, step)]
            copies.start(("normed", step), mine, mine, partner)
            tail = all_normed.at[pl.ds((step + 1) * micro_rows - BLOCK, BLOCK)]
            copies.start(
                ("halo", step),
                tail,
                all_normed.at[halo_place(step)],
                neighbour(1),
                can_send(1) & (core == 1),
            )

        def clear():
            all_normed[rows:, :] = jnp.zeros((all_rows - rows, width), LOW)

        pl.when(at.chip == 0)(clear)

    def halo_on():
        for step in range(micro):
            found = all_normed.at[halo_place(step)]
            received = (at.chip > 0) & (core == 1)
            copies.arrived(("halo", step), found, received)
            copies.start(("halo on", step), found, found, partner, received)

    def all_normed_ready():
        for step in range(micro):
            copies.arrived(("normed", step), all_normed.at[own_place(1 - core, step)])
            copies.arrived(
                ("halo on", step), all_normed.at[halo_place(step)], (at.chip > 0) & (core == 0)
            )

    tile = 256

    def mix():
        def body(step):
            columns = pl.ds(pl.multiple_of(step * tile, tile), tile)
            result = dot(all_normed[...], in_whole[:, columns]) + mixed_bias[:, columns]
            mixed[:, columns] = result.astype(LOW)

        loop(3 * part_width // tile, body)

    left = lax.broadcasted_iota(jnp.int32, (BLOCK, BLOCK), 1) < HD

    def attend(column):
        def body(step):
            row, previous = block_rows(step, blocks, rows)
            allowed = allowed_keys(starts, row)
            queries = mixed[pl.ds(row, BLOCK), column : column + BLOCK]
            keys = window(mixed, row, previous, part_width + column)
            values = window(mixed, row, previous, 2 * part_width + column)
            parts = []
            for side in (left, ~left):
                soft = soft_weights(jnp.where(side, queries, 0), keys, allowed)
                parts.append(dot(soft.astype(LOW), values))
            branch[pl.ds(row, BLOCK), column : column + BLOCK] = jnp.where(
                left, parts[0], parts[1]
            ).astype(LOW)

        loop(rows // BLOCK, body)

    def project(side, target):
        for step in range(micro):
            place = pl.ds(step * own_micro, own_micro)
            left_rows = branch[own_place(side, step), :]

            def body(part):
                columns = pl.ds(pl.multiple_of(part * tile, tile), tile)
                target[place, columns] = dot(left_rows, out_whole[:, columns])

            loop(width // tile, body)

    def second_norm():
        copies.arrived(("partial",), came)

        def body(step):
            place, chip_place = own_lines(step)
            total = tokens[place, :].astype(F32) + (middle[place, :] + came[place, :])
            total = total + vectors[4:5, :]
            middle[place, :] = total
            unit, _ = normalize(total)
            normed_two[chip_place, :] = (unit * vectors[5:6, :] + vectors[6:7, :]).astype(LOW)

        loop(own_rows // lines, body)
        for step in range(micro):
            mine = normed_two.at[own_place(core, step)]
            copies.start(("normed two", step), mine, mine, partner)

    def feed(first, last):
        def body(step):
            columns = pl.ds(pl.multiple_of((first + step) * tile, tile), tile)
            result = dot(normed_two[...], up_whole[:, columns]) + up_bias[:, columns]
            hidden[:, columns] = result
            activated[:, columns] = gelu_tanh(result).astype(LOW)

        loop(last - first, body)

    open_z(0)
    load_tokens.wait()
    spread_vectors()
    pass_on(0, 1)
    open_z(1)
    first_norm()
    pass_on(0, 2)
    across(0, 1)
    open_z(2)
    pass_on(0, 3)
    halo_on()
    across(0, 2)
    for distance in range(1, chips):
        pass_on(1, distance)
    across(0, 3)
    for distance in range(1, chips):
        across(1, distance)
    all_normed_ready()
    pass_on(2, 1)
    open_z(3)
    close(0)
    pass_on(2, 2)
    keep(in_whole, in_out)
    keep(all_normed, all_normed_out)
    mix()
    keep(mixed, mixed_out)
    pass_on(2, 3)
    across(2, 1)
    attend(0)
    across(2, 2)
    pass_on(3, 1)
    attend(BLOCK)
    pass_on(3, 2)
    attend(2 * BLOCK)
    across(2, 3)
    attend(3 * BLOCK)
    pass_on(3, 3)
    keep(branch, branch_out)
    close(1)
    keep(out_whole, out_out)
    project(1 - core, give)
    copies.start(("partial",), give, came, partner)
    project(core, middle)
    second_norm()
    across(3, 1)
    keep(middle, middle_out)
    for copy in load_low:
        copy.wait()
    for step in range(micro):
        copies.arrived(("low", step), low.at[own_place(1 - core, step)])
    keep(low, low_out)
    close(2)
    keep(up_whole, up_out)
    for step in range(micro):
        copies.arrived(("normed two", step), normed_two.at[own_place(1 - core, step)])
    keep(normed_two, normed_two_out)
    tiles = activated.shape[1] // tile
    staged[0].wait()
    feed(0, tiles // 2)
    across(3, 2)
    feed(tiles // 2, tiles)
    keep(activated, activated_out)
    keep(hidden, hidden_out)
    across(3, 3)
    close(3)
    for copy in moved[sum(len(group) for group in kept) + 2 + len(load_low) :]:
        if copy is not staged[0]:
            copy.wait()
    copies.finish()


def forward(chips, micro, blocks, splits, packed, matrices, tokens, cotangent, starts):
    any_space = pl.BlockSpec(memory_space=pl.ANY)
    vmem = pl.BlockSpec(memory_space=pltpu.VMEM)
    own_rows, width = tokens.shape
    rows, half = 2 * own_rows, width // 2
    all_rows = rows + micro * BLOCK
    shapes = []
    for matrix, count in zip(matrices, splits):
        shard_rows, columns = matrix.shape
        whole = (chips * shard_rows, columns)
        shapes.append(whole if count is None else (2 * chips * shard_rows, columns // 2))
    hidden_width = shapes[2][1]

    def low(*shape):
        return jax.ShapeDtypeStruct(shape, LOW)

    def full(*shape):
        return jax.ShapeDtypeStruct(shape, F32)

    outs = [low(*shape) for shape in shapes] + [
        low(all_rows, 3 * half),
        low(rows, half),
        low(all_rows, width),
        low(rows, width),
        low(rows, hidden_width),
        full(rows, hidden_width),
        full(own_rows, width),
        low(rows, width),
        full(packed.shape[0], width),
    ]
    scratch = [pltpu.VMEM(shape, LOW) for shape in shapes[:3]] + [
        pltpu.VMEM((2 * chips,) + packed.shape, LOW),
        pltpu.VMEM((1, 3 * half), F32),
        pltpu.VMEM((1, hidden_width), F32),
        pltpu.VMEM((own_rows, width), LOW),
        pltpu.VMEM((rows, width), LOW),
        pltpu.VMEM((all_rows, width), LOW),
        pltpu.VMEM((all_rows, 3 * half), LOW),
        pltpu.VMEM((rows, half), LOW),
        pltpu.VMEM((own_rows, width), F32),
        pltpu.VMEM((own_rows, width), F32),
        pltpu.VMEM((own_rows, width), F32),
        pltpu.VMEM((rows, width), LOW),
        pltpu.VMEM((rows, hidden_width), LOW),
        pltpu.VMEM((rows, hidden_width), F32),
        pltpu.SemaphoreType.DMA((180,)),
        pltpu.SemaphoreType.DMA((180,)),
        pltpu.SemaphoreType.DMA((48,)),
    ]
    return pl.pallas_call(
        partial(forward_kernel, chips, micro, blocks, splits),
        out_shape=tuple(outs),
        in_specs=[any_space] * 7 + [vmem],
        out_specs=tuple([any_space] * 12 + [vmem]),
        scratch_shapes=scratch,
        compiler_params=pltpu.CompilerParams(
            collective_id=0, has_side_effects=True, vmem_limit_bytes=63_000_000
        ),
    )(packed, *matrices, tokens, cotangent, starts)


class Reduction:
    def __init__(self, at, copies, blocks_of, outs):
        self.at, self.copies, self.blocks_of, self.outs = at, copies, blocks_of, outs
        self.x_side, self.y_side = at.other(x=1), at.other(y=1)
        self.rep_x, self.rep_y, self.rep_xy = at.flipped(1), at.flipped(2), at.flipped(3)
        self.chunks = []

    def add(self, index, line, first, grad, across, from_x, from_y, from_z, totals):
        self.chunks.append((index, line, first, grad, across, from_x, from_y, from_z, totals))

    def send_across(self, n):
        _, _, _, grad, across, from_x, from_y, _, _ = self.chunks[n]
        half = grad.shape[2] // 2
        upper, lower = pl.ds(0, half), pl.ds(half, half)
        start = self.copies.start
        start(("ax", n), grad.at[:, self.rep_xy, upper], across.at[0], self.x_side)
        start(("ay", n), grad.at[:, self.rep_xy, lower], across.at[1], self.y_side)
        start(("bx", n), grad.at[:, self.rep_x, upper], from_x.at[:, upper], self.x_side)
        start(("by", n), grad.at[:, self.rep_y, lower], from_y.at[:, lower], self.y_side)

    def add_across(self, n):
        _, _, _, grad, across, from_x, from_y, _, _ = self.chunks[n]
        half = grad.shape[2] // 2
        upper, lower = pl.ds(0, half), pl.ds(half, half)
        self.copies.arrived(("ay", n), across.at[1])
        across[1] = (
            across[1].astype(F32) + grad[:, self.rep_x, half : 2 * half].astype(F32)
        ).astype(LOW)
        self.copies.start(("cx", n), across.at[1], from_x.at[:, lower], self.x_side)
        self.copies.arrived(("ax", n), across.at[0])
        across[0] = (across[0].astype(F32) + grad[:, self.rep_y, 0:half].astype(F32)).astype(LOW)
        self.copies.start(("cy", n), across.at[0], from_y.at[:, upper], self.y_side)

    def add_reps(self, n):
        _, _, _, grad, _, from_x, from_y, from_z, _ = self.chunks[n]
        at, half = self.at, grad.shape[2] // 2
        upper, lower = pl.ds(0, half), pl.ds(half, half)
        self.copies.arrived(("bx", n), from_x.at[:, upper])
        self.copies.arrived(("by", n), from_y.at[:, lower])
        self.copies.arrived(("cx", n), from_x.at[:, lower])
        self.copies.arrived(("cy", n), from_y.at[:, upper])
        from_x[...] = (
            grad[:, at.rep].astype(F32) + from_x[...].astype(F32) + from_y[...].astype(F32)
        ).astype(LOW)
        for step in range(1, at.chips):
            chip = lax.rem(at.chip + step, at.chips)
            self.copies.start(
                ("z", n, step), from_x.at[chip], from_z.at[step - 1], at.other(chip=chip)
            )

    def add_chips(self, n):
        _, _, _, grad, _, from_x, _, from_z, totals = self.chunks[n]
        at = self.at
        total = from_x[at.chip].astype(F32)
        for step in range(1, at.chips):
            self.copies.arrived(("z", n, step), from_z.at[step - 1])
            total = total + from_z[step - 1].astype(F32)
        totals[at.rep] = total.astype(LOW)
        own = totals.at[at.rep]
        self.copies.start(("ex", n), own, own, self.x_side)
        self.copies.start(("ey", n), own, own, self.y_side)

    def spread(self, n):
        totals = self.chunks[n][-1]
        half = totals.shape[1] // 2
        self.copies.arrived(("ex", n), totals.at[self.rep_x])
        part = totals.at[self.rep_x, pl.ds(0, half)]
        self.copies.start(("exy", n), part, part, self.y_side)
        self.copies.arrived(("ey", n), totals.at[self.rep_y])
        part = totals.at[self.rep_y, pl.ds(half, half)]
        self.copies.start(("eyx", n), part, part, self.x_side)

    def sides(self, n):
        index, first, width = self.chunks[n][0], self.chunks[n][2], self.chunks[n][-1].shape[2]
        block = self.blocks_of[index]
        for start in range(0, width, block):
            yield start, ((first + start) // block) * 2, block

    def deliver(self, n):
        index, line, first, totals = *self.chunks[n][:3], self.chunks[n][-1]
        quarter, width = totals.shape[1:]
        half, at = quarter // 2, self.at
        self.copies.arrived(("exy", n), totals.at[self.rep_xy, pl.ds(0, half)])
        self.copies.arrived(("eyx", n), totals.at[self.rep_xy, pl.ds(half, half)])
        out = self.outs[index]
        if self.blocks_of[index] is None:
            out[:, line : line + quarter, first : first + width] = totals[...]
            return
        for start, place, block in self.sides(n):
            columns = pl.ds(pl.multiple_of((place + at.core) * block, block), block)
            self.copies.start(
                ("pair", n, start),
                totals.at[pl.ds(2 * (1 - at.core), 2), :, pl.ds(start, block)],
                out.at[:, :, columns],
                at.other(core=1),
            )
            out[:, :, columns] = totals[pl.ds(2 * at.core, 2), :, start : start + block]

    def receive(self, n):
        index = self.chunks[n][0]
        if self.blocks_of[index] is None:
            return
        for start, place, block in self.sides(n):
            columns = pl.ds(pl.multiple_of((place + 1 - self.at.core) * block, block), block)
            self.copies.arrived(("pair", n, start), self.outs[index].at[:, :, columns])

    def tick(self, time):
        stages = (
            self.add_across,
            self.send_across,
            self.add_reps,
            self.add_chips,
            self.spread,
            self.deliver,
            self.receive,
        )
        for stage, offset in zip(stages, OFFSETS):
            if 0 <= time - offset < len(self.chunks):
                stage(time - offset)


OFFSETS = (1, 0, 2, 3, 5, 6, 7)
PART = 512
VECTOR_ROWS = 16


def gelu_slope(values):
    slope = float(2.0 / 3.141592653589793) ** 0.5
    square = values * values
    bend = jnp.tanh(slope * (values + 0.044715 * (values * square)))
    return 0.5 * (1.0 + bend) + 0.5 * values * (1.0 - bend * bend) * slope * (
        1.0 + 0.134145 * square
    )


def loop(count, body):
    def step(index, carry):
        body(index)
        return carry

    lax.fori_loop(0, count, step, 0)


def backward_kernel(chips, micro, blocks, blocks_of, *refs):
    (
        activated_in,
        down_low_in,
        hidden_in,
        normed_two_in,
        up_in,
        out_in,
        in_in,
        down_in,
        branch_in,
        mixed_in,
        all_normed_in,
        middle_in,
        tokens_in,
        starts,
        gains,
    ) = refs[:15]
    outs, vectors_out, input_grad_out, block_out = refs[15:19], refs[19], refs[20], refs[21]
    refs = refs[22:]
    (
        wide,
        deep,
        matrix,
        out_matrix,
        low,
        normed,
        branch,
        attended,
        give,
        came,
        middle,
        tokens,
        key_sums,
        halo,
        vectors,
        vectors_came,
    ) = refs[:16]
    credit, send, recv, local = refs[-4:]
    pools = refs[16:-4]
    at = Place(chips)
    core = at.core
    width = down_low_in.shape[1]
    rows = down_low_in.shape[0]
    body_rows, all_rows = rows, mixed_in.shape[0]
    part_width = mixed_in.shape[1] // 3
    hidden_width = hidden_in.shape[1]
    own_rows, micro_rows = rows // 2, rows // micro
    own_micro = micro_rows // 2
    copies = Copies(send, recv, at)

    loads = []

    def load(source, target):
        copy = pltpu.make_async_copy(source, target, local.at[len(loads)])
        copy.start()
        loads.append(copy)
        return copy

    half_give = own_rows // 2
    tile_sems = local.at[pl.ds(24, 2)]
    activated = wide.at[pl.ds(0, rows)]
    hidden_low = deep.at[pl.ds(0, rows)]
    mixed = wide.at[:, pl.ds(0, 3 * part_width)]
    mixed_grad = deep.at[:, pl.ds(0, 3 * part_width)]
    in_matrix = matrix.at[:, pl.ds(0, 3 * part_width)]
    normed_two = normed.at[pl.ds(0, rows)]
    load_first = [load(activated_in, activated), load(down_low_in, low)]
    down_matrix_rows = matrix.shape[1]
    load_down = [
        load(down_in.at[pl.ds(side * width, width)], matrix.at[:, pl.ds(side * width, width)])
        for side in range(down_matrix_rows // width)
    ]
    load_up = [load(normed_two_in, normed_two), load(middle_in, middle)]
    load_three = [load(out_in, out_matrix), load(branch_in, branch), load(tokens_in, tokens)]
    vectors[...] = jnp.zeros_like(vectors)
    at.greet(at.neighbours())

    reduction = Reduction(at, copies, blocks_of, outs)
    (
        grad_pool,
        grad_pool_out,
        across_pool,
        across_out,
        x_pool,
        x_out,
        y_pool,
        y_out,
        z_pool,
        z_out,
        t_pool,
        t_out,
    ) = pools
    quarter = PART // 8

    def pooled(n, grad_place, index, line, first):
        reduction.add(
            index,
            line,
            first,
            grad_pool.at[grad_place],
            across_pool.at[n],
            x_pool.at[n],
            y_pool.at[n],
            z_pool.at[n],
            t_pool.at[n],
        )

    down_parts, up_parts, in_parts = width // PART, hidden_width // PART, 3 * part_width // PART
    for part in range(down_parts):
        for line in range(2):
            n = 2 * part + line
            pooled(n, n, 3, line * quarter, part * PART)
    for part in range(up_parts):
        n = 2 * down_parts + part
        pooled(n, n, 2, 0, part * PART)
    reduction.add(1, 0, 0, grad_pool_out, across_out, x_out, y_out, z_out, t_out)
    first_in = len(reduction.chunks)
    for part in range(in_parts):
        pooled(first_in - 1 + part, part, 0, 0, part * PART)

    def own_place(row_side, step):
        return pl.ds(pl.multiple_of(step * micro_rows + row_side * own_micro, own_micro), own_micro)

    def dot_down(part):
        block = activated_in.shape[1] // chips

        def body(chip):
            left = activated[:, pl.ds(pl.multiple_of(chip * block, block), block)]
            result = rows_dot(left, low[:, part * PART : (part + 1) * PART]).astype(LOW)
            result = result.reshape(4, 2, quarter, PART)
            grad_pool[2 * part, chip] = result[:, 0]
            grad_pool[2 * part + 1, chip] = result[:, 1]

        loop(chips, body)

    def dot_pair(place, left, right, part):
        block = width // chips

        def body(chip):
            columns = left[:, pl.ds(pl.multiple_of(chip * block, block), block)]
            result = rows_dot(columns, right[:, part * PART : (part + 1) * PART]).astype(LOW)
            grad_pool[place, chip] = result.reshape(4, quarter, PART)

        loop(chips, body)

    def dot_up(part):
        dot_pair(2 * down_parts + part, normed_two, hidden_low, part)

    def dot_in(part):
        for key in ("ax", "ay", "bx", "by"):
            copies.sent((key, part))
        dot_pair(part, normed, mixed_grad, part)

    def dot_out():
        block = part_width // chips

        def body(chip):
            left = branch[:, pl.ds(pl.multiple_of(chip * block, block), block)]
            grad_pool_out[chip] = rows_dot(left, low[...]).astype(LOW).reshape(4, block // 4, width)

        loop(chips, body)

    def back_product(left, left_rows, right, target, target_rows, adding):
        tile = 256

        def body(step):
            columns = pl.ds(pl.multiple_of(step * tile, tile), tile)
            result = back_dot(left[left_rows, :], right[columns, :])
            if adding:
                result = result + target[target_rows, columns]
            target[target_rows, columns] = result.astype(target.dtype)

        loop(right.shape[0] // tile, body)

    def hidden_tile(row, side, slot):
        return pltpu.make_async_copy(
            hidden_in.at[
                pl.ds(pl.multiple_of(row * half_give, half_give), half_give),
                pl.ds(side * width, width),
            ],
            give.at[pl.ds(slot * half_give, half_give)],
            tile_sems.at[slot],
        )

    def hidden_gradient(part):
        count = rows // half_give
        for side in range(2):
            if part == 0:
                hidden_tile(0, side, side).start()

        def body(part_row):
            row = part_row + part * (count // 2)
            place = pl.ds(pl.multiple_of(row * half_give, half_give), half_give)
            for side in range(2):
                hidden_tile(row, side, side).wait()

                def strip(part):
                    start = side * width + part * 256
                    columns = pl.ds(pl.multiple_of(start, 256), 256)
                    from_place = pl.ds(pl.multiple_of(part * 256, 256), 256)
                    values = give[side * half_give : (side + 1) * half_give, from_place]
                    product = back_dot(low[place, :], matrix[from_place, side * width : (side + 1) * width])
                    hidden_low[place, columns] = (product * gelu_slope(values)).astype(LOW)

                loop(width // 256, strip)

                def following():
                    hidden_tile(row + 1, side, side).start()

                pl.when(row + 1 < count)(following)

        loop(count // 2, body)

    def down_product(left_rows, target_rows, finish):
        def body(step):
            columns = pl.ds(pl.multiple_of(step * 256, 256), 256)
            result = None
            for side in range(2):
                start = pl.multiple_of(side * width + step * 256, 256)
                term = dot(
                    activated[left_rows, side * width : (side + 1) * width],
                    matrix[:, pl.ds(start, 256)],
                )
                result = term if result is None else result + term
            finish(target_rows, columns, result)

        loop(width // 256, body)

    def give_result():
        def finish(place, columns, result):
            give[place, columns] = result

        for step in range(micro):
            place = pl.ds(step * own_micro, own_micro)
            down_product(own_place(1 - core, step), place, finish)
        copies.start(("result",), give, came, at.other(core=1))

    def own_result():
        copies.arrived(("result",), came)

        def finish(place, columns, result):
            total = middle[place, columns] + (result + came[place, columns])
            block_out[place, columns] = (total + gains[7:8, columns]).astype(LOW)

        for step in range(micro):
            place = pl.ds(step * own_micro, own_micro)
            down_product(own_place(core, step), place, finish)
        pl.semaphore_signal(
            credit, 1, device_id=at.other(core=1), device_id_type=pl.DeviceIdType.MESH
        )

    def give_partial(name, left, right):
        for step in range(micro):
            place = pl.ds(step * own_micro, own_micro)
            back_product(left, own_place(1 - core, step), right, give, place, False)
        copies.start(name, give, came, at.other(core=1))

    def own_partial(name, left, right):
        copies.arrived(name, came)
        for step in range(micro):
            place = pl.ds(step * own_micro, own_micro)
            back_product(left, own_place(core, step), right, came, place, True)

    def column_sum(row, values):
        vectors[0, row : row + 1, :] += jnp.sum(values, axis=0, keepdims=True)

    lines = 32

    def second_norm_back():
        gain = gains[5:6, :]

        def body(step):
            place = pl.ds(pl.multiple_of(step * lines, lines), lines)
            chip_row = step // (own_micro // lines) * micro_rows + core * own_micro
            chip_row = chip_row + lax.rem(step, own_micro // lines) * lines
            chip_place = pl.ds(pl.multiple_of(chip_row, lines), lines)
            unit, inverse = normalize(middle[place, :])
            upper = came[place, :]
            upstream = low[chip_place, :].astype(F32)
            total = upstream + normalize_back(upper, gain, unit, inverse)
            middle[place, :] = total
            rounded = total.astype(LOW)
            low[chip_place, :] = rounded
            column_sum(2, rounded.astype(F32))
            column_sum(3, upper * unit)
            column_sum(4, upper)
            column_sum(5, upstream)

        loop(own_rows // lines, body)
        for step in range(micro):
            place = low.at[own_place(core, step)]
            copies.start(("low", step), place, place, at.other(core=1))

    def first_norm_back():
        gain = gains[0:1, :]

        def body(step):
            place = pl.ds(pl.multiple_of(step * lines, lines), lines)
            unit, inverse = normalize(tokens[place, :].astype(F32))
            upper = came[place, :]
            total = middle[place, :] + normalize_back(upper, gain, unit, inverse)
            input_grad_out[place, :] = total.astype(LOW)
            column_sum(0, upper * unit)
            column_sum(1, upper)

        loop(own_rows // lines, body)

    def hidden_sums():
        def body(step):
            place = pl.ds(pl.multiple_of(step * lines, lines), lines)
            for side in range(hidden_width // width):
                column_sum(
                    9 + side, hidden_low[place, side * width : (side + 1) * width].astype(F32)
                )

        loop(rows // lines, body)

    def mixed_sums():
        def body(step):
            place = pl.ds(pl.multiple_of(step * lines, lines), lines)
            joined = jnp.concatenate(
                [
                    mixed_grad[place, 0:part_width].astype(F32),
                    mixed_grad[place, 2 * part_width : 3 * part_width].astype(F32),
                ],
                axis=1,
            )
            column_sum(8, joined)

        loop(all_rows // lines, body)

    left = lax.broadcasted_iota(jnp.int32, (BLOCK, BLOCK), 1) < HD
    left_tall = lax.broadcasted_iota(jnp.int32, (2 * BLOCK, BLOCK), 1) < HD
    scale = float(HD) ** (-0.5)

    def attention_group(column):
        key_sums[...] = jnp.zeros_like(key_sums)

        def body(step):
            row, previous = block_rows(step, blocks, body_rows)
            allowed = allowed_keys(starts, row)
            queries = mixed[pl.ds(row, BLOCK), column : column + BLOCK]
            keys = window(mixed, row, previous, part_width + column)
            values = window(mixed, row, previous, 2 * part_width + column)
            upper = attended[pl.ds(row, BLOCK), column : column + BLOCK]
            parts = []
            for side in (left, ~left):
                soft = soft_weights(jnp.where(side, queries, 0), keys, allowed)
                soft_grad = back_dot(jnp.where(side, upper, 0), values)
                total = jnp.sum(soft * soft_grad, axis=1, keepdims=True)
                score_low = (soft * (soft_grad - total)).astype(LOW)
                parts.append(
                    (
                        dot(score_low, keys) * scale,
                        rows_dot(score_low, queries) * scale,
                        rows_dot(soft.astype(LOW), upper),
                    )
                )
            mixed_grad[pl.ds(row, BLOCK), column : column + BLOCK] = jnp.where(
                left, parts[0][0], parts[1][0]
            ).astype(LOW)
            for slot in (1, 2):
                joined = jnp.where(left_tall, parts[0][slot], parts[1][slot])
                place = (slot - 1) * BLOCK
                key_sums[pl.ds(previous, BLOCK), place : place + BLOCK] += joined[:BLOCK]
                key_sums[pl.ds(row, BLOCK), place : place + BLOCK] += joined[BLOCK:]

        loop(body_rows // BLOCK, body)
        for slot in (1, 2):
            place = (slot - 1) * BLOCK
            mixed_grad[:, slot * part_width + column : slot * part_width + column + BLOCK] = (
                key_sums[:, place : place + BLOCK].astype(LOW)
            )
        mixed_grad[body_rows:, column : column + BLOCK] = jnp.zeros(
            (all_rows - body_rows, BLOCK), LOW
        )

    lower_chip = at.other(chip=jnp.maximum(at.chip - 1, 0))

    def send_halo():
        copies.start(
            ("halo",),
            mixed_grad.at[pl.ds(body_rows, all_rows - body_rows), pl.ds(part_width, 2 * part_width)],
            halo,
            lower_chip,
            at.chip > 0,
        )

    def add_halo():
        copies.arrived(("halo",), halo, at.chip < chips - 1)

        def body():
            for step in range(micro):
                place = pl.ds((step + 1) * micro_rows - BLOCK, BLOCK)
                mixed_grad[place, part_width : 3 * part_width] = (
                    mixed_grad[place, part_width : 3 * part_width].astype(F32)
                    + halo[step * BLOCK : (step + 1) * BLOCK, :].astype(F32)
                ).astype(LOW)

        pl.when(at.chip < chips - 1)(body)

    time = iter(range(100))

    def tick():
        reduction.tick(next(time))

    def wait_for(members):
        for member in members:
            member.wait()

    wait_for(load_first)
    dot_down(0)
    tick()
    for part in range(1, down_parts):
        dot_down(part)
    wait_for(load_down)
    hidden_gradient(0)
    tick()
    hidden_gradient(1)
    tick()
    wait_for(load_up)
    give_result()
    for part in range(up_parts // 2):
        dot_up(part)
    own_result()
    load_two = [load(up_in, matrix), load(mixed_in, mixed)]
    tick()
    for part in range(up_parts // 2, up_parts):
        dot_up(part)
    wait_for(load_two)
    copies.sent(("result",))
    pl.semaphore_wait(credit, 1)
    give_partial(("partial", 0), hidden_low, matrix)
    hidden_sums()
    load_normed = [load(all_normed_in, normed)]
    own_partial(("partial", 0), hidden_low, matrix)
    load_last = [load(in_in, in_matrix)] + load_normed
    tick()
    second_norm_back()
    wait_for(load_three)
    for step in range(micro):
        back_product(
            low, own_place(core, step), out_matrix, attended, own_place(core, step), False
        )
    for step in range(micro):
        copies.arrived(("low", step), low.at[own_place(1 - core, step)])
        back_product(
            low, own_place(1 - core, step), out_matrix, attended, own_place(1 - core, step), False
        )
    dot_out()
    tick()
    for column in range(0, part_width, BLOCK):
        attention_group(column)
        if column < part_width - BLOCK:
            tick()
    send_halo()
    wait_for(load_last)
    dot_in(0)
    tick()
    for part in range(1, in_parts):
        dot_in(part)
        if part == 1:
            mixed_sums()
        if part == in_parts - 1:
            copies.sent(("halo",))
            add_halo()
            copies.sent(("partial", 0))
            give_partial(("partial", 1), mixed_grad, in_matrix)
        tick()
    own_partial(("partial", 1), mixed_grad, in_matrix)
    tick()
    first_norm_back()
    copies.start(("sum", "core"), vectors.at[0, pl.ds(0, 8)], vectors_came.at[0, pl.ds(0, 8)], at.other(core=1))
    tick()
    copies.arrived(("sum", "core"), vectors_came.at[0, pl.ds(0, 8)])
    vectors[1, 0:8, :] = vectors[0, 0:8, :] + vectors_came[0, 0:8, :]
    vectors[1, 8:16, :] = vectors[0, 8:16, :]
    copies.start(("sum", "x"), vectors.at[1], vectors_came.at[1], at.other(x=1))
    tick()
    copies.arrived(("sum", "x"), vectors_came.at[1])
    vectors[2] = vectors[1] + vectors_came[1]
    copies.start(("sum", "y"), vectors.at[2], vectors_came.at[2], at.other(y=1))
    tick()
    copies.arrived(("sum", "y"), vectors_came.at[2])
    vectors[3] = vectors[2] + vectors_came[2]
    for step in range(1, chips):
        copies.start(
            ("sum", "z", step),
            vectors.at[3],
            vectors_came.at[2 + step],
            at.other(chip=lax.rem(at.chip + step, chips)),
        )
    tick()
    total = vectors[3]
    for step in range(1, chips):
        copies.arrived(("sum", "z", step), vectors_came.at[2 + step])
        total = total + vectors_came[2 + step]
    vectors_out[...] = total
    for _ in range(7):
        tick()
    copies.finish()


def backward(chips, micro, blocks, blocks_of, members, starts, gains):
    down_low, hidden_low, branch, mixed = members[1], members[2], members[8], members[9]
    rows, width = down_low.shape
    all_rows, hidden_width, part_width = mixed.shape[0], hidden_low.shape[1], branch.shape[1]
    own_rows = rows // 2
    quarter = PART // 8
    down_parts, up_parts, in_parts = width // PART, hidden_width // PART, 3 * part_width // PART
    pooled = 2 * down_parts + up_parts + in_parts
    any_space = pl.BlockSpec(memory_space=pl.ANY)
    vmem = pl.BlockSpec(memory_space=pltpu.VMEM)

    def low(*shape):
        return pltpu.VMEM(shape, LOW)

    def full(*shape):
        return pltpu.VMEM(shape, F32)

    out_quarter = part_width // (4 * chips)
    scratch = [
        low(all_rows, hidden_width),
        low(all_rows, hidden_width),
        low(width, hidden_width),
        low(part_width, width),
        low(rows, width),
        low(all_rows, width),
        low(rows, part_width),
        low(rows, part_width),
        full(own_rows, width),
        full(own_rows, width),
        full(own_rows, width),
        low(own_rows, width),
        full(all_rows, 2 * BLOCK),
        low(all_rows - rows, 2 * part_width),
        full(4, VECTOR_ROWS, width),
        full(chips + 2, VECTOR_ROWS, width),
        low(2 * down_parts + up_parts, chips, 4, quarter, PART),
        low(chips, 4, out_quarter, width),
        low(pooled, 2, chips, quarter // 2, PART),
        low(2, chips, out_quarter // 2, width),
        low(pooled, chips, quarter, PART),
        low(chips, out_quarter, width),
        low(pooled, chips, quarter, PART),
        low(chips, out_quarter, width),
        low(pooled, chips - 1, quarter, PART),
        low(chips - 1, out_quarter, width),
        low(pooled, 4, quarter, PART),
        low(4, out_quarter, width),
        pltpu.SemaphoreType.REGULAR,
        pltpu.SemaphoreType.DMA((240,)),
        pltpu.SemaphoreType.DMA((240,)),
        pltpu.SemaphoreType.DMA((26,)),
    ]
    out_shapes = [
        jax.ShapeDtypeStruct((2, width // (4 * chips), 6 * part_width), LOW),
        jax.ShapeDtypeStruct((4, out_quarter, width), LOW),
        jax.ShapeDtypeStruct((2, width // (4 * chips), 2 * hidden_width), LOW),
        jax.ShapeDtypeStruct((4, hidden_width // (4 * chips), width), LOW),
        jax.ShapeDtypeStruct((VECTOR_ROWS, width), F32),
        jax.ShapeDtypeStruct((own_rows, width), LOW),
        jax.ShapeDtypeStruct((own_rows, width), LOW),
    ]
    results = pl.pallas_call(
        partial(backward_kernel, chips, micro, blocks, blocks_of),
        out_shape=tuple(out_shapes),
        in_specs=[any_space] * 13 + [vmem] * 2,
        out_specs=tuple([vmem] * 7),
        scratch_shapes=scratch,
        compiler_params=pltpu.CompilerParams(
            collective_id=1, has_side_effects=True, vmem_limit_bytes=67_000_000
        ),
    )(*members, starts, gains)
    return results


def shards_general(
    chips,
    reps,
    tokens,
    cotangent,
    seq_lengths,
    dealing,
    attention_gain,
    attention_shift,
    input_weight,
    query_bias,
    value_bias,
    output_weight,
    output_bias,
    feed_gain,
    feed_shift,
    up_weight,
    up_bias,
    down_weight,
    down_bias,
):
    links = Links(chips, reps)
    core, chip = links.core, links.chip
    micro, tok_rows, width = tokens.shape
    shard_count = 2 * chips
    own_rows = micro * tok_rows
    blocks = 2 * tok_rows // BLOCK

    def own_of(values):
        return pick(values.reshape(micro, 2, tok_rows, -1), core, 1).reshape(own_rows, -1)

    def other_of(values):
        return pick(values.reshape(micro, 2, tok_rows, -1), 1 - core, 1).reshape(own_rows, -1)

    def pair_rows(own):
        came = links.swap(own, core=1)
        shape = (micro, 1, tok_rows, own.shape[-1])
        return links.by_core(own.reshape(shape), came.reshape(shape), 1).reshape(2 * own_rows, -1)

    def pair_sum(partial_values):
        return own_of(partial_values) + links.swap(other_of(partial_values), core=1)

    vectors = (
        attention_gain,
        attention_shift,
        query_bias,
        value_bias,
        output_bias,
        feed_gain,
        feed_shift,
        down_bias,
        up_bias,
    )
    lengths = [member.shape[0] for member in vectors]
    table = links.gather_vectors(jnp.concatenate(vectors)).astype(F32)
    wholes, at = [], 0
    for length in lengths:
        wholes.append(table[:, at : at + length])
        at += length

    def whole(index):
        return wholes[index].reshape(1, -1)

    def core_part(index):
        return pick(wholes[index].reshape(chips, 2, -1), core, 1).reshape(1, -1)

    input_part = links.gather(links.halves(input_weight, 3))
    output_part = links.gather(output_weight)
    up_part = links.gather(links.halves(up_weight, 1))
    down_part = links.gather(down_weight)

    inputs = tokens.reshape(own_rows, width).astype(F32)
    unit_one, inverse_one = normalize(inputs)
    normed = (unit_one * whole(0) + whole(1)).astype(LOW)
    chip_normed = pair_rows(normed)
    tail = chip_normed.reshape(micro, 2 * tok_rows, width)[:, 2 * tok_rows - BLOCK :]
    halo = links.shift(tail.reshape(micro * BLOCK, width), 1)
    all_normed = jnp.concatenate([chip_normed, halo], axis=0)
    down_low = pair_rows(cotangent.reshape(own_rows, width))
    first = chip * 2 * tok_rows
    starts = jnp.stack(
        [
            sequence_starts(seq_lengths[m, 0], dealing[m, 0], first, 2 * tok_rows)
            for m in range(micro)
        ]
    )
    block_first = first + jnp.arange(2 * tok_rows, dtype=jnp.int32) // BLOCK * BLOCK - BLOCK
    starts = (starts - block_first[None, :]).reshape(2 * own_rows, 1)

    half = width // 2
    bias = jnp.concatenate([core_part(2), jnp.zeros((1, half), F32), core_part(3)], axis=1)
    mixed = (dot(all_normed, input_part) + bias).astype(LOW)
    branch = attention(mixed, starts, blocks)
    middle = inputs + pair_sum(dot(branch, output_part)) + whole(4)
    unit_two, inverse_two = normalize(middle)
    normed_two = pair_rows((unit_two * whole(5) + whole(6)).astype(LOW))
    hidden = dot(normed_two, up_part) + core_part(8)
    activated, gelu_back = jax.vjp(gelu_tanh, hidden)
    activated = activated.astype(LOW)
    down_grad = links.reduce(rows_dot(activated, down_low)).astype(F32)
    result = middle + pair_sum(dot(activated, down_part)) + whole(7)

    upstream = cotangent.reshape(own_rows, width).astype(F32)
    (hidden_grad,) = gelu_back(back_dot(down_low, down_part))
    hidden_low = hidden_grad.astype(LOW)
    up_grad = links.unhalves(links.reduce(rows_dot(normed_two, hidden_low)), 1).astype(F32)
    upper_two = pair_sum(back_dot(hidden_low, up_part))
    middle_grad = upstream + normalize_back(upper_two, whole(5), unit_two, inverse_two)
    output_own = middle_grad.astype(LOW)
    output_low = pair_rows(output_own)
    output_grad = links.reduce(rows_dot(branch, output_low)).astype(F32)
    attended = back_dot(output_low, output_part).astype(LOW)
    mixed_grad = attention_back(mixed, starts, attended, blocks)
    input_weight_grad = links.unhalves(links.reduce(rows_dot(all_normed, mixed_grad)), 3).astype(F32)
    back_halo = links.shift(mixed_grad[2 * own_rows :, half:], -1)
    body = mixed_grad[: 2 * own_rows].reshape(micro, 2 * tok_rows, 3 * half)
    tail_grad = body[:, 2 * tok_rows - BLOCK :, half:].astype(F32) + back_halo.reshape(
        micro, BLOCK, width
    ).astype(F32)
    body = body.at[:, 2 * tok_rows - BLOCK :, half:].set(tail_grad.astype(LOW))
    upper_one = pair_sum(back_dot(body.reshape(2 * own_rows, 3 * half), input_part))
    input_grad = middle_grad + normalize_back(upper_one, whole(0), unit_one, inverse_one)

    def by_shard(values):
        return values.reshape(shard_count, -1)

    def by_core_shard(values):
        spread = values.reshape(chips, 1, -1)
        mask = jnp.arange(2, dtype=jnp.int32)[None, :, None] == core
        return jnp.where(mask, spread, 0.0).reshape(shard_count, -1)

    def column_sum(values):
        return jnp.sum(values.astype(F32), axis=0)

    packed = jnp.concatenate(
        [
            by_shard(column_sum(upper_one * unit_one)),
            by_shard(column_sum(upper_one)),
            by_core_shard(column_sum(mixed_grad[:, :half])),
            by_core_shard(column_sum(mixed_grad[:, width:])),
            by_shard(column_sum(output_own)),
            by_shard(column_sum(upper_two * unit_two)),
            by_shard(column_sum(upper_two)),
            by_shard(column_sum(upstream)),
            by_core_shard(column_sum(hidden_low)),
        ],
        axis=1,
    )
    sums = links.reduce_vectors(packed)
    vector_grads, at = [], 0
    for length in lengths:
        vector_grads.append(sums[at : at + length])
        at += length
    return (
        result.astype(LOW).reshape(tokens.shape),
        input_grad.astype(LOW).reshape(tokens.shape),
        vector_grads[0],
        vector_grads[1],
        input_weight_grad,
        vector_grads[2],
        vector_grads[3],
        output_grad,
        vector_grads[4],
        vector_grads[5],
        vector_grads[6],
        up_grad,
        vector_grads[8],
        down_grad,
        vector_grads[7],
    )


def finish_kernel(chips, parts, *refs):
    sums, vectors = refs[parts], refs[2 * parts + 1 :]
    for source, target in zip(refs[:parts], refs[parts + 1 : 2 * parts + 1]):
        target[...] = source[...].astype(target.dtype)

    def own_vectors():
        shard = lax.axis_index("shard")
        chip = shard // 2
        own = pl.ds(pl.multiple_of(shard * BLOCK, BLOCK), BLOCK)
        for row in range(6):
            vectors[row][...] = sums[row : row + 1, own]
        half = sums.shape[1] // 2
        for side in range(2):
            place = pl.multiple_of(side * half + chip * BLOCK, BLOCK)
            vectors[6 + side][...] = sums[8:9, pl.ds(place, BLOCK)]
        length = vectors[8].shape[1]
        each = sums.shape[1] // length
        for at in range(chips):

            def copy():
                row, place = 9 + at // each, at % each * length
                vectors[8][...] = sums[row : row + 1, place : place + length]

            pl.when(chip == at)(copy)

    pl.when(pl.program_id(0) == 0)(own_vectors)


def finish(chips, grads, sums, rows):
    steps = 4
    members = list(grads) + list(rows)
    specs = [
        pl.BlockSpec((member.shape[0] // steps, member.shape[1]), lambda step: (step, 0))
        for member in members
    ]
    lengths = [BLOCK] * 8 + [grads[2].shape[1] // (2 * chips)]
    out_shapes = (
        [jax.ShapeDtypeStruct(member.shape, F32) for member in grads]
        + [jax.ShapeDtypeStruct(member.shape, LOW) for member in rows]
        + [jax.ShapeDtypeStruct((1, length), F32) for length in lengths]
    )
    small = [pl.BlockSpec((1, length), lambda step: (0, 0)) for length in lengths]
    return pl.pallas_call(
        partial(finish_kernel, chips, len(members)),
        grid=(steps,),
        out_shape=tuple(out_shapes),
        in_specs=specs + [pl.BlockSpec(sums.shape, lambda step: (0, 0))],
        out_specs=tuple(specs + small),
        compiler_params=pltpu.CompilerParams(vmem_limit_bytes=67_000_000),
    )(*members, sums)


def shards(
    chips,
    reps,
    tokens,
    cotangent,
    seq_lengths,
    dealing,
    *weights,
):
    if chips != 4 or reps != 4:
        return shards_general(chips, reps, tokens, cotangent, seq_lengths, dealing, *weights)
    (
        attention_gain,
        attention_shift,
        input_weight,
        query_bias,
        value_bias,
        output_weight,
        output_bias,
        feed_gain,
        feed_shift,
        up_weight,
        up_bias,
        down_weight,
        down_bias,
    ) = weights
    shard = lax.axis_index("shard")
    chip = shard // 2
    micro, tok_rows, width = tokens.shape
    shard_count, half = 2 * chips, width // 2
    own_rows = micro * tok_rows
    blocks = 2 * tok_rows // BLOCK
    hidden_half = up_weight.shape[1] // 2

    members = [
        attention_gain,
        attention_shift,
        query_bias,
        value_bias,
        output_bias,
        feed_gain,
        feed_shift,
        down_bias,
    ] + [up_bias[at : at + BLOCK] for at in range(0, up_bias.shape[0], BLOCK)]
    line = lax.broadcasted_iota(jnp.int32, (VECTOR_ROWS, BLOCK), 0)
    packed = jnp.zeros((VECTOR_ROWS, BLOCK), LOW)
    for index, member in enumerate(members):
        packed = jnp.where(line == index, member[None, :], packed)
    first = chip * 2 * tok_rows
    starts = jnp.stack(
        [
            sequence_starts(seq_lengths[m, 0], dealing[m, 0], first, 2 * tok_rows)
            for m in range(micro)
        ]
    )
    block_first = first + jnp.arange(2 * tok_rows, dtype=jnp.int32) // BLOCK * BLOCK - BLOCK
    starts = (starts - block_first[None, :]).reshape(2 * own_rows, 1)
    own_tokens = tokens.reshape(own_rows, width)
    (
        input_part,
        output_part,
        up_part,
        down_part,
        mixed,
        branch,
        all_normed,
        normed_two,
        activated,
        hidden,
        middle,
        down_low,
        vectors,
    ) = forward(
        chips,
        micro,
        blocks,
        (3 * chips, None, chips, None),
        packed,
        (input_weight, output_weight, up_weight, down_weight),
        own_tokens,
        cotangent.reshape(own_rows, width),
        starts,
    )
    results = backward(
        chips,
        micro,
        blocks,
        (width // shard_count, None, hidden_half // chips, None),
        (
            activated,
            down_low,
            hidden,
            normed_two,
            up_part,
            output_part,
            input_part,
            down_part,
            branch,
            mixed,
            all_normed,
            middle,
            own_tokens,
        ),
        starts,
        vectors,
    )
    flat = [member.reshape(-1, member.shape[2]) for member in results[:4]]
    finished = finish(chips, flat, results[4], results[5:])
    vector_grads = [member.reshape(-1) for member in finished[6:]]
    return (
        finished[5].reshape(tokens.shape),
        finished[4].reshape(tokens.shape),
        vector_grads[0],
        vector_grads[1],
        finished[0],
        vector_grads[6],
        vector_grads[7],
        finished[1],
        vector_grads[2],
        vector_grads[3],
        vector_grads[4],
        finished[2],
        vector_grads[8],
        finished[3],
        vector_grads[5],
    )


def solution(mesh):
    rows_spec = P(None, ("shard", "rep"), None)
    vector, matrix = P("shard"), P("shard", None)
    weight_specs = (
        vector,
        vector,
        matrix,
        vector,
        vector,
        matrix,
        vector,
        vector,
        vector,
        matrix,
        vector,
        matrix,
        vector,
    )
    return jax.shard_map(
        partial(shards, mesh.shape["shard"] // 2, mesh.shape["rep"]),
        mesh=mesh,
        in_specs=(rows_spec, rows_spec, P(None, "rep", None, None), P(None, "rep", None))
        + weight_specs,
        out_specs=(rows_spec, rows_spec) + weight_specs,
        check_vma=False,
    )
```
